32 devices in a mesh: dom: 16 (over z, y, x), edge: 2 (over core).
Axes of the slice: x: 2, y: 2, z: 4, core: 2. Of those that a mesh axis runs over, the one named last changes fastest.
Arguments:
- node_lat: bfloat16 [8192, 256], P(('dom', 'edge')), may hold values from -6 to 6
- edge_lat: bfloat16 [98304, 256], P(('dom', 'edge')), may hold values from -6 to 6
- senders: int32 [98304], P(('dom', 'edge')), may hold values from 0 to 1535
- receivers: int32 [98304], P(('dom', 'edge')), may hold values from 0 to 511
- live_edges: int32 [16, 2], P('dom', 'edge'), may hold values from 768 to 3072, as said below
- send_rows: int32 [32, 4, 128], P(('dom', 'edge')), may hold values from 0 to 255, as said below
- edge_w1: bfloat16 [2, 768, 256], replicated, may hold values from -0.21875 to 0.21875
- edge_b1: float32 [2, 256], replicated, may hold values from -3 to 3
- edge_w2: bfloat16 [2, 256, 256], replicated, may hold values from -0.375 to 0.375
- edge_gain: float32 [2, 256], replicated, may hold values from 0.1 to 1.9
- node_w1: bfloat16 [2, 512, 256], replicated, may hold values from -0.25 to 0.25
- node_b1: float32 [2, 256], replicated, may hold values from -3 to 3
- node_w2: bfloat16 [2, 256, 256], replicated, may hold values from -0.375 to 0.375
- node_gain: float32 [2, 256], replicated, may hold values from 0.1 to 1.9
Outputs:
- node_out: bfloat16 [8192, 256], P(('dom', 'edge'))
- edge_out: bfloat16 [98304, 256], P(('dom', 'edge'))
The draws below stay inside these ranges and needn't reach their ends.
Inputs may be any that keep to these rules, and one draw needn't show every extreme that they name: `send_rows`: for each device and face, 128 distinct rows of the device's own 256 nodes. `live_edges`: a multiple of 128 for every device; some device is full in every draw. `senders`: rows of the domain's node table. `receivers`: nodes of the edge's own domain.
All inputs are finite; a program needn't handle non-finite values.
Results may differ from the reference program's by a relative error of at most 0.014.
Values may be sent and summed in bfloat16 or wider, within the bound.
No kernel may reach another device: no remote copies, remote signals or barrier semaphores. Data moves between devices by JAX's collectives and lax.ppermute only.
A program may use at most 64 MiB of HBM per device.

```python
import jax
import jax.numpy as jnp
from jax import lax

LATENT = 256
HIDDEN_SIZE = 256
NODE_DEV = 256
EDGE_DEV = 3072
HALO_DEV = 128
BLOCK = 128
LAYERS = 2
FACES = 4
NODE_DOM = 512
TABLE_ROWS = 1536
NODES = 8192
EDGES = 98304
N_DOM = 16
N_EDGE = 2


def draw_live_edges(key, part):
    block_total = EDGE_DEV // BLOCK
    lowest = max(1, block_total // 4)
    first_key, second_key = jax.random.split(key)
    block_counts = jax.random.randint(first_key, (N_DOM * N_EDGE,), lowest, block_total + 1)
    full_device = jax.random.randint(second_key, (), 0, N_DOM * N_EDGE)
    block_counts = jnp.where(jnp.arange(N_DOM * N_EDGE) == full_device, block_total, block_counts)
    return (block_counts * BLOCK).reshape(N_DOM, N_EDGE).astype(jnp.int32)


def draw_send_rows(key, part):
    list_total = N_DOM * N_EDGE * FACES
    key_list = jax.random.split(key, list_total)

    def pick_rows(one_key):
        return jax.random.permutation(one_key, NODE_DEV)[:HALO_DEV]
    picked = jax.vmap(pick_rows)(key_list)
    return picked.reshape(N_DOM * N_EDGE, FACES, HALO_DEV).astype(jnp.int32)


def touch_ends(entries, rng, least, top_value):
    extent = entries.shape
    spot = [jax.random.randint(jax.random.fold_in(rng, axis), (), 0, extent[axis]) for axis in range(len(extent))]
    entries = entries.at[tuple(spot)].set(least)
    longest = extent.index(max(extent))
    spot[longest] = (spot[longest] + 1) % extent[longest]
    return entries.at[tuple(spot)].set(top_value)


def block_levels(rng, shape, pieces, least, high):
    gain, own = 1.0, jax.random.fold_in(rng, 6)
    for dim, blocks in pieces:
        draws = jnp.exp(jax.random.uniform(jax.random.fold_in(own, dim), (blocks,), jnp.float32, least / len(pieces), high / len(pieces)))
        gain = gain * jnp.repeat(draws, shape[dim] // blocks).reshape([-1 if axis == dim else 1 for axis in range(len(shape))])
    return gain


def gaussian(key, extent, scale, most, shards=(), held_as=jnp.bfloat16):
    entries = jax.random.normal(key, extent, jnp.float32) * scale
    if len(shards) > 0:
        entries = block_levels(key, extent, shards, -0.22, 0.18) * entries
    return jnp.clip(entries, min=-most, max=most).astype(held_as)


def setup_inputs(seed: int = 0) -> dict:
    key_of = jax.random.split(jax.random.key(seed), 15)
    return {
        "node_lat": gaussian(key_of[0], (NODES, LATENT), 1.0, 6.0, ((0, 32),)),
        "edge_lat": gaussian(key_of[1], (EDGES, LATENT), 1.0, 6.0, ((0, 32),)),
        "senders": touch_ends(jax.random.randint(key_of[2], (EDGES,), 0, TABLE_ROWS), jax.random.fold_in(key_of[2], 1), 0, TABLE_ROWS - 1).astype(jnp.int32),
        "receivers": touch_ends(jax.random.randint(key_of[3], (EDGES,), 0, NODE_DOM), jax.random.fold_in(key_of[3], 1), 0, NODE_DOM - 1).astype(jnp.int32),
        "live_edges": draw_live_edges(jax.random.fold_in(key_of[14], 71), 0),
        "send_rows": draw_send_rows(jax.random.fold_in(key_of[14], 71), 0),
        "edge_w1": gaussian(key_of[6], (LAYERS, 3 * LATENT, HIDDEN_SIZE), (3 * LATENT) ** -0.5, 0.21875),
        "edge_b1": gaussian(key_of[7], (LAYERS, HIDDEN_SIZE), 0.5, 3.0, (), jnp.float32),
        "edge_w2": gaussian(key_of[8], (LAYERS, HIDDEN_SIZE, LATENT), HIDDEN_SIZE ** -0.5, 0.375),
        "edge_gain": jnp.clip(1.0 + 0.18 * jax.random.normal(key_of[9], (LAYERS, LATENT), jnp.float32), 0.1, 1.9),
        "node_w1": gaussian(key_of[10], (LAYERS, 2 * LATENT, HIDDEN_SIZE), (2 * LATENT) ** -0.5, 0.25),
        "node_b1": gaussian(key_of[11], (LAYERS, HIDDEN_SIZE), 0.5, 3.0, (), jnp.float32),
        "node_w2": gaussian(key_of[12], (LAYERS, HIDDEN_SIZE, LATENT), HIDDEN_SIZE ** -0.5, 0.375),
        "node_gain": jnp.clip(1.0 + 0.18 * jax.random.normal(key_of[13], (LAYERS, LATENT), jnp.float32), 0.1, 1.9),
    }


eps_norm = 1e-05

def layer_norm(values, norm_gain):
    center = values - lax.optimization_barrier(jnp.mean(values, axis=-1, keepdims=True))
    spread = lax.optimization_barrier(jnp.mean(center * center, axis=-1, keepdims=True))
    return center * lax.rsqrt(spread + eps_norm) * norm_gain.astype(jnp.float32)

def edge_update(edge_rows, sender_rows, receiver_rows, weight_in, bias_in, weight_out, norm_gain, live_rows):
    feature_width = edge_rows.shape[1]
    pre_act = jnp.dot(edge_rows, weight_in[:feature_width], preferred_element_type=jnp.float32)
    pre_act = pre_act + jnp.dot(sender_rows, weight_in[feature_width:2 * feature_width], preferred_element_type=jnp.float32)
    pre_act = pre_act + jnp.dot(receiver_rows, weight_in[2 * feature_width:], preferred_element_type=jnp.float32)
    hidden_rows = jax.nn.relu(pre_act + bias_in.astype(jnp.float32)).astype(jnp.bfloat16)
    messages = layer_norm(jnp.dot(hidden_rows, weight_out, preferred_element_type=jnp.float32), norm_gain)
    messages = jnp.where(live_rows[:, None], messages, jnp.float32(0.0))
    return ((edge_rows.astype(jnp.float32) + messages).astype(jnp.bfloat16), messages)

def node_update(node_rows, aggregate, weight_in, bias_in, weight_out, norm_gain):
    feature_width = node_rows.shape[1]
    pre_act = jnp.dot(node_rows, weight_in[:feature_width], preferred_element_type=jnp.float32)
    pre_act = pre_act + jnp.dot(aggregate, weight_in[feature_width:], preferred_element_type=jnp.float32)
    hidden_rows = jax.nn.relu(pre_act + bias_in.astype(jnp.float32)).astype(jnp.bfloat16)
    update = layer_norm(jnp.dot(hidden_rows, weight_out, preferred_element_type=jnp.float32), norm_gain)
    return (node_rows.astype(jnp.float32) + update).astype(jnp.bfloat16)

def reference(node_lat, edge_lat, senders, receivers, live_edges, send_rows, edge_w1, edge_b1, edge_w2, edge_gain, node_w1, node_b1, node_w2, node_gain):
    stride = N_DOM // 4
    offsets = (1, -1, stride, -stride)
    node_dom = N_EDGE * NODE_DEV
    rank_base = (jnp.arange(N_DOM * N_EDGE, dtype=jnp.int32) * NODE_DEV)[:, None, None]
    picks = (send_rows + rank_base).astype(jnp.int32).reshape(N_DOM, N_EDGE, FACES, HALO_DEV)
    live_all = jnp.arange(EDGE_DEV, dtype=jnp.int32)[None, None, :] < live_edges[:, :, None]
    live_all = live_all.reshape(N_DOM, N_EDGE * EDGE_DEV)
    sender_dom = senders.reshape(N_DOM, N_EDGE * EDGE_DEV)
    receiver_dom = receivers.reshape(N_DOM, N_EDGE * EDGE_DEV)
    owned_rows = node_lat
    edge_rows = edge_lat
    for layer_index in range(LAYERS):
        sent = jnp.take(owned_rows, picks, axis=0)
        received = jnp.stack([jnp.roll(sent[:, :, face_index], offsets[face_index], axis=0) for face_index in range(FACES)], axis=2)
        halo_all = received.reshape(N_DOM, N_EDGE * FACES * HALO_DEV, LATENT)
        domain_rows = owned_rows.reshape(N_DOM, node_dom, LATENT)
        node_table = jnp.concatenate([domain_rows, halo_all], axis=1)
        edge_dom = edge_rows.reshape(N_DOM, N_EDGE * EDGE_DEV, LATENT)

        def one_domain(items):
            table_one, domain_one, edges_one, send_one, recv_one, live_one = items
            new_edges, messages = edge_update(edges_one, jnp.take(table_one, send_one, axis=0), jnp.take(domain_one, recv_one, axis=0), edge_w1[layer_index], edge_b1[layer_index], edge_w2[layer_index], edge_gain[layer_index], live_one)
            message_parts = messages.reshape(N_EDGE, EDGE_DEV, LATENT)
            recv_parts = recv_one.reshape(N_EDGE, EDGE_DEV)
            summed = jnp.zeros((node_dom, LATENT), jnp.float32)
            for rank_index in range(N_EDGE):
                partial_sum = jax.ops.segment_sum(message_parts[rank_index], recv_parts[rank_index], num_segments=node_dom)
                rounded = lax.optimization_barrier(partial_sum.astype(jnp.bfloat16))
                summed = summed + rounded.astype(jnp.float32)
            return (new_edges, summed.astype(jnp.bfloat16))
        new_edges, aggregate = lax.map(one_domain, (node_table, domain_rows, edge_dom, sender_dom, receiver_dom, live_all))
        edge_rows = new_edges.reshape(-1, LATENT)
        owned_rows = node_update(owned_rows, aggregate.reshape(-1, LATENT), node_w1[layer_index], node_b1[layer_index], node_w2[layer_index], node_gain[layer_index])
    return (owned_rows, edge_rows)
```

```python
import functools

import jax
import jax.numpy as jnp
from jax import lax
from jax.experimental import pallas as pl
from jax.experimental.pallas import tpu as pltpu
from jax.sharding import PartitionSpec as P

LAYERS = 2


eps_norm = 1e-05


def passed_along(value, axis, steps):
    count = lax.axis_size(axis)
    pairs = [(source, (source + steps) % count) for source in range(count)]
    return lax.ppermute(value, axis, pairs)


def layer_norm(values, norm_gain):
    center = values - jnp.mean(values, axis=-1, keepdims=True)
    spread = jnp.mean(center * center, axis=-1, keepdims=True)
    return center * lax.rsqrt(spread + eps_norm) * norm_gain


def edge_update(
    edge_rows, sender_rows, receiver_rows, weight_in, bias_in, weight_out, norm_gain, live_rows
):
    feature_width = edge_rows.shape[1]
    pre_act = jnp.dot(edge_rows, weight_in[:feature_width], preferred_element_type=jnp.float32)
    pre_act = pre_act + jnp.dot(
        sender_rows,
        weight_in[feature_width : 2 * feature_width],
        preferred_element_type=jnp.float32,
    )
    pre_act = pre_act + jnp.dot(
        receiver_rows, weight_in[2 * feature_width :], preferred_element_type=jnp.float32
    )
    hidden_rows = jax.nn.relu(pre_act + bias_in).astype(jnp.bfloat16)
    messages = layer_norm(
        jnp.dot(hidden_rows, weight_out, preferred_element_type=jnp.float32), norm_gain
    )
    messages = jnp.where(live_rows[:, None], messages, jnp.float32(0.0))
    return ((edge_rows.astype(jnp.float32) + messages).astype(jnp.bfloat16), messages)


def node_update(node_rows, aggregate, weight_in, bias_in, weight_out, norm_gain):
    feature_width = node_rows.shape[1]
    pre_act = jnp.dot(node_rows, weight_in[:feature_width], preferred_element_type=jnp.float32)
    pre_act = pre_act + jnp.dot(
        aggregate, weight_in[feature_width:], preferred_element_type=jnp.float32
    )
    hidden_rows = jax.nn.relu(pre_act + bias_in).astype(jnp.bfloat16)
    update = layer_norm(
        jnp.dot(hidden_rows, weight_out, preferred_element_type=jnp.float32), norm_gain
    )
    return (node_rows.astype(jnp.float32) + update).astype(jnp.bfloat16)


F32 = jnp.float32
BF16 = jnp.bfloat16
TILE = 256
HALF = 128
ROWS = 512
IN_VMEM = pl.BlockSpec(memory_space=pltpu.VMEM)
IN_SMEM = pl.BlockSpec(memory_space=pltpu.SMEM)


def shaped(shape, dtype):
    return jax.ShapeDtypeStruct(shape, dtype)


def call(kernel, outs, args, scratch=(), smem=(), flops=0, limit=24, name=None):
    nbytes = sum(a.size * a.dtype.itemsize for a in args)
    return pl.pallas_call(
        kernel,
        out_shape=outs,
        in_specs=[IN_SMEM if k in smem else IN_VMEM for k in range(len(args))],
        out_specs=jax.tree.map(lambda _: IN_VMEM, outs),
        scratch_shapes=scratch,
        compiler_params=pltpu.CompilerParams(vmem_limit_bytes=limit << 20),
        cost_estimate=pl.CostEstimate(flops=flops, transcendentals=0, bytes_accessed=nbytes),
        name=name,
    )(*args)


def place(stride):
    dom = lax.axis_index("dom")
    core = lax.axis_index("edge")
    return core, lax.rem(dom, 2), lax.rem(lax.div(dom, stride), 2)


def mm(a, b):
    return jnp.dot(a, b, preferred_element_type=F32)


def column(row):
    return jnp.transpose(jnp.broadcast_to(row.astype(F32), (HALF, HALF)))


def one_hot_rows(row):
    col = column(row)
    lane = lax.broadcasted_iota(jnp.int32, (HALF, HALF), 1).astype(F32)
    parts = [jnp.where(col == lane + float(k), 1.0, 0.0) for k in (0, HALF)]
    return jnp.concatenate(parts, axis=1).astype(BF16)


def dyn(start, size):
    return pl.ds(pl.multiple_of(start, size), size)


def pick_kernel(stride, nodes_ref, lists_ref, far_d, far_s, near_d, near_s):
    _, par_d, par_s = place(stride)
    nodes = nodes_ref[...]
    for face, out in (
        (1 - par_d, far_d),
        (3 - par_s, far_s),
        (par_d, near_d),
        (2 + par_s, near_s),
    ):
        out[...] = mm(one_hot_rows(lists_ref[0, pl.ds(face, 1), :]), nodes).astype(BF16)


def index_kernel(stride, edges, send_ref, recv_ref, live_ref, cols, rows):
    _, par_d, par_s = place(stride)
    live = live_ref[0, 0]
    lane = lax.broadcasted_iota(jnp.int32, (1, HALF), 1)
    for k in range(edges // HALF):
        at = pl.ds(k * HALF, HALF)
        v = send_ref[:, at]
        j = v - 2 * TILE
        owner = lax.shift_right_arithmetic(j, 9)
        face = lax.shift_right_arithmetic(j, 7) & 3
        core = lax.shift_right_arithmetic(face, 1)
        par = jnp.where(core == 0, par_d, par_s)
        near = (face & 1) != par
        tile = jnp.where(near, 2, 4) + core
        at_tile = ((owner ^ core) & 1) * HALF + (j & (HALF - 1))
        local = v < 2 * TILE
        hi = jnp.where(local, lax.shift_right_arithmetic(v, 8), tile)
        lo = jnp.where(local, v & (TILE - 1), at_tile)
        cols[0, at, :] = column(hi).astype(BF16)
        cols[1, at, :] = column(lo).astype(BF16)
        v = recv_ref[:, at]
        hi = lax.shift_right_arithmetic(v, 8)
        lo = v & (TILE - 1)
        cols[2, at, :] = column(hi).astype(BF16)
        cols[3, at, :] = column(lo).astype(BF16)
        rows[0:1, at] = jnp.where(lane + k * HALF < live, hi, -1).astype(F32)
        rows[1:2, at] = lo.astype(F32)


def lane_iota(rows):
    lane = lax.broadcasted_iota(jnp.int32, (rows, HALF), 1).astype(F32)
    return lane.astype(BF16), (lane + float(HALF)).astype(BF16)


def hits(hi, lo, tile, lanes):
    at = jnp.where(hi == tile, lo, jnp.asarray(-1, BF16))
    one = jnp.ones(at.shape, BF16)
    zero = jnp.zeros(at.shape, BF16)
    return jnp.concatenate([jnp.where(at == lane, one, zero) for lane in lanes], axis=1)


def local_kernel(layer, stacked, edge_ref, cols, *refs):
    if stacked:
        dom_ref, w1_ref, b1_ref, pre_ref, t_s, t_r = refs
        dom = dom_ref[...]
        t_s[...] = mm(dom, w1_ref[layer, TILE : 2 * TILE, :]).astype(BF16)
        t_r[...] = mm(dom, w1_ref[layer, 2 * TILE :, :]).astype(BF16)
    else:
        own_ref, peer_ref, w1_ref, b1_ref, pre_ref, t_s, t_r = refs
        core = lax.axis_index("edge")
        for owner, ref in ((core, own_ref), (1 - core, peer_ref)):
            at = dyn(owner * TILE, TILE)
            t_s[at, :] = mm(ref[...], w1_ref[layer, TILE : 2 * TILE, :]).astype(BF16)
            t_r[at, :] = mm(ref[...], w1_ref[layer, 2 * TILE :, :]).astype(BF16)
    lanes = lane_iota(ROWS)
    bias = b1_ref[layer : layer + 1, :]
    w_e = w1_ref[layer, 0:TILE, :]

    def step(k, carry):
        at = dyn(k * ROWS, ROWS)
        acc = mm(edge_ref[at, :], w_e)
        for base, table in ((0, t_s), (2, t_r)):
            hi = cols[base, at, :]
            lo = cols[base + 1, at, :]
            for tile in range(2):
                acc = acc + mm(
                    hits(hi, lo, jnp.asarray(tile, BF16), lanes),
                    table[tile * TILE : (tile + 1) * TILE, :],
                )
        pre_ref[at, :] = acc + bias
        return carry

    lax.fori_loop(0, edge_ref.shape[0] // ROWS, step, 0)


def halo_tables(layer, first, halves, w1_ref, refs, table):
    core = lax.axis_index("edge")
    w_s = w1_ref[layer, TILE : 2 * TILE, :]
    if halves:
        own_d, own_s, peer_d, peer_s = refs
        for axis, owner, ref in (
            (0, core, own_d),
            (1, core, own_s),
            (0, 1 - core, peer_d),
            (1, 1 - core, peer_s),
        ):
            row = axis * TILE + lax.rem(owner + axis, 2) * HALF
            table[dyn(row, HALF), :] = mm(ref[...], w_s).astype(BF16)
    else:
        own, peer = refs
        for axis, ref in ((core, own), (1 - core, peer)):
            table[dyn(axis * TILE, TILE), :] = mm(ref[...], w_s).astype(BF16)
    return first, first + 1


def near_kernel(layer, halves, pre_ref, cols, w1_ref, *refs):
    refs, (out_ref, table) = refs[:-2], refs[-2:]
    tiles = halo_tables(layer, 2, halves, w1_ref, refs, table)
    lanes = lane_iota(ROWS)

    def step(k, carry):
        at = dyn(k * ROWS, ROWS)
        hi = cols[0, at, :]
        lo = cols[1, at, :]
        acc = pre_ref[at, :]
        for n, tile in enumerate(tiles):
            acc = acc + mm(
                hits(hi, lo, jnp.asarray(tile, BF16), lanes), table[n * TILE : (n + 1) * TILE, :]
            )
        out_ref[at, :] = acc
        return carry

    lax.fori_loop(0, pre_ref.shape[0] // ROWS, step, 0)


def edge_kernel(layer, halves, split, live_ref, pre_ref, cols, rows, edge_ref, w1_ref, w2_ref, gain_ref, *refs):
    if split:
        refs, (out_ref, keep_ref, give_ref, table, msgs) = refs[:-5], refs[-5:]
    else:
        refs, (out_ref, part_ref, table, msgs) = refs[:-4], refs[-4:]
    tiles = halo_tables(layer, 4, halves, w1_ref, refs, table)
    lanes = lane_iota(ROWS)
    live = live_ref[0, 0]
    gain = gain_ref[layer : layer + 1, :]
    w2 = w2_ref[layer]
    place_in = lax.broadcasted_iota(jnp.int32, (ROWS, TILE), 0)

    def step(k, carry):
        at = dyn(k * ROWS, ROWS)
        hi = cols[0, at, :]
        lo = cols[1, at, :]
        acc = pre_ref[at, :]
        for n, tile in enumerate(tiles):
            acc = acc + mm(
                hits(hi, lo, jnp.asarray(tile, BF16), lanes), table[n * TILE : (n + 1) * TILE, :]
            )
        hidden = jnp.maximum(acc, 0.0).astype(BF16)
        message = layer_norm(mm(hidden, w2), gain)
        msgs[at, :] = message.astype(BF16)
        message = jnp.where(place_in + k * ROWS < live, message, 0.0)
        out_ref[at, :] = (edge_ref[at, :].astype(F32) + message).astype(BF16)
        return carry

    count = edge_ref.shape[0] // ROWS
    lax.fori_loop(0, count, step, 0)
    spot = lax.broadcasted_iota(jnp.int32, (TILE, ROWS), 0).astype(F32).astype(BF16)
    one = jnp.ones((TILE, ROWS), BF16)
    zero = jnp.zeros((TILE, ROWS), BF16)
    sums = [None, None]
    for k in range(count):
        at = pl.ds(k * ROWS, ROWS)
        hi = rows[0:1, at]
        lo = rows[1:2, at]
        msg = msgs[at, :]
        for n in range(2):
            here = jnp.where(hi == float(n), lo, -1.0).astype(BF16)
            hot = jnp.where(jnp.broadcast_to(here, (TILE, ROWS)) == spot, one, zero)
            part = mm(hot, msg)
            sums[n] = part if sums[n] is None else sums[n] + part
    if split:
        core = lax.axis_index("edge")
        mine = core == 0
        keep_ref[...] = jnp.where(mine, sums[0], sums[1]).astype(BF16)
        give_ref[...] = jnp.where(mine, sums[1], sums[0]).astype(BF16)
    else:
        for n in range(2):
            part_ref[n * TILE : (n + 1) * TILE, :] = sums[n].astype(BF16)


def updated(layer, nodes, first, second, w1_ref, b1_ref, w2_ref, gain_ref):
    total = (first.astype(F32) + second.astype(F32)).astype(BF16)
    pre = mm(nodes, w1_ref[layer, 0:TILE, :]) + mm(total, w1_ref[layer, TILE:, :])
    hidden = jnp.maximum(pre + b1_ref[layer : layer + 1, :], 0.0).astype(BF16)
    step = layer_norm(mm(hidden, w2_ref[layer]), gain_ref[layer : layer + 1, :])
    return (nodes.astype(F32) + step).astype(BF16)


def node_kernel(
    stride, layer, own_ref, peer_ref, first, second, list_own, list_peer, w1, b1, w2, gain, out, far, near
):
    core, par_d, par_s = place(stride)
    for owner, ref in ((core, own_ref), (1 - core, peer_ref)):
        at = dyn(owner * TILE, TILE)
        out[at, :] = updated(layer, ref[...], first[at, :], second[at, :], w1, b1, w2, gain)
    par = jnp.where(core == 0, par_d, par_s)
    for face, ref in ((2 * core + 1 - par, far), (2 * core + par, near)):
        for n, (owner, lists) in enumerate(((core, list_own), (1 - core, list_peer))):
            hot = one_hot_rows(lists[0, pl.ds(face, 1), :])
            ref[n * HALF : (n + 1) * HALF, :] = mm(hot, out[dyn(owner * TILE, TILE), :]).astype(BF16)


def last_kernel(layer, nodes_ref, first, second, w1, b1, w2, gain, out):
    core = lax.axis_index("edge")
    nodes = nodes_ref[dyn(core * TILE, TILE), :]
    out[...] = updated(layer, nodes, first[...], second[...], w1, b1, w2, gain)


def met(count, stride, odd):
    pairs = []
    for dom in range(count):
        ahead = (dom // stride) % 2 == odd
        pairs.append((dom + (stride if ahead else -stride)) % count)
    return pairs


def swapped(value):
    return lax.ppermute(value, "edge", [(0, 1), (1, 0)])


def fast_shards(
    node_lat,
    edge_lat,
    senders,
    receivers,
    live_edges,
    send_rows,
    edge_w1,
    edge_b1,
    edge_w2,
    edge_gain,
    node_w1,
    node_b1,
    node_w2,
    node_gain,
):
    domains = lax.axis_size("dom")
    stride = domains // 4
    edges, width = edge_lat.shape
    nodes = node_lat.shape[0]
    near_d, far_d = met(domains, 1, 0), met(domains, 1, 1)
    near_s, far_s = met(domains, stride, 0), met(domains, stride, 1)

    def sent(value, partner):
        return lax.ppermute(value, "dom", list(enumerate(partner)))

    def sent_by_core(value, partner_d, partner_s):
        pairs = [(2 * d, 2 * p) for d, p in enumerate(partner_d)]
        pairs += [(2 * d + 1, 2 * p + 1) for d, p in enumerate(partner_s)]
        return lax.ppermute(value, ("dom", "edge"), pairs)

    face = shaped((HALF, width), BF16)
    table = pltpu.VMEM((2 * TILE, width), BF16)
    messages = pltpu.VMEM((edges, width), BF16)
    pre_shape = shaped((edges, width), F32)
    pass_flops = 2 * edges * TILE * width

    picked = call(
        functools.partial(pick_kernel, stride), [face] * 4, (node_lat, send_rows), name="pick"
    )
    halo = [
        sent(value, partner) for value, partner in zip(picked, (far_d, far_s, near_d, near_s))
    ]
    peer_nodes = swapped(node_lat)
    peer_lists = swapped(send_rows)
    cols, rows = call(
        functools.partial(index_kernel, stride, edges),
        [shaped((4, edges, HALF), BF16), shaped((2, edges), F32)],
        (senders[None], receivers[None], live_edges),
        smem=(2,),
        name="index",
    )
    own_nodes = node_lat
    edge_rows = edge_lat
    for layer in range(LAYERS):
        last = layer == LAYERS - 1
        if layer == 0:
            node_args = (node_lat, peer_nodes)
            far = (halo[0], halo[1], swapped(halo[0]), swapped(halo[1]))
            near = (halo[2], halo[3], swapped(halo[2]), swapped(halo[3]))
        else:
            node_args = (all_nodes,)
            far = sent_by_core(far_rows, far_d, far_s)
            near = sent_by_core(near_rows, near_d, near_s)
            far = (far, swapped(far))
            near = (near, swapped(near))
        pre = call(
            functools.partial(local_kernel, layer, layer > 0),
            pre_shape,
            (edge_rows, cols, *node_args, edge_w1, edge_b1),
            scratch=[table, table],
            flops=5 * pass_flops,
            name="local",
        )
        pre = call(
            functools.partial(near_kernel, layer, layer == 0),
            pre_shape,
            (pre, cols, edge_w1, *near),
            scratch=[table],
            flops=2 * pass_flops,
            name="near",
        )
        if last:
            outs = [shaped((nodes, width), BF16)] * 2
        else:
            outs = [shaped((2 * nodes, width), BF16)]
        edge_rows, *partial = call(
            functools.partial(edge_kernel, layer, layer == 0, last),
            [shaped((edges, width), BF16)] + outs,
            (live_edges, pre, cols, rows, edge_rows, edge_w1, edge_w2, edge_gain, *far),
            scratch=[table, messages],
            smem=(0,),
            flops=5 * pass_flops,
            name="far",
        )
        other = swapped(partial[-1])
        weights = (node_w1, node_b1, node_w2, node_gain)
        if last:
            out = call(
                functools.partial(last_kernel, layer),
                shaped((nodes, width), BF16),
                (all_nodes, partial[0], other, *weights),
                name="last",
            )
        else:
            rows_out = shaped((TILE, width), BF16)
            all_nodes, far_rows, near_rows = call(
                functools.partial(node_kernel, stride, layer),
                [shaped((2 * nodes, width), BF16), rows_out, rows_out],
                (*node_args, partial[0], other, send_rows, peer_lists, *weights),
                name="nodes",
            )
    return out, edge_rows


def shards(*args):
    node_lat, edge_lat, _, _, _, send_rows = args[:6]
    domains = lax.axis_size("dom")
    fits = (
        lax.axis_size("edge") == 2
        and domains % 8 == 0
        and node_lat.shape == (TILE, TILE)
        and edge_lat.shape[0] % ROWS == 0
        and send_rows.shape[1:] == (4, HALF)
        and args[6].shape == (LAYERS, 3 * TILE, TILE)
    )
    return (fast_shards if fits else general_shards)(*args)


def general_shards(
    node_lat,
    edge_lat,
    senders,
    receivers,
    live_edges,
    send_rows,
    edge_w1,
    edge_b1,
    edge_w2,
    edge_gain,
    node_w1,
    node_b1,
    node_w2,
    node_gain,
):
    rank_count = lax.axis_size("edge")
    domains = lax.axis_size("dom")
    stride = domains // 4
    offsets = (1, -1, stride, -stride)
    node_count = node_lat.shape[0]
    face_count = send_rows.shape[1]
    latent = node_lat.shape[1]
    live_rows = lax.broadcasted_iota(jnp.int32, (edge_lat.shape[0],), 0) < live_edges[0, 0]
    lists_all = None
    lists_all = lax.all_gather(send_rows, "edge", axis=0, tiled=True)
    lists_all = lists_all + (jnp.arange(rank_count, dtype=jnp.int32) * node_count)[:, None, None]
    owned_rows = node_lat
    edge_rows = edge_lat
    for layer_index in range(LAYERS):
        received = []
        domain_rows = lax.all_gather(owned_rows, "edge", axis=0, tiled=True)
        face_rows = jnp.take(domain_rows, lists_all, axis=0)
        for face_index in range(face_count):
            received.append(passed_along(face_rows[:, face_index], "dom", offsets[face_index]))
        halo_all = jnp.stack(received, axis=1).reshape(-1, latent)
        node_table = jnp.concatenate([domain_rows, halo_all], axis=0)
        sender_rows = jnp.take(node_table, senders, axis=0)
        receiver_rows = jnp.take(domain_rows, receivers, axis=0)
        edge_rows, messages = edge_update(
            edge_rows,
            sender_rows,
            receiver_rows,
            edge_w1[layer_index],
            edge_b1[layer_index],
            edge_w2[layer_index],
            edge_gain[layer_index],
            live_rows,
        )
        summed = lax.psum_scatter(
            jax.ops.segment_sum(
                messages, receivers, num_segments=lax.axis_size("edge") * node_count
            ).astype(jnp.bfloat16),
            "edge",
            scatter_dimension=0,
            tiled=True,
        )
        owned_rows = node_update(
            owned_rows,
            summed,
            node_w1[layer_index],
            node_b1[layer_index],
            node_w2[layer_index],
            node_gain[layer_index],
        )
    return (owned_rows, edge_rows)


def solution(mesh):
    in_specs = (
        P(("dom", "edge"), None),
        P(("dom", "edge"), None),
        P(("dom", "edge")),
        P(("dom", "edge")),
        P("dom", "edge"),
        P(("dom", "edge"), None, None),
        P(),
        P(),
        P(),
        P(),
        P(),
        P(),
        P(),
        P(),
    )
    out_specs = (P(("dom", "edge"), None), P(("dom", "edge"), None))
    return jax.shard_map(shards, mesh=mesh, in_specs=in_specs, out_specs=out_specs, check_vma=False)
```

```python
import functools

import jax
import jax.numpy as jnp
from jax import lax
from jax.experimental import pallas as pl
from jax.experimental.pallas import tpu as pltpu
from jax.sharding import PartitionSpec as P

LAYERS = 2


eps_norm = 1e-05


def passed_along(value, axis, steps):
    count = lax.axis_size(axis)
    pairs = [(source, (source + steps) % count) for source in range(count)]
    return lax.ppermute(value, axis, pairs)


def layer_norm(values, norm_gain):
    center = values - jnp.mean(values, axis=-1, keepdims=True)
    spread = jnp.mean(center * center, axis=-1, keepdims=True)
    return center * lax.rsqrt(spread + eps_norm) * norm_gain


def edge_update(
    edge_rows, sender_rows, receiver_rows, weight_in, bias_in, weight_out, norm_gain, live_rows
):
    feature_width = edge_rows.shape[1]
    pre_act = jnp.dot(edge_rows, weight_in[:feature_width], preferred_element_type=jnp.float32)
    pre_act = pre_act + jnp.dot(
        sender_rows,
        weight_in[feature_width : 2 * feature_width],
        preferred_element_type=jnp.float32,
    )
    pre_act = pre_act + jnp.dot(
        receiver_rows, weight_in[2 * feature_width :], preferred_element_type=jnp.float32
    )
    hidden_rows = jax.nn.relu(pre_act + bias_in).astype(jnp.bfloat16)
    messages = layer_norm(
        jnp.dot(hidden_rows, weight_out, preferred_element_type=jnp.float32), norm_gain
    )
    messages = jnp.where(live_rows[:, None], messages, jnp.float32(0.0))
    return ((edge_rows.astype(jnp.float32) + messages).astype(jnp.bfloat16), messages)


def node_update(node_rows, aggregate, weight_in, bias_in, weight_out, norm_gain):
    feature_width = node_rows.shape[1]
    pre_act = jnp.dot(node_rows, weight_in[:feature_width], preferred_element_type=jnp.float32)
    pre_act = pre_act + jnp.dot(
        aggregate, weight_in[feature_width:], preferred_element_type=jnp.float32
    )
    hidden_rows = jax.nn.relu(pre_act + bias_in).astype(jnp.bfloat16)
    update = layer_norm(
        jnp.dot(hidden_rows, weight_out, preferred_element_type=jnp.float32), norm_gain
    )
    return (node_rows.astype(jnp.float32) + update).astype(jnp.bfloat16)


F32 = jnp.float32
BF16 = jnp.bfloat16
TILE = 256
HALF = 128
ROWS = 512
IN_VMEM = pl.BlockSpec(memory_space=pltpu.VMEM)
IN_SMEM = pl.BlockSpec(memory_space=pltpu.SMEM)
IN_HBM = pl.BlockSpec(memory_space=pltpu.HBM)


def shaped(shape, dtype):
    return jax.ShapeDtypeStruct(shape, dtype)


def call(kernel, outs, args, scratch=(), smem=(), stay=(), flops=0, limit=24, name=None):
    nbytes = sum(a.size * a.dtype.itemsize for a in args)
    return pl.pallas_call(
        kernel,
        out_shape=outs,
        in_specs=[
            IN_SMEM if k in smem else IN_HBM if k in stay else IN_VMEM for k in range(len(args))
        ],
        out_specs=jax.tree.map(lambda _: IN_VMEM, outs),
        scratch_shapes=scratch,
        compiler_params=pltpu.CompilerParams(vmem_limit_bytes=limit << 20),
        cost_estimate=pl.CostEstimate(flops=flops, transcendentals=0, bytes_accessed=nbytes),
        name=name,
    )(*args)


def place(stride):
    dom = lax.axis_index("dom")
    core = lax.axis_index("edge")
    return core, lax.rem(dom, 2), lax.rem(lax.div(dom, stride), 2)


def mm(a, b):
    return jnp.dot(a, b, preferred_element_type=F32)


def column(row):
    return jnp.transpose(jnp.broadcast_to(row.astype(F32), (HALF, HALF)))


def one_hot_rows(row):
    col = column(row)
    lane = lax.broadcasted_iota(jnp.int32, (HALF, HALF), 1).astype(F32)
    parts = [jnp.where(col == lane + float(k), 1.0, 0.0) for k in (0, HALF)]
    return jnp.concatenate(parts, axis=1).astype(BF16)


def dyn(start, size):
    return pl.ds(pl.multiple_of(start, size), size)


def face_rows(stride, lists, nodes, far, near):
    core, par_d, par_s = place(stride)
    par = jnp.where(core == 0, par_d, par_s)
    for face, ref in ((2 * core + 1 - par, far), (2 * core + par, near)):
        for n in range(2):
            hot = one_hot_rows(lists[n][0, pl.ds(face, 1), :])
            ref[n * HALF : (n + 1) * HALF, :] = mm(hot, nodes[n]()).astype(BF16)


def pick_kernel(stride, own_ref, peer_ref, list_own, list_peer, far, near):
    nodes = (lambda: own_ref[...]), (lambda: peer_ref[...])
    face_rows(stride, (list_own, list_peer), nodes, far, near)


def index_kernel(stride, edges, loads, live_ref, *refs):
    hbm, (cols, rows), refs = refs[: loads + 2], refs[loads + 2 : loads + 4], refs[loads + 4 :]
    vmem, (send_ref, recv_ref, sems) = refs[:loads], refs[loads:]
    copies = [
        pltpu.make_async_copy(src, dst, sems.at[k])
        for k, (src, dst) in enumerate(zip(hbm, (send_ref, recv_ref, *vmem)))
    ]
    for copy in copies:
        copy.start()
    _, par_d, par_s = place(stride)
    for copy in copies[:2]:
        copy.wait()
    live = jnp.broadcast_to(live_ref[...], (1, HALF))
    lane = lax.broadcasted_iota(jnp.int32, (1, HALF), 1)
    for k in range(edges // HALF):
        at = pl.ds(k * HALF, HALF)
        v = send_ref[:, at]
        j = v - 2 * TILE
        owner = lax.shift_right_arithmetic(j, 9)
        face = lax.shift_right_arithmetic(j, 7) & 3
        core = lax.shift_right_arithmetic(face, 1)
        par = jnp.where(core == 0, par_d, par_s)
        near = (face & 1) != par
        tile = jnp.where(near, 2, 4) + core
        at_tile = ((owner ^ core) & 1) * HALF + (j & (HALF - 1))
        local = v < 2 * TILE
        hi = jnp.where(local, lax.shift_right_arithmetic(v, 8), tile)
        lo = jnp.where(local, v & (TILE - 1), at_tile)
        cols[0, at, :] = column(hi).astype(BF16)
        cols[1, at, :] = column(lo).astype(BF16)
        v = recv_ref[:, at]
        hi = lax.shift_right_arithmetic(v, 8)
        lo = v & (TILE - 1)
        cols[2, at, :] = column(hi).astype(BF16)
        cols[3, at, :] = column(lo).astype(BF16)
        rows[0:1, at] = jnp.where(lane + k * HALF < live, hi, -1).astype(F32)
        rows[1:2, at] = lo.astype(F32)
    rows[2:3, :] = jnp.concatenate([live] * (edges // HALF), axis=1).astype(F32)
    for copy in copies[2:]:
        copy.wait()


def lane_iota(rows):
    lane = lax.broadcasted_iota(jnp.int32, (rows, HALF), 1).astype(F32)
    return lane.astype(BF16), (lane + float(HALF)).astype(BF16)


def hits(hi, lo, tile, lanes):
    at = jnp.where(hi == tile, lo, jnp.asarray(-1, BF16))
    one = jnp.ones(at.shape, BF16)
    zero = jnp.zeros(at.shape, BF16)
    return jnp.concatenate([jnp.where(at == lane, one, zero) for lane in lanes], axis=1)


def local_kernel(layer, stacked, edge_ref, cols, *refs):
    if stacked:
        dom_ref, w1_ref, b1_ref, pre_ref, t_s, t_r = refs
        dom = dom_ref[...]
        t_s[...] = mm(dom, w1_ref[layer, TILE : 2 * TILE, :]).astype(BF16)
        t_r[...] = mm(dom, w1_ref[layer, 2 * TILE :, :]).astype(BF16)
    else:
        own_ref, peer_ref, w1_ref, b1_ref, pre_ref, t_s, t_r = refs
        core = lax.axis_index("edge")
        for owner, ref in ((core, own_ref), (1 - core, peer_ref)):
            at = dyn(owner * TILE, TILE)
            t_s[at, :] = mm(ref[...], w1_ref[layer, TILE : 2 * TILE, :]).astype(BF16)
            t_r[at, :] = mm(ref[...], w1_ref[layer, 2 * TILE :, :]).astype(BF16)
    lanes = lane_iota(ROWS)
    bias = b1_ref[layer : layer + 1, :]
    w_e = w1_ref[layer, 0:TILE, :]

    def step(k, carry):
        at = dyn(k * ROWS, ROWS)
        acc = mm(edge_ref[at, :], w_e)
        for base, table in ((0, t_s), (2, t_r)):
            hi = cols[base, at, :]
            lo = cols[base + 1, at, :]
            for tile in range(2):
                acc = acc + mm(
                    hits(hi, lo, jnp.asarray(tile, BF16), lanes),
                    table[tile * TILE : (tile + 1) * TILE, :],
                )
        pre_ref[at, :] = acc + bias
        return carry

    lax.fori_loop(0, edge_ref.shape[0] // ROWS, step, 0)


def halo_tables(layer, own, peer, w1_ref, table):
    core = lax.axis_index("edge")
    w_s = w1_ref[layer, TILE : 2 * TILE, :]
    for axis, ref in ((core, own), (1 - core, peer)):
        table[dyn(axis * TILE, TILE), :] = mm(ref[...], w_s).astype(BF16)


def near_kernel(layer, pre_ref, cols, w1_ref, own, peer, out_ref, table):
    halo_tables(layer, own, peer, w1_ref, table)
    lanes = lane_iota(ROWS)

    def step(k, carry):
        at = dyn(k * ROWS, ROWS)
        hi = cols[0, at, :]
        lo = cols[1, at, :]
        acc = pre_ref[at, :]
        for n in range(2):
            acc = acc + mm(
                hits(hi, lo, jnp.asarray(2 + n, BF16), lanes), table[n * TILE : (n + 1) * TILE, :]
            )
        out_ref[at, :] = acc
        return carry

    lax.fori_loop(0, pre_ref.shape[0] // ROWS, step, 0)


def edge_kernel(
    layer, split, pre_ref, cols, rows, edge_ref, w1_ref, w2_ref, gain_ref, own, peer, out_ref, *refs
):
    if split:
        keep_ref, give_ref, table, msgs = refs
    else:
        part_ref, table, msgs = refs
    halo_tables(layer, own, peer, w1_ref, table)
    lanes = lane_iota(ROWS)
    live = jnp.broadcast_to(rows[2:3, 0:TILE], (ROWS, TILE)).astype(jnp.int32)
    gain = gain_ref[layer : layer + 1, :]
    w2 = w2_ref[layer]
    place_in = lax.broadcasted_iota(jnp.int32, (ROWS, TILE), 0)

    def step(k, carry):
        at = dyn(k * ROWS, ROWS)
        hi = cols[0, at, :]
        lo = cols[1, at, :]
        acc = pre_ref[at, :]
        for n in range(2):
            acc = acc + mm(
                hits(hi, lo, jnp.asarray(4 + n, BF16), lanes), table[n * TILE : (n + 1) * TILE, :]
            )
        hidden = jnp.maximum(acc, 0.0).astype(BF16)
        message = layer_norm(mm(hidden, w2), gain)
        msgs[at, :] = message.astype(BF16)
        message = jnp.where(place_in + k * ROWS < live, message, 0.0)
        out_ref[at, :] = (edge_ref[at, :].astype(F32) + message).astype(BF16)
        return carry

    count = edge_ref.shape[0] // ROWS
    lax.fori_loop(0, count, step, 0)
    spot = lax.broadcasted_iota(jnp.int32, (TILE, ROWS), 0).astype(F32).astype(BF16)
    one = jnp.ones((TILE, ROWS), BF16)
    zero = jnp.zeros((TILE, ROWS), BF16)
    sums = [None, None]
    for k in range(count):
        at = pl.ds(k * ROWS, ROWS)
        hi = rows[0:1, at]
        lo = rows[1:2, at]
        msg = msgs[at, :]
        for n in range(2):
            here = jnp.where(hi == float(n), lo, -1.0).astype(BF16)
            hot = jnp.where(jnp.broadcast_to(here, (TILE, ROWS)) == spot, one, zero)
            part = mm(hot, msg)
            sums[n] = part if sums[n] is None else sums[n] + part
    if split:
        core = lax.axis_index("edge")
        mine = core == 0
        keep_ref[...] = jnp.where(mine, sums[0], sums[1]).astype(BF16)
        give_ref[...] = jnp.where(mine, sums[1], sums[0]).astype(BF16)
    else:
        for n in range(2):
            part_ref[n * TILE : (n + 1) * TILE, :] = sums[n].astype(BF16)


def updated(layer, nodes, first, second, w1_ref, b1_ref, w2_ref, gain_ref):
    total = (first.astype(F32) + second.astype(F32)).astype(BF16)
    pre = mm(nodes, w1_ref[layer, 0:TILE, :]) + mm(total, w1_ref[layer, TILE:, :])
    hidden = jnp.maximum(pre + b1_ref[layer : layer + 1, :], 0.0).astype(BF16)
    step = layer_norm(mm(hidden, w2_ref[layer]), gain_ref[layer : layer + 1, :])
    return (nodes.astype(F32) + step).astype(BF16)


def node_kernel(
    stride, layer, own_ref, peer_ref, first, second, list_own, list_peer, w1, b1, w2, gain, out, far, near
):
    core = lax.axis_index("edge")
    for owner, ref in ((core, own_ref), (1 - core, peer_ref)):
        at = dyn(owner * TILE, TILE)
        out[at, :] = updated(layer, ref[...], first[at, :], second[at, :], w1, b1, w2, gain)
    nodes = [
        functools.partial(out.__getitem__, (dyn(owner * TILE, TILE), slice(None)))
        for owner in (core, 1 - core)
    ]
    face_rows(stride, (list_own, list_peer), nodes, far, near)


def last_kernel(layer, nodes_ref, first, second, w1, b1, w2, gain, out):
    core = lax.axis_index("edge")
    nodes = nodes_ref[dyn(core * TILE, TILE), :]
    out[...] = updated(layer, nodes, first[...], second[...], w1, b1, w2, gain)


def met(count, stride, odd):
    pairs = []
    for dom in range(count):
        ahead = (dom // stride) % 2 == odd
        pairs.append((dom + (stride if ahead else -stride)) % count)
    return pairs


def swapped(value):
    return lax.ppermute(value, "edge", [(0, 1), (1, 0)])


def fast_shards(
    node_lat,
    edge_lat,
    senders,
    receivers,
    live_edges,
    send_rows,
    edge_w1,
    edge_b1,
    edge_w2,
    edge_gain,
    node_w1,
    node_b1,
    node_w2,
    node_gain,
):
    domains = lax.axis_size("dom")
    stride = domains // 4
    edges, width = edge_lat.shape
    nodes = node_lat.shape[0]
    near_d, far_d = met(domains, 1, 0), met(domains, 1, 1)
    near_s, far_s = met(domains, stride, 0), met(domains, stride, 1)

    def sent_by_core(value, partner_d, partner_s):
        pairs = [(2 * d, 2 * p) for d, p in enumerate(partner_d)]
        pairs += [(2 * d + 1, 2 * p + 1) for d, p in enumerate(partner_s)]
        return lax.ppermute(value, ("dom", "edge"), pairs)

    table = pltpu.VMEM((2 * TILE, width), BF16)
    messages = pltpu.VMEM((edges, width), BF16)
    pre_shape = shaped((edges, width), F32)
    rows_out = shaped((TILE, width), BF16)
    pass_flops = 2 * edges * TILE * width

    peer_nodes = swapped(node_lat)
    peer_lists = swapped(send_rows)
    loads = (edge_lat, edge_w1, edge_w2, node_w1, node_w2, edge_b1, edge_gain, node_b1, node_gain)
    hbm = [pltpu.with_memory_space_constraint(a, pltpu.HBM) for a in (senders[None], receivers[None], *loads)]
    cols, rows, edge_rows, edge_w1, edge_w2, node_w1, node_w2, edge_b1, edge_gain, node_b1, node_gain = call(
        functools.partial(index_kernel, stride, edges, len(loads)),
        [shaped((4, edges, HALF), BF16), shaped((3, edges), F32)]
        + [shaped(a.shape, a.dtype) for a in loads],
        (live_edges, *hbm),
        scratch=[pltpu.VMEM((1, edges), jnp.int32)] * 2 + [pltpu.SemaphoreType.DMA((len(hbm),))],
        stay=range(1, len(hbm) + 1),
        name="index",
    )
    far_rows, near_rows = call(
        functools.partial(pick_kernel, stride),
        [rows_out, rows_out],
        (node_lat, peer_nodes, send_rows, peer_lists),
        name="pick",
    )
    for layer in range(LAYERS):
        last = layer == LAYERS - 1
        node_args = (all_nodes,) if layer else (node_lat, peer_nodes)
        far = sent_by_core(far_rows, far_d, far_s)
        near = sent_by_core(near_rows, near_d, near_s)
        pre = call(
            functools.partial(local_kernel, layer, layer > 0),
            pre_shape,
            (edge_rows, cols, *node_args, edge_w1, edge_b1),
            scratch=[table, table],
            flops=5 * pass_flops,
            name="local",
        )
        pre, near, far = lax.optimization_barrier((pre, near, far))
        near = (near, swapped(near))
        far = (far, swapped(far))
        pre = call(
            functools.partial(near_kernel, layer),
            pre_shape,
            (pre, cols, edge_w1, *near),
            scratch=[table],
            flops=2 * pass_flops,
            name="near",
        )
        if last:
            outs = [shaped((nodes, width), BF16)] * 2
        else:
            outs = [shaped((2 * nodes, width), BF16)]
        edge_rows, *partial = call(
            functools.partial(edge_kernel, layer, last),
            [shaped((edges, width), BF16)] + outs,
            (pre, cols, rows, edge_rows, edge_w1, edge_w2, edge_gain, *far),
            scratch=[table, messages],
            flops=5 * pass_flops,
            name="far",
        )
        other = swapped(partial[-1])
        weights = (node_w1, node_b1, node_w2, node_gain)
        if last:
            out = call(
                functools.partial(last_kernel, layer),
                shaped((nodes, width), BF16),
                (all_nodes, partial[0], other, *weights),
                name="last",
            )
        else:
            all_nodes, far_rows, near_rows = call(
                functools.partial(node_kernel, stride, layer),
                [shaped((2 * nodes, width), BF16), rows_out, rows_out],
                (*node_args, partial[0], other, send_rows, peer_lists, *weights),
                name="nodes",
            )
    return out, edge_rows


def shards(*args):
    node_lat, edge_lat, _, _, _, send_rows = args[:6]
    domains = lax.axis_size("dom")
    fits = (
        lax.axis_size("edge") == 2
        and domains % 8 == 0
        and node_lat.shape == (TILE, TILE)
        and edge_lat.shape[0] % ROWS == 0
        and send_rows.shape[1:] == (4, HALF)
        and args[6].shape == (LAYERS, 3 * TILE, TILE)
    )
    return (fast_shards if fits else general_shards)(*args)


def general_shards(
    node_lat,
    edge_lat,
    senders,
    receivers,
    live_edges,
    send_rows,
    edge_w1,
    edge_b1,
    edge_w2,
    edge_gain,
    node_w1,
    node_b1,
    node_w2,
    node_gain,
):
    rank_count = lax.axis_size("edge")
    domains = lax.axis_size("dom")
    stride = domains // 4
    offsets = (1, -1, stride, -stride)
    node_count = node_lat.shape[0]
    face_count = send_rows.shape[1]
    latent = node_lat.shape[1]
    live_rows = lax.broadcasted_iota(jnp.int32, (edge_lat.shape[0],), 0) < live_edges[0, 0]
    lists_all = None
    lists_all = lax.all_gather(send_rows, "edge", axis=0, tiled=True)
    lists_all = lists_all + (jnp.arange(rank_count, dtype=jnp.int32) * node_count)[:, None, None]
    owned_rows = node_lat
    edge_rows = edge_lat
    for layer_index in range(LAYERS):
        received = []
        domain_rows = lax.all_gather(owned_rows, "edge", axis=0, tiled=True)
        face_rows = jnp.take(domain_rows, lists_all, axis=0)
        for face_index in range(face_count):
            received.append(passed_along(face_rows[:, face_index], "dom", offsets[face_index]))
        halo_all = jnp.stack(received, axis=1).reshape(-1, latent)
        node_table = jnp.concatenate([domain_rows, halo_all], axis=0)
        sender_rows = jnp.take(node_table, senders, axis=0)
        receiver_rows = jnp.take(domain_rows, receivers, axis=0)
        edge_rows, messages = edge_update(
            edge_rows,
            sender_rows,
            receiver_rows,
            edge_w1[layer_index],
            edge_b1[layer_index],
            edge_w2[layer_index],
            edge_gain[layer_index],
            live_rows,
        )
        summed = lax.psum_scatter(
            jax.ops.segment_sum(
                messages, receivers, num_segments=lax.axis_size("edge") * node_count
            ).astype(jnp.bfloat16),
            "edge",
            scatter_dimension=0,
            tiled=True,
        )
        owned_rows = node_update(
            owned_rows,
            summed,
            node_w1[layer_index],
            node_b1[layer_index],
            node_w2[layer_index],
            node_gain[layer_index],
        )
    return (owned_rows, edge_rows)


def solution(mesh):
    in_specs = (
        P(("dom", "edge"), None),
        P(("dom", "edge"), None),
        P(("dom", "edge")),
        P(("dom", "edge")),
        P("dom", "edge"),
        P(("dom", "edge"), None, None),
        P(),
        P(),
        P(),
        P(),
        P(),
        P(),
        P(),
        P(),
    )
    out_specs = (P(("dom", "edge"), None), P(("dom", "edge"), None))
    return jax.shard_map(shards, mesh=mesh, in_specs=in_specs, out_specs=out_specs, check_vma=False)
```

```python
import functools

import jax
import jax.numpy as jnp
from jax import lax
from jax.experimental import pallas as pl
from jax.experimental.pallas import tpu as pltpu
from jax.sharding import PartitionSpec as P

LAYERS = 2


eps_norm = 1e-05


def passed_along(value, axis, steps):
    count = lax.axis_size(axis)
    pairs = [(source, (source + steps) % count) for source in range(count)]
    return lax.ppermute(value, axis, pairs)


def layer_norm(values, norm_gain):
    center = values - jnp.mean(values, axis=-1, keepdims=True)
    spread = jnp.mean(center * center, axis=-1, keepdims=True)
    return center * lax.rsqrt(spread + eps_norm) * norm_gain


def edge_update(
    edge_rows, sender_rows, receiver_rows, weight_in, bias_in, weight_out, norm_gain, live_rows
):
    feature_width = edge_rows.shape[1]
    pre_act = jnp.dot(edge_rows, weight_in[:feature_width], preferred_element_type=jnp.float32)
    pre_act = pre_act + jnp.dot(
        sender_rows,
        weight_in[feature_width : 2 * feature_width],
        preferred_element_type=jnp.float32,
    )
    pre_act = pre_act + jnp.dot(
        receiver_rows, weight_in[2 * feature_width :], preferred_element_type=jnp.float32
    )
    hidden_rows = jax.nn.relu(pre_act + bias_in).astype(jnp.bfloat16)
    messages = layer_norm(
        jnp.dot(hidden_rows, weight_out, preferred_element_type=jnp.float32), norm_gain
    )
    messages = jnp.where(live_rows[:, None], messages, jnp.float32(0.0))
    return ((edge_rows.astype(jnp.float32) + messages).astype(jnp.bfloat16), messages)


def node_update(node_rows, aggregate, weight_in, bias_in, weight_out, norm_gain):
    feature_width = node_rows.shape[1]
    pre_act = jnp.dot(node_rows, weight_in[:feature_width], preferred_element_type=jnp.float32)
    pre_act = pre_act + jnp.dot(
        aggregate, weight_in[feature_width:], preferred_element_type=jnp.float32
    )
    hidden_rows = jax.nn.relu(pre_act + bias_in).astype(jnp.bfloat16)
    update = layer_norm(
        jnp.dot(hidden_rows, weight_out, preferred_element_type=jnp.float32), norm_gain
    )
    return (node_rows.astype(jnp.float32) + update).astype(jnp.bfloat16)


F32 = jnp.float32
BF16 = jnp.bfloat16
TILE = 256
HALF = 128
ROWS = 512
LOCAL_ROWS = 1024
I16 = jnp.int16
IN_VMEM = pl.BlockSpec(memory_space=pltpu.VMEM)
IN_SMEM = pl.BlockSpec(memory_space=pltpu.SMEM)
IN_HBM = pl.BlockSpec(memory_space=pltpu.HBM)


def shaped(shape, dtype):
    return jax.ShapeDtypeStruct(shape, dtype)


def call(kernel, outs, args, scratch=(), smem=(), stay=(), flops=0, limit=24, name=None):
    nbytes = sum(a.size * a.dtype.itemsize for a in args)
    return pl.pallas_call(
        kernel,
        out_shape=outs,
        in_specs=[
            IN_SMEM if k in smem else IN_HBM if k in stay else IN_VMEM for k in range(len(args))
        ],
        out_specs=jax.tree.map(lambda _: IN_VMEM, outs),
        scratch_shapes=scratch,
        compiler_params=pltpu.CompilerParams(vmem_limit_bytes=limit << 20),
        cost_estimate=pl.CostEstimate(flops=flops, transcendentals=0, bytes_accessed=nbytes),
        name=name,
    )(*args)


def place(stride):
    dom = lax.axis_index("dom")
    core = lax.axis_index("edge")
    return core, lax.rem(dom, 2), lax.rem(lax.div(dom, stride), 2)


def mm(a, b):
    return jnp.dot(a, b, preferred_element_type=F32)


def column(row):
    return jnp.transpose(jnp.broadcast_to(row, (HALF, HALF)))


def one_hot_rows(row):
    col = column(row)
    lane = lax.broadcasted_iota(jnp.int32, (HALF, HALF), 1)
    parts = [jnp.where(col == lane + k, 1.0, 0.0) for k in (0, HALF)]
    return jnp.concatenate(parts, axis=1).astype(BF16)


def dyn(start, size, unit=None):
    return pl.ds(pl.multiple_of(start, unit or size), size)


def face_rows(stride, lists, nodes, far, near):
    core, par_d, par_s = place(stride)
    par = jnp.where(core == 0, par_d, par_s)
    for face, ref in ((2 * core + 1 - par, far), (2 * core + par, near)):
        for n in range(2):
            hot = one_hot_rows(lists[n][0, pl.ds(face, 1), :])
            ref[n * HALF : (n + 1) * HALF, :] = mm(hot, nodes[n]()).astype(BF16)


def pick_kernel(stride, own_ref, peer_ref, list_own, list_peer, far, near):
    nodes = (lambda: own_ref[...]), (lambda: peer_ref[...])
    face_rows(stride, (list_own, list_peer), nodes, far, near)


def index_kernel(stride, edges, loads, *refs):
    hbm, cols, refs = refs[: loads + 2], refs[loads + 2], refs[loads + 3 :]
    recv_ref, vmem, (send_ref, sems) = refs[0], refs[1 : loads + 1], refs[loads + 1 :]
    copies = [
        pltpu.make_async_copy(src, dst, sems.at[k])
        for k, (src, dst) in enumerate(zip(hbm, (send_ref, recv_ref, *vmem)))
    ]
    for copy in copies:
        copy.start()
    _, par_d, par_s = place(stride)
    for copy in copies[:2]:
        copy.wait()
    for k in range(edges // HALF):
        at = pl.ds(k * HALF, HALF)
        v = send_ref[:, at]
        j = v - 2 * TILE
        owner = lax.shift_right_arithmetic(j, 9)
        face = lax.shift_right_arithmetic(j, 7) & 3
        core = lax.shift_right_arithmetic(face, 1)
        par = jnp.where(core == 0, par_d, par_s)
        near = (face & 1) != par
        tile = jnp.where(near, 2, 4) + core
        at_tile = ((owner ^ core) & 1) * HALF + (j & (HALF - 1))
        spot = jnp.where(v < 2 * TILE, v, tile * TILE + at_tile)
        cols[0, at, :] = column(spot).astype(I16)
        cols[1, at, :] = column(recv_ref[:, at]).astype(I16)
    for copy in copies[2:]:
        copy.wait()


def hits(spots, first, tiles):
    one = jnp.ones(spots.shape, BF16)
    zero = jnp.zeros(spots.shape, BF16)
    lane = lax.broadcasted_iota(jnp.int32, spots.shape, 1)
    parts = [
        jnp.where(spots == (lane + (first * TILE + k * HALF)).astype(I16), one, zero)
        for k in range(2 * tiles)
    ]
    return jnp.concatenate(parts, axis=1)


def local_kernel(layer, edge_ref, cols, *refs):
    if layer:
        dom_ref, w1_ref, b1_ref, pre_ref, table = refs
        parts = ((0, 2 * TILE, dom_ref),)
    else:
        own_ref, peer_ref, w1_ref, b1_ref, pre_ref, table = refs
        core = lax.axis_index("edge")
        parts = ((core * TILE, TILE, own_ref), ((1 - core) * TILE, TILE, peer_ref))
    for k in (1, 2):
        for start, size, ref in parts:
            table[dyn((2 * k - 2) * TILE + start, size, TILE), :] = mm(
                ref[...], w1_ref[layer, k * TILE : (k + 1) * TILE, :]
            ).astype(BF16)
    bias = b1_ref[layer : layer + 1, :]

    def step(k, carry):
        at = dyn(k * LOCAL_ROWS, LOCAL_ROWS)
        acc = mm(edge_ref[at, :], w1_ref[layer, 0:TILE, :])
        acc = acc + mm(hits(cols[0, at, :], 0, 2), table[0 : 2 * TILE, :])
        acc = acc + mm(hits(cols[1, at, :], 0, 2), table[2 * TILE :, :])
        pre_ref[at, :] = acc + bias
        return carry

    lax.fori_loop(0, edge_ref.shape[0] // LOCAL_ROWS, step, 0)


def halo_tables(layer, own, peer, w1_ref, table):
    core = lax.axis_index("edge")
    w_s = w1_ref[layer, TILE : 2 * TILE, :]
    for axis, ref in ((core, own), (1 - core, peer)):
        table[dyn(axis * TILE, TILE), :] = mm(ref[...], w_s).astype(BF16)


def near_kernel(layer, pre_ref, cols, w1_ref, own, peer, out_ref, table):
    halo_tables(layer, own, peer, w1_ref, table)

    def step(k, carry):
        at = dyn(k * LOCAL_ROWS, LOCAL_ROWS)
        out_ref[at, :] = pre_ref[at, :] + mm(hits(cols[0, at, :], 2, 2), table[...])
        return carry

    lax.fori_loop(0, pre_ref.shape[0] // LOCAL_ROWS, step, 0)


def edge_kernel(
    layer, split, live_ref, pre_ref, cols, recv_ref, edge_ref, w1_ref, w2_ref, gain_ref, own, peer, out_ref, *refs
):
    if split:
        keep_ref, give_ref, table, raw, msgs, sums = refs
    else:
        part_ref, table, raw, msgs, sums = refs
    halo_tables(layer, own, peer, w1_ref, table)
    gain = gain_ref[layer : layer + 1, :]
    live = live_ref[0, 0]
    count = edge_ref.shape[0] // ROWS

    def gather(at):
        acc = pre_ref[at, :] + mm(hits(cols[0, at, :], 4, 2), table[...])
        hidden = jnp.maximum(acc.astype(BF16), jnp.asarray(0, BF16))
        raw[at, :] = mm(hidden, w2_ref[layer])

    def norm(at, first):
        values = raw[at, :]
        center = values - jnp.mean(values, axis=-1, keepdims=True)
        spread = jnp.mean(center * center, axis=-1, keepdims=True)
        scale = lax.rsqrt(spread + eps_norm)
        row = lax.broadcasted_iota(jnp.int32, scale.shape, 0) + first
        scale = jnp.where(row < live, scale, 0.0)
        message = (center * scale * gain).astype(BF16)
        msgs[at, :] = message
        out_ref[at, :] = edge_ref[at, :] + message

    def segment(at, first):
        shape = (2 * TILE, ROWS)
        spot = lax.broadcasted_iota(jnp.int32, shape, 0).astype(I16)
        here = jnp.broadcast_to(recv_ref[:, at].astype(I16), shape)
        hot = jnp.where(here == spot, jnp.ones(shape, BF16), jnp.zeros(shape, BF16))
        part = mm(hot, msgs[at, :])
        sums[...] = part if first else sums[...] + part

    for k in range(count + 2):
        if k >= 2:
            segment(pl.ds((k - 2) * ROWS, ROWS), k == 2)
        if 1 <= k <= count:
            norm(pl.ds((k - 1) * ROWS, ROWS), (k - 1) * ROWS)
        if k < count:
            gather(pl.ds(k * ROWS, ROWS))
    if split:
        core = lax.axis_index("edge")
        keep_ref[...] = sums[dyn(core * TILE, TILE), :].astype(BF16)
        give_ref[...] = sums[dyn((1 - core) * TILE, TILE), :].astype(BF16)
    else:
        part_ref[...] = sums[...].astype(BF16)


def updated(layer, nodes, first, second, w1_ref, b1_ref, w2_ref, gain_ref):
    total = (first.astype(F32) + second.astype(F32)).astype(BF16)
    pre = mm(nodes, w1_ref[layer, 0:TILE, :]) + mm(total, w1_ref[layer, TILE:, :])
    hidden = jnp.maximum(pre + b1_ref[layer : layer + 1, :], 0.0).astype(BF16)
    step = layer_norm(mm(hidden, w2_ref[layer]), gain_ref[layer : layer + 1, :])
    return (nodes.astype(F32) + step).astype(BF16)


def node_kernel(
    stride, layer, own_ref, peer_ref, first, second, list_own, list_peer, w1, b1, w2, gain, out, far, near
):
    core = lax.axis_index("edge")
    for owner, ref in ((core, own_ref), (1 - core, peer_ref)):
        at = dyn(owner * TILE, TILE)
        out[at, :] = updated(layer, ref[...], first[at, :], second[at, :], w1, b1, w2, gain)
    nodes = [
        functools.partial(out.__getitem__, (dyn(owner * TILE, TILE), slice(None)))
        for owner in (core, 1 - core)
    ]
    face_rows(stride, (list_own, list_peer), nodes, far, near)


def last_kernel(layer, nodes_ref, first, second, w1, b1, w2, gain, out):
    core = lax.axis_index("edge")
    nodes = nodes_ref[dyn(core * TILE, TILE), :]
    out[...] = updated(layer, nodes, first[...], second[...], w1, b1, w2, gain)


def met(count, stride, odd):
    pairs = []
    for dom in range(count):
        ahead = (dom // stride) % 2 == odd
        pairs.append((dom + (stride if ahead else -stride)) % count)
    return pairs


def swapped(value):
    return lax.ppermute(value, "edge", [(0, 1), (1, 0)])


def fast_shards(
    node_lat,
    edge_lat,
    senders,
    receivers,
    live_edges,
    send_rows,
    edge_w1,
    edge_b1,
    edge_w2,
    edge_gain,
    node_w1,
    node_b1,
    node_w2,
    node_gain,
):
    domains = lax.axis_size("dom")
    stride = domains // 4
    edges, width = edge_lat.shape
    nodes = node_lat.shape[0]
    near_d, far_d = met(domains, 1, 0), met(domains, 1, 1)
    near_s, far_s = met(domains, stride, 0), met(domains, stride, 1)

    def sent_by_core(value, partner_d, partner_s):
        pairs = [(2 * d, 2 * p) for d, p in enumerate(partner_d)]
        pairs += [(2 * d + 1, 2 * p + 1) for d, p in enumerate(partner_s)]
        return lax.ppermute(value, ("dom", "edge"), pairs)

    table = pltpu.VMEM((2 * TILE, width), BF16)
    messages = pltpu.VMEM((edges, width), BF16)
    pre_shape = shaped((edges, width), F32)
    rows_out = shaped((TILE, width), BF16)
    pass_flops = 2 * edges * TILE * width

    peer_nodes = swapped(node_lat)
    peer_lists = swapped(send_rows)
    loads = (edge_lat, edge_w1, edge_w2, node_w1, node_w2, edge_b1, edge_gain, node_b1, node_gain)
    hbm = [pltpu.with_memory_space_constraint(a, pltpu.HBM) for a in (senders[None], receivers[None], *loads)]
    cols, recv_row, edge_rows, edge_w1, edge_w2, node_w1, node_w2, edge_b1, edge_gain, node_b1, node_gain = call(
        functools.partial(index_kernel, stride, edges, len(loads)),
        [shaped((2, edges, HALF), I16), shaped((1, edges), jnp.int32)]
        + [shaped(a.shape, a.dtype) for a in loads],
        hbm,
        scratch=[pltpu.VMEM((1, edges), jnp.int32), pltpu.SemaphoreType.DMA((len(hbm),))],
        stay=range(len(hbm)),
        name="index",
    )
    far_rows, near_rows = call(
        functools.partial(pick_kernel, stride),
        [rows_out, rows_out],
        (node_lat, peer_nodes, send_rows, peer_lists),
        name="pick",
    )
    for layer in range(LAYERS):
        last = layer == LAYERS - 1
        node_args = (all_nodes,) if layer else (node_lat, peer_nodes)
        near = sent_by_core(near_rows, near_d, near_s)
        far = sent_by_core(far_rows, far_d, far_s)
        pre = call(
            functools.partial(local_kernel, layer),
            pre_shape,
            (edge_rows, cols, *node_args, edge_w1, edge_b1),
            scratch=[pltpu.VMEM((4 * TILE, width), BF16)],
            flops=5 * pass_flops,
            name="local",
        )
        pre, near, far, live_edges = lax.optimization_barrier((pre, near, far, live_edges))
        near = (near, swapped(near))
        far = (far, swapped(far))
        pre = call(
            functools.partial(near_kernel, layer),
            pre_shape,
            (pre, cols, edge_w1, *near),
            scratch=[table],
            flops=2 * pass_flops,
            name="near",
        )
        if last:
            outs = [shaped((nodes, width), BF16)] * 2
        else:
            outs = [shaped((2 * nodes, width), BF16)]
        edge_rows, *partial = call(
            functools.partial(edge_kernel, layer, last),
            [shaped((edges, width), BF16)] + outs,
            (live_edges, pre, cols, recv_row, edge_rows, edge_w1, edge_w2, edge_gain, *far),
            scratch=[table, pltpu.VMEM((edges, width), F32), messages, pltpu.VMEM((2 * nodes, width), F32)],
            smem=(0,),
            flops=5 * pass_flops,
            name="far",
        )
        other = swapped(partial[-1])
        weights = (node_w1, node_b1, node_w2, node_gain)
        if last:
            out = call(
                functools.partial(last_kernel, layer),
                shaped((nodes, width), BF16),
                (all_nodes, partial[0], other, *weights),
                name="last",
            )
        else:
            all_nodes, far_rows, near_rows = call(
                functools.partial(node_kernel, stride, layer),
                [shaped((2 * nodes, width), BF16), rows_out, rows_out],
                (*node_args, partial[0], other, send_rows, peer_lists, *weights),
                name="nodes",
            )
    return out, edge_rows


def shards(*args):
    node_lat, edge_lat, _, _, _, send_rows = args[:6]
    domains = lax.axis_size("dom")
    fits = (
        lax.axis_size("edge") == 2
        and domains % 8 == 0
        and node_lat.shape == (TILE, TILE)
        and edge_lat.shape[0] % ROWS == 0
        and send_rows.shape[1:] == (4, HALF)
        and args[6].shape == (LAYERS, 3 * TILE, TILE)
    )
    return (fast_shards if fits else general_shards)(*args)


def general_shards(
    node_lat,
    edge_lat,
    senders,
    receivers,
    live_edges,
    send_rows,
    edge_w1,
    edge_b1,
    edge_w2,
    edge_gain,
    node_w1,
    node_b1,
    node_w2,
    node_gain,
):
    rank_count = lax.axis_size("edge")
    domains = lax.axis_size("dom")
    stride = domains // 4
    offsets = (1, -1, stride, -stride)
    node_count = node_lat.shape[0]
    face_count = send_rows.shape[1]
    latent = node_lat.shape[1]
    live_rows = lax.broadcasted_iota(jnp.int32, (edge_lat.shape[0],), 0) < live_edges[0, 0]
    lists_all = None
    lists_all = lax.all_gather(send_rows, "edge", axis=0, tiled=True)
    lists_all = lists_all + (jnp.arange(rank_count, dtype=jnp.int32) * node_count)[:, None, None]
    owned_rows = node_lat
    edge_rows = edge_lat
    for layer_index in range(LAYERS):
        received = []
        domain_rows = lax.all_gather(owned_rows, "edge", axis=0, tiled=True)
        face_rows = jnp.take(domain_rows, lists_all, axis=0)
        for face_index in range(face_count):
            received.append(passed_along(face_rows[:, face_index], "dom", offsets[face_index]))
        halo_all = jnp.stack(received, axis=1).reshape(-1, latent)
        node_table = jnp.concatenate([domain_rows, halo_all], axis=0)
        sender_rows = jnp.take(node_table, senders, axis=0)
        receiver_rows = jnp.take(domain_rows, receivers, axis=0)
        edge_rows, messages = edge_update(
            edge_rows,
            sender_rows,
            receiver_rows,
            edge_w1[layer_index],
            edge_b1[layer_index],
            edge_w2[layer_index],
            edge_gain[layer_index],
            live_rows,
        )
        summed = lax.psum_scatter(
            jax.ops.segment_sum(
                messages, receivers, num_segments=lax.axis_size("edge") * node_count
            ).astype(jnp.bfloat16),
            "edge",
            scatter_dimension=0,
            tiled=True,
        )
        owned_rows = node_update(
            owned_rows,
            summed,
            node_w1[layer_index],
            node_b1[layer_index],
            node_w2[layer_index],
            node_gain[layer_index],
        )
    return (owned_rows, edge_rows)


def solution(mesh):
    in_specs = (
        P(("dom", "edge"), None),
        P(("dom", "edge"), None),
        P(("dom", "edge")),
        P(("dom", "edge")),
        P("dom", "edge"),
        P(("dom", "edge"), None, None),
        P(),
        P(),
        P(),
        P(),
        P(),
        P(),
        P(),
        P(),
    )
    out_specs = (P(("dom", "edge"), None), P(("dom", "edge"), None))
    return jax.shard_map(shards, mesh=mesh, in_specs=in_specs, out_specs=out_specs, check_vma=False)
```

```python
import functools

import jax
import jax.numpy as jnp
from jax import lax
from jax.experimental import pallas as pl
from jax.experimental.pallas import tpu as pltpu
from jax.sharding import PartitionSpec as P

LAYERS = 2


eps_norm = 1e-05


def passed_along(value, axis, steps):
    count = lax.axis_size(axis)
    pairs = [(source, (source + steps) % count) for source in range(count)]
    return lax.ppermute(value, axis, pairs)


def layer_norm(values, norm_gain):
    center = values - jnp.mean(values, axis=-1, keepdims=True)
    spread = jnp.mean(center * center, axis=-1, keepdims=True)
    return center * lax.rsqrt(spread + eps_norm) * norm_gain


def edge_update(
    edge_rows, sender_rows, receiver_rows, weight_in, bias_in, weight_out, norm_gain, live_rows
):
    feature_width = edge_rows.shape[1]
    pre_act = jnp.dot(edge_rows, weight_in[:feature_width], preferred_element_type=jnp.float32)
    pre_act = pre_act + jnp.dot(
        sender_rows,
        weight_in[feature_width : 2 * feature_width],
        preferred_element_type=jnp.float32,
    )
    pre_act = pre_act + jnp.dot(
        receiver_rows, weight_in[2 * feature_width :], preferred_element_type=jnp.float32
    )
    hidden_rows = jax.nn.relu(pre_act + bias_in).astype(jnp.bfloat16)
    messages = layer_norm(
        jnp.dot(hidden_rows, weight_out, preferred_element_type=jnp.float32), norm_gain
    )
    messages = jnp.where(live_rows[:, None], messages, jnp.float32(0.0))
    return ((edge_rows.astype(jnp.float32) + messages).astype(jnp.bfloat16), messages)


def node_update(node_rows, aggregate, weight_in, bias_in, weight_out, norm_gain):
    feature_width = node_rows.shape[1]
    pre_act = jnp.dot(node_rows, weight_in[:feature_width], preferred_element_type=jnp.float32)
    pre_act = pre_act + jnp.dot(
        aggregate, weight_in[feature_width:], preferred_element_type=jnp.float32
    )
    hidden_rows = jax.nn.relu(pre_act + bias_in).astype(jnp.bfloat16)
    update = layer_norm(
        jnp.dot(hidden_rows, weight_out, preferred_element_type=jnp.float32), norm_gain
    )
    return (node_rows.astype(jnp.float32) + update).astype(jnp.bfloat16)


F32 = jnp.float32
BF16 = jnp.bfloat16
TILE = 256
HALF = 128
ROWS = 512
LOCAL_ROWS = 1024
I16 = jnp.int16
IN_VMEM = pl.BlockSpec(memory_space=pltpu.VMEM)
IN_SMEM = pl.BlockSpec(memory_space=pltpu.SMEM)
IN_HBM = pl.BlockSpec(memory_space=pltpu.HBM)


def shaped(shape, dtype):
    return jax.ShapeDtypeStruct(shape, dtype)


def call(kernel, outs, args, scratch=(), smem=(), stay=(), leave=(), flops=0, limit=24, name=None):
    nbytes = sum(a.size * a.dtype.itemsize for a in args)
    return pl.pallas_call(
        kernel,
        out_shape=outs,
        in_specs=[
            IN_SMEM if k in smem else IN_HBM if k in stay else IN_VMEM for k in range(len(args))
        ],
        out_specs=[IN_HBM if k in leave else IN_VMEM for k in range(len(outs))]
        if isinstance(outs, list)
        else IN_VMEM,
        scratch_shapes=scratch,
        compiler_params=pltpu.CompilerParams(vmem_limit_bytes=limit << 20),
        cost_estimate=pl.CostEstimate(flops=flops, transcendentals=0, bytes_accessed=nbytes),
        name=name,
    )(*args)


def place(stride):
    dom = lax.axis_index("dom")
    core = lax.axis_index("edge")
    return core, lax.rem(dom, 2), lax.rem(lax.div(dom, stride), 2)


def mm(a, b):
    return jnp.dot(a, b, preferred_element_type=F32)


def column(row):
    return jnp.transpose(jnp.broadcast_to(row, (HALF, HALF)))


def one_hot_rows(row):
    col = column(row)
    lane = lax.broadcasted_iota(jnp.int32, (HALF, HALF), 1)
    parts = [jnp.where(col == lane + k, 1.0, 0.0) for k in (0, HALF)]
    return jnp.concatenate(parts, axis=1).astype(BF16)


def dyn(start, size, unit=None):
    return pl.ds(pl.multiple_of(start, unit or size), size)


def face_rows(stride, lists, nodes, far, near):
    core, par_d, par_s = place(stride)
    par = jnp.where(core == 0, par_d, par_s)
    for face, ref in ((2 * core + 1 - par, far), (2 * core + par, near)):
        for n in range(2):
            hot = one_hot_rows(lists[n][0, pl.ds(face, 1), :])
            ref[n * HALF : (n + 1) * HALF, :] = mm(hot, nodes[n]).astype(BF16)


def pick_kernel(stride, own_ref, peer_ref, list_own, list_peer, far, near):
    face_rows(stride, (list_own, list_peer), (own_ref[...], peer_ref[...]), far, near)


def load_kernel(count, *refs):
    hbm, vmem, sems = refs[:count], refs[count:-1], refs[-1]
    copies = [
        pltpu.make_async_copy(src, dst, sems.at[k]) for k, (src, dst) in enumerate(zip(hbm, vmem))
    ]
    for copy in copies:
        copy.start()
    for copy in copies:
        copy.wait()


def in_hbm(arrays):
    return [pltpu.with_memory_space_constraint(a, pltpu.HBM) for a in arrays]


def index_kernel(stride, edges, loads, *refs):
    hbm, cols, refs = refs[: loads + 2], refs[loads + 2], refs[loads + 3 :]
    recv_ref, vmem, (send_ref, sems) = refs[0], refs[1 : loads + 1], refs[loads + 1 :]
    copies = [
        pltpu.make_async_copy(src, dst, sems.at[k])
        for k, (src, dst) in enumerate(zip(hbm, (send_ref, recv_ref, *vmem)))
    ]
    for copy in copies:
        copy.start()
    _, par_d, par_s = place(stride)
    for copy in copies[:2]:
        copy.wait()
    for k in range(edges // HALF):
        at = pl.ds(k * HALF, HALF)
        v = send_ref[:, at]
        j = v - 2 * TILE
        owner = lax.shift_right_arithmetic(j, 9)
        face = lax.shift_right_arithmetic(j, 7) & 3
        core = lax.shift_right_arithmetic(face, 1)
        par = jnp.where(core == 0, par_d, par_s)
        near = (face & 1) != par
        tile = jnp.where(near, 2, 4) + core
        at_tile = ((owner ^ core) & 1) * HALF + (j & (HALF - 1))
        spot = jnp.where(v < 2 * TILE, v, tile * TILE + at_tile)
        cols[0, at, :] = column(spot).astype(I16)
        cols[1, at, :] = column(recv_ref[:, at]).astype(I16)
    for copy in copies[2:]:
        copy.wait()


def hits(spots, first, tiles):
    one = jnp.ones(spots.shape, BF16)
    zero = jnp.zeros(spots.shape, BF16)
    lane = lax.broadcasted_iota(jnp.int32, spots.shape, 1)
    parts = [
        jnp.where(spots == (lane + (first * TILE + k * HALF)).astype(I16), one, zero)
        for k in range(2 * tiles)
    ]
    return jnp.concatenate(parts, axis=1)


def local_kernel(layer, edge_ref, cols, *refs):
    if layer:
        dom_ref, w1_ref, b1_ref, pre_ref, table = refs
        parts = ((0, 2 * TILE, dom_ref),)
    else:
        own_ref, peer_ref, w1_ref, b1_ref, pre_ref, table = refs
        core = lax.axis_index("edge")
        parts = ((core * TILE, TILE, own_ref), ((1 - core) * TILE, TILE, peer_ref))
    for k in (1, 2):
        for start, size, ref in parts:
            table[dyn((2 * k - 2) * TILE + start, size, TILE), :] = mm(
                ref[...], w1_ref[layer, k * TILE : (k + 1) * TILE, :]
            ).astype(BF16)
    bias = b1_ref[layer : layer + 1, :]

    def step(k, carry):
        at = dyn(k * LOCAL_ROWS, LOCAL_ROWS)
        acc = mm(edge_ref[at, :], w1_ref[layer, 0:TILE, :])
        acc = acc + mm(hits(cols[0, at, :], 0, 2), table[0 : 2 * TILE, :])
        acc = acc + mm(hits(cols[1, at, :], 0, 2), table[2 * TILE :, :])
        pre_ref[at, :] = acc + bias
        return carry

    lax.fori_loop(0, edge_ref.shape[0] // LOCAL_ROWS, step, 0)


def halo_tables(layer, own, peer, w1_ref, table):
    core = lax.axis_index("edge")
    w_s = w1_ref[layer, TILE : 2 * TILE, :]
    for axis, ref in ((core, own), (1 - core, peer)):
        table[dyn(axis * TILE, TILE), :] = mm(ref[...], w_s).astype(BF16)


def near_kernel(layer, peer, pre_ref, cols, w1_ref, rows_ref, out_ref):
    core = lax.axis_index("edge")
    tile = 3 - core if peer else 2 + core
    table = mm(rows_ref[...], w1_ref[layer, TILE : 2 * TILE, :]).astype(BF16)

    def step(k, carry):
        at = dyn(k * LOCAL_ROWS, LOCAL_ROWS)
        out_ref[at, :] = pre_ref[at, :] + mm(hits(cols[0, at, :], tile, 1), table)
        return carry

    lax.fori_loop(0, pre_ref.shape[0] // LOCAL_ROWS, step, 0)


def edge_kernel(
    layer, split, live_ref, pre_ref, cols, recv_ref, edge_ref, w1_ref, w2_ref, gain_ref, own, peer, out_ref, *refs
):
    if split:
        keep_ref, give_ref, table, raw, msgs, sums, block_ref, sems = refs
    else:
        part_ref, table, raw, msgs, sums = refs
        block_ref = out_ref
    halo_tables(layer, own, peer, w1_ref, table)
    gain = gain_ref[layer : layer + 1, :]
    live = live_ref[0, 0]
    count = edge_ref.shape[0] // ROWS

    def gather(at):
        acc = pre_ref[at, :] + mm(hits(cols[0, at, :], 4, 2), table[...])
        hidden = jnp.maximum(acc.astype(BF16), jnp.asarray(0, BF16))
        raw[at, :] = mm(hidden, w2_ref[layer])

    def norm(at, first):
        values = raw[at, :]
        center = values - jnp.mean(values, axis=-1, keepdims=True)
        spread = jnp.mean(center * center, axis=-1, keepdims=True)
        scale = lax.rsqrt(spread + eps_norm)
        row = lax.broadcasted_iota(jnp.int32, scale.shape, 0) + first
        scale = jnp.where(row < live, scale, 0.0)
        message = (center * scale * gain).astype(BF16)
        msgs[at, :] = message
        block_ref[at, :] = edge_ref[at, :] + message

    def segment(at, first):
        shape = (2 * TILE, ROWS)
        spot = lax.broadcasted_iota(jnp.int32, shape, 0).astype(I16)
        here = jnp.broadcast_to(recv_ref[:, at].astype(I16), shape)
        hot = jnp.where(here == spot, jnp.ones(shape, BF16), jnp.zeros(shape, BF16))
        part = mm(hot, msgs[at, :])
        sums[...] = part if first else sums[...] + part

    copies = []
    for k in range(count + 2):
        if k >= 2:
            segment(pl.ds((k - 2) * ROWS, ROWS), k == 2)
        if 1 <= k <= count:
            at = pl.ds((k - 1) * ROWS, ROWS)
            norm(at, (k - 1) * ROWS)
            if split:
                copies.append(
                    pltpu.make_async_copy(block_ref.at[at, :], out_ref.at[at, :], sems.at[k - 1])
                )
                copies[-1].start()
        if k < count:
            gather(pl.ds(k * ROWS, ROWS))
    if split:
        core = lax.axis_index("edge")
        keep_ref[...] = sums[dyn(core * TILE, TILE), :].astype(BF16)
        give_ref[...] = sums[dyn((1 - core) * TILE, TILE), :].astype(BF16)
        for copy in copies:
            copy.wait()
    else:
        part_ref[...] = sums[...].astype(BF16)


def updated(layer, nodes, first, second, w1_ref, b1_ref, w2_ref, gain_ref):
    total = (first.astype(F32) + second.astype(F32)).astype(BF16)
    pre = mm(nodes, w1_ref[layer, 0:TILE, :]) + mm(total, w1_ref[layer, TILE:, :])
    hidden = jnp.maximum(pre + b1_ref[layer : layer + 1, :], 0.0).astype(BF16)
    step = layer_norm(mm(hidden, w2_ref[layer]), gain_ref[layer : layer + 1, :])
    return (nodes.astype(F32) + step).astype(BF16)


def node_kernel(
    stride, layer, own_ref, peer_ref, first, second, list_own, list_peer, w1, b1, w2, gain, out, far, near
):
    core = lax.axis_index("edge")
    nodes = []
    for owner, ref in ((core, own_ref), (1 - core, peer_ref)):
        at = dyn(owner * TILE, TILE)
        nodes.append(updated(layer, ref[...], first[at, :], second[at, :], w1, b1, w2, gain))
        out[at, :] = nodes[-1]
    face_rows(stride, (list_own, list_peer), nodes, far, near)


def last_kernel(layer, nodes_ref, first, second, w1, b1, w2, gain, out):
    core = lax.axis_index("edge")
    nodes = nodes_ref[dyn(core * TILE, TILE), :]
    out[...] = updated(layer, nodes, first[...], second[...], w1, b1, w2, gain)


def met(count, stride, odd):
    pairs = []
    for dom in range(count):
        ahead = (dom // stride) % 2 == odd
        pairs.append((dom + (stride if ahead else -stride)) % count)
    return pairs


def swapped(value):
    return lax.ppermute(value, "edge", [(0, 1), (1, 0)])


def fast_shards(
    node_lat,
    edge_lat,
    senders,
    receivers,
    live_edges,
    send_rows,
    edge_w1,
    edge_b1,
    edge_w2,
    edge_gain,
    node_w1,
    node_b1,
    node_w2,
    node_gain,
):
    domains = lax.axis_size("dom")
    stride = domains // 4
    edges, width = edge_lat.shape
    nodes = node_lat.shape[0]
    near_d, far_d = met(domains, 1, 0), met(domains, 1, 1)
    near_s, far_s = met(domains, stride, 0), met(domains, stride, 1)

    def sent_by_core(value, partner_d, partner_s):
        pairs = [(2 * d, 2 * p) for d, p in enumerate(partner_d)]
        pairs += [(2 * d + 1, 2 * p + 1) for d, p in enumerate(partner_s)]
        return lax.ppermute(value, ("dom", "edge"), pairs)

    table = pltpu.VMEM((2 * TILE, width), BF16)
    messages = pltpu.VMEM((edges, width), BF16)
    pre_shape = shaped((edges, width), F32)
    rows_out = shaped((TILE, width), BF16)
    pass_flops = 2 * edges * TILE * width

    peer_nodes = swapped(node_lat)
    peer_lists = swapped(send_rows)
    node_lat, send_rows = call(
        functools.partial(load_kernel, 2),
        [shaped(a.shape, a.dtype) for a in (node_lat, send_rows)],
        in_hbm((node_lat, send_rows)),
        scratch=[pltpu.SemaphoreType.DMA((2,))],
        stay=(0, 1),
        name="load",
    )
    far_rows, near_rows = call(
        functools.partial(pick_kernel, stride),
        [rows_out, rows_out],
        (node_lat, peer_nodes, send_rows, peer_lists),
        name="pick",
    )
    loads = (edge_lat, edge_w1, edge_w2, node_w1, node_w2, edge_b1, edge_gain, node_b1, node_gain)
    far_rows, near_rows, *hbm = lax.optimization_barrier(
        (far_rows, near_rows, senders[None], receivers[None], *loads)
    )
    hbm = in_hbm(hbm)
    cols, recv_row, edge_rows, edge_w1, edge_w2, node_w1, node_w2, edge_b1, edge_gain, node_b1, node_gain = call(
        functools.partial(index_kernel, stride, edges, len(loads)),
        [shaped((2, edges, HALF), I16), shaped((1, edges), jnp.int32)]
        + [shaped(a.shape, a.dtype) for a in loads],
        hbm,
        scratch=[pltpu.VMEM((1, edges), jnp.int32), pltpu.SemaphoreType.DMA((len(hbm),))],
        stay=range(len(hbm)),
        name="index",
    )
    for layer in range(LAYERS):
        last = layer == LAYERS - 1
        node_args = (all_nodes,) if layer else (node_lat, peer_nodes)
        near = sent_by_core(near_rows, near_d, near_s)
        far = sent_by_core(far_rows, far_d, far_s)
        pre = call(
            functools.partial(local_kernel, layer),
            pre_shape,
            (edge_rows, cols, *node_args, edge_w1, edge_b1),
            scratch=[pltpu.VMEM((4 * TILE, width), BF16)],
            flops=5 * pass_flops,
            name="local",
        )
        pre, near, live_edges = lax.optimization_barrier((pre, near, live_edges))
        near_other = swapped(near)
        add = functools.partial(
            call, outs=pre_shape, flops=pass_flops, name="near"
        )
        pre = add(functools.partial(near_kernel, layer, False), args=(pre, cols, edge_w1, near))
        pre, far = lax.optimization_barrier((pre, far))
        far_other = swapped(far)
        pre = add(functools.partial(near_kernel, layer, True), args=(pre, cols, edge_w1, near_other))
        if last:
            outs = [shaped((nodes, width), BF16)] * 2
        else:
            outs = [shaped((2 * nodes, width), BF16)]
        edge_rows, *partial = call(
            functools.partial(edge_kernel, layer, last),
            [shaped((edges, width), BF16)] + outs,
            (live_edges, pre, cols, recv_row, edge_rows, edge_w1, edge_w2, edge_gain, far, far_other),
            scratch=[
                table,
                pltpu.VMEM((edges, width), F32),
                messages,
                pltpu.VMEM((2 * nodes, width), F32),
            ]
            + last * [messages, pltpu.SemaphoreType.DMA((edges // ROWS,))],
            smem=(0,),
            leave=last * (0,),
            flops=5 * pass_flops,
            name="far",
        )
        other = swapped(partial[-1])
        weights = (node_w1, node_b1, node_w2, node_gain)
        if last:
            out = call(
                functools.partial(last_kernel, layer),
                shaped((nodes, width), BF16),
                (all_nodes, partial[0], other, *weights),
                name="last",
            )
        else:
            all_nodes, far_rows, near_rows = call(
                functools.partial(node_kernel, stride, layer),
                [shaped((2 * nodes, width), BF16), rows_out, rows_out],
                (*node_args, partial[0], other, send_rows, peer_lists, *weights),
                name="nodes",
            )
    return out, edge_rows


def shards(*args):
    node_lat, edge_lat, _, _, _, send_rows = args[:6]
    domains = lax.axis_size("dom")
    fits = (
        lax.axis_size("edge") == 2
        and domains % 8 == 0
        and node_lat.shape == (TILE, TILE)
        and edge_lat.shape[0] % ROWS == 0
        and send_rows.shape[1:] == (4, HALF)
        and args[6].shape == (LAYERS, 3 * TILE, TILE)
    )
    return (fast_shards if fits else general_shards)(*args)


def general_shards(
    node_lat,
    edge_lat,
    senders,
    receivers,
    live_edges,
    send_rows,
    edge_w1,
    edge_b1,
    edge_w2,
    edge_gain,
    node_w1,
    node_b1,
    node_w2,
    node_gain,
):
    rank_count = lax.axis_size("edge")
    domains = lax.axis_size("dom")
    stride = domains // 4
    offsets = (1, -1, stride, -stride)
    node_count = node_lat.shape[0]
    face_count = send_rows.shape[1]
    latent = node_lat.shape[1]
    live_rows = lax.broadcasted_iota(jnp.int32, (edge_lat.shape[0],), 0) < live_edges[0, 0]
    lists_all = None
    lists_all = lax.all_gather(send_rows, "edge", axis=0, tiled=True)
    lists_all = lists_all + (jnp.arange(rank_count, dtype=jnp.int32) * node_count)[:, None, None]
    owned_rows = node_lat
    edge_rows = edge_lat
    for layer_index in range(LAYERS):
        received = []
        domain_rows = lax.all_gather(owned_rows, "edge", axis=0, tiled=True)
        face_rows = jnp.take(domain_rows, lists_all, axis=0)
        for face_index in range(face_count):
            received.append(passed_along(face_rows[:, face_index], "dom", offsets[face_index]))
        halo_all = jnp.stack(received, axis=1).reshape(-1, latent)
        node_table = jnp.concatenate([domain_rows, halo_all], axis=0)
        sender_rows = jnp.take(node_table, senders, axis=0)
        receiver_rows = jnp.take(domain_rows, receivers, axis=0)
        edge_rows, messages = edge_update(
            edge_rows,
            sender_rows,
            receiver_rows,
            edge_w1[layer_index],
            edge_b1[layer_index],
            edge_w2[layer_index],
            edge_gain[layer_index],
            live_rows,
        )
        summed = lax.psum_scatter(
            jax.ops.segment_sum(
                messages, receivers, num_segments=lax.axis_size("edge") * node_count
            ).astype(jnp.bfloat16),
            "edge",
            scatter_dimension=0,
            tiled=True,
        )
        owned_rows = node_update(
            owned_rows,
            summed,
            node_w1[layer_index],
            node_b1[layer_index],
            node_w2[layer_index],
            node_gain[layer_index],
        )
    return (owned_rows, edge_rows)


def solution(mesh):
    in_specs = (
        P(("dom", "edge"), None),
        P(("dom", "edge"), None),
        P(("dom", "edge")),
        P(("dom", "edge")),
        P("dom", "edge"),
        P(("dom", "edge"), None, None),
        P(),
        P(),
        P(),
        P(),
        P(),
        P(),
        P(),
        P(),
    )
    out_specs = (P(("dom", "edge"), None), P(("dom", "edge"), None))
    return jax.shard_map(shards, mesh=mesh, in_specs=in_specs, out_specs=out_specs, check_vma=False)
```

```python
import functools

import jax
import jax.numpy as jnp
from jax import lax
from jax.experimental import pallas as pl
from jax.experimental.pallas import tpu as pltpu
from jax.sharding import PartitionSpec as P

LAYERS = 2


eps_norm = 1e-05


def passed_along(value, axis, steps):
    count = lax.axis_size(axis)
    pairs = [(source, (source + steps) % count) for source in range(count)]
    return lax.ppermute(value, axis, pairs)


def layer_norm(values, norm_gain):
    center = values - jnp.mean(values, axis=-1, keepdims=True)
    spread = jnp.mean(center * center, axis=-1, keepdims=True)
    return center * lax.rsqrt(spread + eps_norm) * norm_gain


def edge_update(
    edge_rows, sender_rows, receiver_rows, weight_in, bias_in, weight_out, norm_gain, live_rows
):
    feature_width = edge_rows.shape[1]
    pre_act = jnp.dot(edge_rows, weight_in[:feature_width], preferred_element_type=jnp.float32)
    pre_act = pre_act + jnp.dot(
        sender_rows,
        weight_in[feature_width : 2 * feature_width],
        preferred_element_type=jnp.float32,
    )
    pre_act = pre_act + jnp.dot(
        receiver_rows, weight_in[2 * feature_width :], preferred_element_type=jnp.float32
    )
    hidden_rows = jax.nn.relu(pre_act + bias_in).astype(jnp.bfloat16)
    messages = layer_norm(
        jnp.dot(hidden_rows, weight_out, preferred_element_type=jnp.float32), norm_gain
    )
    messages = jnp.where(live_rows[:, None], messages, jnp.float32(0.0))
    return ((edge_rows.astype(jnp.float32) + messages).astype(jnp.bfloat16), messages)


def node_update(node_rows, aggregate, weight_in, bias_in, weight_out, norm_gain):
    feature_width = node_rows.shape[1]
    pre_act = jnp.dot(node_rows, weight_in[:feature_width], preferred_element_type=jnp.float32)
    pre_act = pre_act + jnp.dot(
        aggregate, weight_in[feature_width:], preferred_element_type=jnp.float32
    )
    hidden_rows = jax.nn.relu(pre_act + bias_in).astype(jnp.bfloat16)
    update = layer_norm(
        jnp.dot(hidden_rows, weight_out, preferred_element_type=jnp.float32), norm_gain
    )
    return (node_rows.astype(jnp.float32) + update).astype(jnp.bfloat16)


F32 = jnp.float32
BF16 = jnp.bfloat16
TILE = 256
HALF = 128
ROWS = 512
LOCAL_ROWS = 1024
I16 = jnp.int16
IN_VMEM = pl.BlockSpec(memory_space=pltpu.VMEM)
IN_SMEM = pl.BlockSpec(memory_space=pltpu.SMEM)
IN_HBM = pl.BlockSpec(memory_space=pltpu.HBM)


def shaped(shape, dtype):
    return jax.ShapeDtypeStruct(shape, dtype)


def call(kernel, outs, args, scratch=(), smem=(), stay=(), leave=(), flops=0, limit=24, name=None):
    nbytes = sum(a.size * a.dtype.itemsize for a in args)
    return pl.pallas_call(
        kernel,
        out_shape=outs,
        in_specs=[
            IN_SMEM if k in smem else IN_HBM if k in stay else IN_VMEM for k in range(len(args))
        ],
        out_specs=[IN_HBM if k in leave else IN_VMEM for k in range(len(outs))]
        if isinstance(outs, list)
        else IN_VMEM,
        scratch_shapes=scratch,
        compiler_params=pltpu.CompilerParams(vmem_limit_bytes=limit << 20),
        cost_estimate=pl.CostEstimate(flops=flops, transcendentals=0, bytes_accessed=nbytes),
        name=name,
    )(*args)


def place(stride):
    dom = lax.axis_index("dom")
    core = lax.axis_index("edge")
    return core, lax.rem(dom, 2), lax.rem(lax.div(dom, stride), 2)


def mm(a, b):
    return jnp.dot(a, b, preferred_element_type=F32)


def column(row):
    return jnp.transpose(jnp.broadcast_to(row, (HALF, HALF)))


def one_hot_rows(row, width):
    col = column(row)
    lane = lax.broadcasted_iota(jnp.int32, (HALF, HALF), 1)
    parts = [jnp.where(col == lane + k, 1.0, 0.0) for k in range(0, width, HALF)]
    return jnp.concatenate(parts, axis=1).astype(BF16)


def dyn(start, size, unit=None):
    return pl.ds(pl.multiple_of(start, unit or size), size)


def faces(stride):
    core, par_d, par_s = place(stride)
    par = jnp.where(core == 0, par_d, par_s)
    return 2 * core + 1 - par, 2 * core + par


def pick_kernel(stride, own_ref, peer_ref, list_own, list_peer, far, near):
    for face, ref in zip(faces(stride), (far, near)):
        for n, (lists, nodes) in enumerate(((list_own, own_ref), (list_peer, peer_ref))):
            hot = one_hot_rows(lists[0, pl.ds(face, 1), :], TILE)
            ref[n * HALF : (n + 1) * HALF, :] = mm(hot, nodes[...]).astype(BF16)


def load_kernel(count, *refs):
    hbm, vmem, sems = refs[:count], refs[count:-1], refs[-1]
    copies = [
        pltpu.make_async_copy(src, dst, sems.at[k]) for k, (src, dst) in enumerate(zip(hbm, vmem))
    ]
    for copy in copies:
        copy.start()
    for copy in copies:
        copy.wait()


def in_hbm(arrays):
    return [pltpu.with_memory_space_constraint(a, pltpu.HBM) for a in arrays]


def index_kernel(stride, edges, loads, send_ref, recv_ref, *refs):
    hbm, cols, vmem, sems = refs[:loads], refs[loads], refs[loads + 1 : -1], refs[-1]
    copies = [
        pltpu.make_async_copy(src, dst, sems.at[k]) for k, (src, dst) in enumerate(zip(hbm, vmem))
    ]
    for copy in copies:
        copy.start()
    _, par_d, par_s = place(stride)
    for k in range(edges // HALF):
        at = pl.ds(k * HALF, HALF)
        v = send_ref[:, at]
        j = v - 2 * TILE
        owner = lax.shift_right_arithmetic(j, 9)
        face = lax.shift_right_arithmetic(j, 7) & 3
        core = lax.shift_right_arithmetic(face, 1)
        par = jnp.where(core == 0, par_d, par_s)
        near = (face & 1) != par
        tile = jnp.where(near, 2, 4) + core
        at_tile = ((owner ^ core) & 1) * HALF + (j & (HALF - 1))
        spot = jnp.where(v < 2 * TILE, v, tile * TILE + at_tile)
        cols[0, at, :] = column(spot).astype(I16)
        cols[1, at, :] = column(recv_ref[:, at]).astype(I16)
    for copy in copies:
        copy.wait()


def hits(spots, first, tiles):
    one = jnp.ones(spots.shape, BF16)
    zero = jnp.zeros(spots.shape, BF16)
    lane = lax.broadcasted_iota(jnp.int32, spots.shape, 1)
    parts = [
        jnp.where(spots == (lane + (first * TILE + k * HALF)).astype(I16), one, zero)
        for k in range(2 * tiles)
    ]
    return jnp.concatenate(parts, axis=1)


def local_kernel(layer, edge_ref, cols, *refs):
    if layer:
        dom_ref, w1_ref, b1_ref, pre_ref, table = refs
        parts = ((0, 2 * TILE, dom_ref),)
    else:
        own_ref, peer_ref, w1_ref, b1_ref, pre_ref, table = refs
        core = lax.axis_index("edge")
        parts = ((core * TILE, TILE, own_ref), ((1 - core) * TILE, TILE, peer_ref))
    for k in (1, 2):
        for start, size, ref in parts:
            table[dyn((2 * k - 2) * TILE + start, size, TILE), :] = mm(
                ref[...], w1_ref[layer, k * TILE : (k + 1) * TILE, :]
            ).astype(BF16)
    bias = b1_ref[layer : layer + 1, :]

    def step(k, carry):
        at = dyn(k * LOCAL_ROWS, LOCAL_ROWS)
        acc = mm(edge_ref[at, :], w1_ref[layer, 0:TILE, :])
        acc = acc + mm(hits(cols[0, at, :], 0, 2), table[0 : 2 * TILE, :])
        acc = acc + mm(hits(cols[1, at, :], 0, 2), table[2 * TILE :, :])
        pre_ref[at, :] = acc + bias
        return carry

    lax.fori_loop(0, edge_ref.shape[0] // LOCAL_ROWS, step, 0)


def halo_tables(layer, own, peer, w1_ref, table):
    core = lax.axis_index("edge")
    w_s = w1_ref[layer, TILE : 2 * TILE, :]
    for axis, ref in ((core, own), (1 - core, peer)):
        table[dyn(axis * TILE, TILE), :] = mm(ref[...], w_s).astype(BF16)


def near_kernel(layer, peer, pre_ref, cols, w1_ref, rows_ref, out_ref):
    core = lax.axis_index("edge")
    tile = 3 - core if peer else 2 + core
    table = mm(rows_ref[...], w1_ref[layer, TILE : 2 * TILE, :]).astype(BF16)

    def step(k, carry):
        at = dyn(k * LOCAL_ROWS, LOCAL_ROWS)
        out_ref[at, :] = pre_ref[at, :] + mm(hits(cols[0, at, :], tile, 1), table)
        return carry

    lax.fori_loop(0, pre_ref.shape[0] // LOCAL_ROWS, step, 0)


def edge_kernel(
    layer, split, live_ref, pre_ref, cols, recv_ref, edge_ref, w1_ref, w2_ref, gain_ref, own, peer, out_ref, *refs
):
    if split:
        keep_ref, give_ref, table, raw, msgs, sums = refs
    else:
        part_ref, table, raw, msgs, sums = refs
    halo_tables(layer, own, peer, w1_ref, table)
    gain = gain_ref[layer : layer + 1, :]
    live = live_ref[0, 0]
    count = edge_ref.shape[0] // ROWS

    def gather(at):
        acc = pre_ref[at, :] + mm(hits(cols[0, at, :], 4, 2), table[...])
        hidden = jnp.maximum(acc.astype(BF16), jnp.asarray(0, BF16))
        raw[at, :] = mm(hidden, w2_ref[layer])

    def norm(at, first):
        values = raw[at, :]
        center = values - jnp.mean(values, axis=-1, keepdims=True)
        spread = jnp.mean(center * center, axis=-1, keepdims=True)
        scale = lax.rsqrt(spread + eps_norm)
        row = lax.broadcasted_iota(jnp.int32, scale.shape, 0) + first
        scale = jnp.where(row < live, scale, 0.0)
        message = (center * scale * gain).astype(BF16)
        msgs[at, :] = message
        out_ref[at, :] = edge_ref[at, :] + message

    def segment(at, first):
        shape = (2 * TILE, ROWS)
        spot = lax.broadcasted_iota(jnp.int32, shape, 0).astype(I16)
        here = jnp.broadcast_to(recv_ref[:, at].astype(I16), shape)
        hot = jnp.where(here == spot, jnp.ones(shape, BF16), jnp.zeros(shape, BF16))
        part = mm(hot, msgs[at, :])
        sums[...] = part if first else sums[...] + part

    for k in range(count + 2):
        if k >= 2:
            segment(pl.ds((k - 2) * ROWS, ROWS), k == 2)
        if 1 <= k <= count:
            norm(pl.ds((k - 1) * ROWS, ROWS), (k - 1) * ROWS)
        if k < count:
            gather(pl.ds(k * ROWS, ROWS))
    if split:
        core = lax.axis_index("edge")
        keep_ref[...] = sums[dyn(core * TILE, TILE), :].astype(BF16)
        give_ref[...] = sums[dyn((1 - core) * TILE, TILE), :].astype(BF16)
    else:
        part_ref[...] = sums[...].astype(BF16)


def updated(layer, nodes, first, second, w1_ref, b1_ref, w2_ref, gain_ref):
    total = (first.astype(F32) + second.astype(F32)).astype(BF16)
    pre = mm(nodes, w1_ref[layer, 0:TILE, :]) + mm(total, w1_ref[layer, TILE:, :])
    hidden = jnp.maximum(pre + b1_ref[layer : layer + 1, :], 0.0).astype(BF16)
    step = layer_norm(mm(hidden, w2_ref[layer]), gain_ref[layer : layer + 1, :])
    return (nodes.astype(F32) + step).astype(BF16)


def node_kernel(
    stride, layer, own_ref, peer_ref, first, second, list_own, list_peer, w1, b1, w2, gain, out, far, near, old
):
    core = lax.axis_index("edge")
    old[dyn(core * TILE, TILE), :] = own_ref[...]
    old[dyn((1 - core) * TILE, TILE), :] = peer_ref[...]
    nodes = updated(layer, old[...], first[...], second[...], w1, b1, w2, gain)
    out[...] = nodes
    for face, ref in zip(faces(stride), (far, near)):
        for n, (owner, lists) in enumerate(((core, list_own), (1 - core, list_peer))):
            hot = one_hot_rows(lists[0, pl.ds(face, 1), :] + owner * TILE, 2 * TILE)
            ref[n * HALF : (n + 1) * HALF, :] = mm(hot, nodes).astype(BF16)


def last_kernel(layer, nodes_ref, first, second, w1, b1, w2, gain, out):
    core = lax.axis_index("edge")
    nodes = nodes_ref[dyn(core * TILE, TILE), :]
    out[...] = updated(layer, nodes, first[...], second[...], w1, b1, w2, gain)


def met(count, stride, odd):
    pairs = []
    for dom in range(count):
        ahead = (dom // stride) % 2 == odd
        pairs.append((dom + (stride if ahead else -stride)) % count)
    return pairs


def swapped(value):
    return lax.ppermute(value, "edge", [(0, 1), (1, 0)])


def fast_shards(
    node_lat,
    edge_lat,
    senders,
    receivers,
    live_edges,
    send_rows,
    edge_w1,
    edge_b1,
    edge_w2,
    edge_gain,
    node_w1,
    node_b1,
    node_w2,
    node_gain,
):
    domains = lax.axis_size("dom")
    stride = domains // 4
    edges, width = edge_lat.shape
    nodes = node_lat.shape[0]
    near_d, far_d = met(domains, 1, 0), met(domains, 1, 1)
    near_s, far_s = met(domains, stride, 0), met(domains, stride, 1)

    def sent_by_core(value, partner_d, partner_s):
        pairs = [(2 * d, 2 * p) for d, p in enumerate(partner_d)]
        pairs += [(2 * d + 1, 2 * p + 1) for d, p in enumerate(partner_s)]
        return lax.ppermute(value, ("dom", "edge"), pairs)

    table = pltpu.VMEM((2 * TILE, width), BF16)
    messages = pltpu.VMEM((edges, width), BF16)
    pre_shape = shaped((edges, width), F32)
    rows_out = shaped((TILE, width), BF16)
    pass_flops = 2 * edges * TILE * width

    peer_nodes = swapped(node_lat)
    peer_lists = swapped(send_rows)
    send_at, recv_at = senders[None], receivers[None]
    first = (node_lat, send_rows, send_at, recv_at)
    node_lat, send_rows, send_at, recv_at = call(
        functools.partial(load_kernel, len(first)),
        [shaped(a.shape, a.dtype) for a in first],
        in_hbm(first),
        scratch=[pltpu.SemaphoreType.DMA((len(first),))],
        stay=range(len(first)),
        name="load",
    )
    far_rows, near_rows = call(
        functools.partial(pick_kernel, stride),
        [rows_out, rows_out],
        (node_lat, peer_nodes, send_rows, peer_lists),
        name="pick",
    )
    loads = (edge_lat, edge_w1, edge_w2, node_w1, node_w2, edge_b1, edge_gain, node_b1, node_gain)
    far_rows, near_rows, send_at, recv_at, *hbm = lax.optimization_barrier(
        (far_rows, near_rows, send_at, recv_at, *loads)
    )
    hbm = in_hbm(hbm)
    cols, edge_rows, edge_w1, edge_w2, node_w1, node_w2, edge_b1, edge_gain, node_b1, node_gain = call(
        functools.partial(index_kernel, stride, edges, len(loads)),
        [shaped((2, edges, HALF), I16)] + [shaped(a.shape, a.dtype) for a in loads],
        (send_at, recv_at, *hbm),
        scratch=[pltpu.SemaphoreType.DMA((len(hbm),))],
        stay=range(2, len(hbm) + 2),
        name="index",
    )
    for layer in range(LAYERS):
        last = layer == LAYERS - 1
        node_args = (all_nodes,) if layer else (node_lat, peer_nodes)
        near = sent_by_core(near_rows, near_d, near_s)
        far = sent_by_core(far_rows, far_d, far_s)
        pre = call(
            functools.partial(local_kernel, layer),
            pre_shape,
            (edge_rows, cols, *node_args, edge_w1, edge_b1),
            scratch=[pltpu.VMEM((4 * TILE, width), BF16)],
            flops=5 * pass_flops,
            name="local",
        )
        pre, near, live_edges = lax.optimization_barrier((pre, near, live_edges))
        near_other = swapped(near)
        add = functools.partial(
            call, outs=pre_shape, flops=pass_flops, name="near"
        )
        pre = add(functools.partial(near_kernel, layer, False), args=(pre, cols, edge_w1, near))
        pre, far = lax.optimization_barrier((pre, far))
        far_other = swapped(far)
        pre = add(functools.partial(near_kernel, layer, True), args=(pre, cols, edge_w1, near_other))
        if last:
            outs = [shaped((nodes, width), BF16)] * 2
        else:
            outs = [shaped((2 * nodes, width), BF16)]
        edge_rows, *partial = call(
            functools.partial(edge_kernel, layer, last),
            [shaped((edges, width), BF16)] + outs,
            (live_edges, pre, cols, recv_at, edge_rows, edge_w1, edge_w2, edge_gain, far, far_other),
            scratch=[
                table,
                pltpu.VMEM((edges, width), F32),
                messages,
                pltpu.VMEM((2 * nodes, width), F32),
            ],
            smem=(0,),
            flops=5 * pass_flops,
            name="far",
        )
        other = swapped(partial[-1])
        weights = (node_w1, node_b1, node_w2, node_gain)
        if last:
            (edge_out,) = call(
                functools.partial(load_kernel, 1),
                [shaped((edges, width), BF16)],
                (edge_rows,),
                scratch=[pltpu.SemaphoreType.DMA((1,))],
                leave=(0,),
                name="store",
            )
            out = call(
                functools.partial(last_kernel, layer),
                shaped((nodes, width), BF16),
                (all_nodes, partial[0], other, *weights),
                name="last",
            )
        else:
            all_nodes, far_rows, near_rows = call(
                functools.partial(node_kernel, stride, layer),
                [shaped((2 * nodes, width), BF16), rows_out, rows_out],
                (*node_args, partial[0], other, send_rows, peer_lists, *weights),
                scratch=[table],
                name="nodes",
            )
    return out, edge_out


def shards(*args):
    node_lat, edge_lat, _, _, _, send_rows = args[:6]
    domains = lax.axis_size("dom")
    fits = (
        lax.axis_size("edge") == 2
        and domains % 8 == 0
        and node_lat.shape == (TILE, TILE)
        and edge_lat.shape[0] % ROWS == 0
        and send_rows.shape[1:] == (4, HALF)
        and args[6].shape == (LAYERS, 3 * TILE, TILE)
    )
    return (fast_shards if fits else general_shards)(*args)


def general_shards(
    node_lat,
    edge_lat,
    senders,
    receivers,
    live_edges,
    send_rows,
    edge_w1,
    edge_b1,
    edge_w2,
    edge_gain,
    node_w1,
    node_b1,
    node_w2,
    node_gain,
):
    rank_count = lax.axis_size("edge")
    domains = lax.axis_size("dom")
    stride = domains // 4
    offsets = (1, -1, stride, -stride)
    node_count = node_lat.shape[0]
    face_count = send_rows.shape[1]
    latent = node_lat.shape[1]
    live_rows = lax.broadcasted_iota(jnp.int32, (edge_lat.shape[0],), 0) < live_edges[0, 0]
    lists_all = None
    lists_all = lax.all_gather(send_rows, "edge", axis=0, tiled=True)
    lists_all = lists_all + (jnp.arange(rank_count, dtype=jnp.int32) * node_count)[:, None, None]
    owned_rows = node_lat
    edge_rows = edge_lat
    for layer_index in range(LAYERS):
        received = []
        domain_rows = lax.all_gather(owned_rows, "edge", axis=0, tiled=True)
        face_rows = jnp.take(domain_rows, lists_all, axis=0)
        for face_index in range(face_count):
            received.append(passed_along(face_rows[:, face_index], "dom", offsets[face_index]))
        halo_all = jnp.stack(received, axis=1).reshape(-1, latent)
        node_table = jnp.concatenate([domain_rows, halo_all], axis=0)
        sender_rows = jnp.take(node_table, senders, axis=0)
        receiver_rows = jnp.take(domain_rows, receivers, axis=0)
        edge_rows, messages = edge_update(
            edge_rows,
            sender_rows,
            receiver_rows,
            edge_w1[layer_index],
            edge_b1[layer_index],
            edge_w2[layer_index],
            edge_gain[layer_index],
            live_rows,
        )
        summed = lax.psum_scatter(
            jax.ops.segment_sum(
                messages, receivers, num_segments=lax.axis_size("edge") * node_count
            ).astype(jnp.bfloat16),
            "edge",
            scatter_dimension=0,
            tiled=True,
        )
        owned_rows = node_update(
            owned_rows,
            summed,
            node_w1[layer_index],
            node_b1[layer_index],
            node_w2[layer_index],
            node_gain[layer_index],
        )
    return (owned_rows, edge_rows)


def solution(mesh):
    in_specs = (
        P(("dom", "edge"), None),
        P(("dom", "edge"), None),
        P(("dom", "edge")),
        P(("dom", "edge")),
        P("dom", "edge"),
        P(("dom", "edge"), None, None),
        P(),
        P(),
        P(),
        P(),
        P(),
        P(),
        P(),
        P(),
    )
    out_specs = (P(("dom", "edge"), None), P(("dom", "edge"), None))
    return jax.shard_map(shards, mesh=mesh, in_specs=in_specs, out_specs=out_specs, check_vma=False)
```

```python
import functools

import jax
import jax.numpy as jnp
from jax import lax
from jax.experimental import pallas as pl
from jax.experimental.pallas import tpu as pltpu
from jax.sharding import PartitionSpec as P

LAYERS = 2


eps_norm = 1e-05


def passed_along(value, axis, steps):
    count = lax.axis_size(axis)
    pairs = [(source, (source + steps) % count) for source in range(count)]
    return lax.ppermute(value, axis, pairs)


def layer_norm(values, norm_gain):
    center = values - jnp.mean(values, axis=-1, keepdims=True)
    spread = jnp.mean(center * center, axis=-1, keepdims=True)
    return center * lax.rsqrt(spread + eps_norm) * norm_gain


def edge_update(
    edge_rows, sender_rows, receiver_rows, weight_in, bias_in, weight_out, norm_gain, live_rows
):
    feature_width = edge_rows.shape[1]
    pre_act = jnp.dot(edge_rows, weight_in[:feature_width], preferred_element_type=jnp.float32)
    pre_act = pre_act + jnp.dot(
        sender_rows,
        weight_in[feature_width : 2 * feature_width],
        preferred_element_type=jnp.float32,
    )
    pre_act = pre_act + jnp.dot(
        receiver_rows, weight_in[2 * feature_width :], preferred_element_type=jnp.float32
    )
    hidden_rows = jax.nn.relu(pre_act + bias_in).astype(jnp.bfloat16)
    messages = layer_norm(
        jnp.dot(hidden_rows, weight_out, preferred_element_type=jnp.float32), norm_gain
    )
    messages = jnp.where(live_rows[:, None], messages, jnp.float32(0.0))
    return ((edge_rows.astype(jnp.float32) + messages).astype(jnp.bfloat16), messages)


def node_update(node_rows, aggregate, weight_in, bias_in, weight_out, norm_gain):
    feature_width = node_rows.shape[1]
    pre_act = jnp.dot(node_rows, weight_in[:feature_width], preferred_element_type=jnp.float32)
    pre_act = pre_act + jnp.dot(
        aggregate, weight_in[feature_width:], preferred_element_type=jnp.float32
    )
    hidden_rows = jax.nn.relu(pre_act + bias_in).astype(jnp.bfloat16)
    update = layer_norm(
        jnp.dot(hidden_rows, weight_out, preferred_element_type=jnp.float32), norm_gain
    )
    return (node_rows.astype(jnp.float32) + update).astype(jnp.bfloat16)


F32 = jnp.float32
BF16 = jnp.bfloat16
TILE = 256
HALF = 128
ROWS = 512
LOCAL_ROWS = 1024
I16 = jnp.int16
IN_VMEM = pl.BlockSpec(memory_space=pltpu.VMEM)
IN_SMEM = pl.BlockSpec(memory_space=pltpu.SMEM)
IN_HBM = pl.BlockSpec(memory_space=pltpu.HBM)


def shaped(shape, dtype):
    return jax.ShapeDtypeStruct(shape, dtype)


def call(kernel, outs, args, scratch=(), smem=(), stay=(), leave=(), flops=0, limit=24, name=None):
    nbytes = sum(a.size * a.dtype.itemsize for a in args)
    return pl.pallas_call(
        kernel,
        out_shape=outs,
        in_specs=[
            IN_SMEM if k in smem else IN_HBM if k in stay else IN_VMEM for k in range(len(args))
        ],
        out_specs=[IN_HBM if k in leave else IN_VMEM for k in range(len(outs))]
        if isinstance(outs, list)
        else IN_VMEM,
        scratch_shapes=scratch,
        compiler_params=pltpu.CompilerParams(vmem_limit_bytes=limit << 20),
        cost_estimate=pl.CostEstimate(flops=flops, transcendentals=0, bytes_accessed=nbytes),
        name=name,
    )(*args)


def place(stride):
    dom = lax.axis_index("dom")
    core = lax.axis_index("edge")
    return core, lax.rem(dom, 2), lax.rem(lax.div(dom, stride), 2)


def mm(a, b):
    return jnp.dot(a, b, preferred_element_type=F32)


def column(row):
    return jnp.transpose(jnp.broadcast_to(row, (HALF, HALF)))


def one_hot_rows(row, width):
    col = column(row)
    lane = lax.broadcasted_iota(jnp.int32, (HALF, HALF), 1)
    parts = [jnp.where(col == lane + k, 1.0, 0.0) for k in range(0, width, HALF)]
    return jnp.concatenate(parts, axis=1).astype(BF16)


def dyn(start, size, unit=None):
    return pl.ds(pl.multiple_of(start, unit or size), size)


def faces(stride):
    core, par_d, par_s = place(stride)
    par = jnp.where(core == 0, par_d, par_s)
    return 2 * core + 1 - par, 2 * core + par


def pick_kernel(stride, own_ref, peer_ref, list_own, list_peer, far, near):
    for face, ref in zip(faces(stride), (far, near)):
        for n, (lists, nodes) in enumerate(((list_own, own_ref), (list_peer, peer_ref))):
            hot = one_hot_rows(lists[0, pl.ds(face, 1), :], TILE)
            ref[n * HALF : (n + 1) * HALF, :] = mm(hot, nodes[...]).astype(BF16)


def load_kernel(count, *refs):
    hbm, vmem, sems = refs[:count], refs[count:-1], refs[-1]
    copies = [
        pltpu.make_async_copy(src, dst, sems.at[k]) for k, (src, dst) in enumerate(zip(hbm, vmem))
    ]
    for copy in copies:
        copy.start()
    for copy in copies:
        copy.wait()


def in_hbm(arrays):
    return [pltpu.with_memory_space_constraint(a, pltpu.HBM) for a in arrays]


def columns(stride, send_ref, recv_ref, cols, at):
    _, par_d, par_s = place(stride)
    v = send_ref[:, at]
    j = v - 2 * TILE
    owner = lax.shift_right_arithmetic(j, 9)
    face = lax.shift_right_arithmetic(j, 7) & 3
    core = lax.shift_right_arithmetic(face, 1)
    par = jnp.where(core == 0, par_d, par_s)
    near = (face & 1) != par
    tile = jnp.where(near, 2, 4) + core
    at_tile = ((owner ^ core) & 1) * HALF + (j & (HALF - 1))
    spot = jnp.where(v < 2 * TILE, v, tile * TILE + at_tile)
    cols[0, at, :] = column(spot).astype(I16)
    cols[1, at, :] = column(recv_ref[:, at]).astype(I16)


def hits(spots, first, tiles):
    one = jnp.ones(spots.shape, BF16)
    zero = jnp.zeros(spots.shape, BF16)
    lane = lax.broadcasted_iota(jnp.int32, spots.shape, 1)
    parts = [
        jnp.where(spots == (lane + (first * TILE + k * HALF)).astype(I16), one, zero)
        for k in range(2 * tiles)
    ]
    return jnp.concatenate(parts, axis=1)


def project(layer, parts, w1_ref, table):
    for k in (1, 2):
        for start, size, ref in parts:
            table[dyn((2 * k - 2) * TILE + start, size, TILE), :] = mm(
                ref[...], w1_ref[layer, k * TILE : (k + 1) * TILE, :]
            ).astype(BF16)


def local_block(layer, at, edge_ref, cols, w1_ref, b1_ref, table, pre_ref):
    acc = mm(edge_ref[at, :], w1_ref[layer, 0:TILE, :])
    acc = acc + mm(hits(cols[0, at, :], 0, 2), table[0 : 2 * TILE, :])
    acc = acc + mm(hits(cols[1, at, :], 0, 2), table[2 * TILE :, :])
    pre_ref[at, :] = acc + b1_ref[layer : layer + 1, :]


def first_kernel(stride, loads, send_ref, recv_ref, own_ref, peer_ref, w1_ref, b1_ref, *refs):
    hbm, (pre_ref, cols), refs = refs[:loads], refs[loads : loads + 2], refs[loads + 2 :]
    vmem, (table, sems) = refs[:loads], refs[loads:]
    edge_hbm, edge_ref = hbm[0], vmem[0]
    edges = edge_ref.shape[0]
    blocks = [pl.ds(start, LOCAL_ROWS) for start in range(0, edges, LOCAL_ROWS)]
    copies = [(edge_hbm.at[at, :], edge_ref.at[at, :]) for at in blocks]
    copies += zip(hbm[1:], vmem[1:])
    copies = [pltpu.make_async_copy(*ends, sems.at[k]) for k, ends in enumerate(copies)]
    for copy in copies:
        copy.start()
    core = lax.axis_index("edge")
    parts = ((core * TILE, TILE, own_ref), ((1 - core) * TILE, TILE, peer_ref))

    def make(k):
        for start in range(k * LOCAL_ROWS, (k + 1) * LOCAL_ROWS, HALF):
            columns(stride, send_ref, recv_ref, cols, pl.ds(start, HALF))

    make(0)
    project(0, parts, w1_ref, table)
    for k, at in enumerate(blocks):
        copies[k].wait()
        if k + 1 < len(blocks):
            make(k + 1)
        local_block(0, at, edge_ref, cols, w1_ref, b1_ref, table, pre_ref)
    for copy in copies[len(blocks) :]:
        copy.wait()


def local_kernel(layer, edge_ref, cols, dom_ref, w1_ref, b1_ref, pre_ref, table):
    project(layer, ((0, 2 * TILE, dom_ref),), w1_ref, table)

    def step(k, carry):
        at = dyn(k * LOCAL_ROWS, LOCAL_ROWS)
        local_block(layer, at, edge_ref, cols, w1_ref, b1_ref, table, pre_ref)
        return carry

    lax.fori_loop(0, edge_ref.shape[0] // LOCAL_ROWS, step, 0)


def halo_tables(layer, own, peer, w1_ref, table):
    core = lax.axis_index("edge")
    w_s = w1_ref[layer, TILE : 2 * TILE, :]
    for axis, ref in ((core, own), (1 - core, peer)):
        table[dyn(axis * TILE, TILE), :] = mm(ref[...], w_s).astype(BF16)


def near_kernel(layer, peer, pre_ref, cols, w1_ref, rows_ref, out_ref):
    core = lax.axis_index("edge")
    tile = 3 - core if peer else 2 + core
    table = mm(rows_ref[...], w1_ref[layer, TILE : 2 * TILE, :]).astype(BF16)

    half = pre_ref.shape[0] // 2

    def step(k, carry):
        at = dyn(k * half, half)
        out_ref[at, :] = pre_ref[at, :] + mm(hits(cols[0, at, :], tile, 1), table)
        return carry

    lax.fori_loop(0, 2, step, 0)


def edge_kernel(
    layer, split, live_ref, pre_ref, cols, recv_ref, edge_ref, w1_ref, w2_ref, gain_ref, own, peer, out_ref, *refs
):
    if split:
        keep_ref, give_ref, table, raw, msgs, sums = refs
    else:
        part_ref, table, raw, msgs, sums = refs
    halo_tables(layer, own, peer, w1_ref, table)
    gain = gain_ref[layer : layer + 1, :]
    live = live_ref[0, 0]
    count = edge_ref.shape[0] // ROWS

    def gather(at):
        acc = pre_ref[at, :] + mm(hits(cols[0, at, :], 4, 2), table[...])
        hidden = jnp.maximum(acc.astype(BF16), jnp.asarray(0, BF16))
        raw[at, :] = mm(hidden, w2_ref[layer])

    def norm(at, first):
        values = raw[at, :]
        center = values - jnp.mean(values, axis=-1, keepdims=True)
        spread = jnp.mean(center * center, axis=-1, keepdims=True)
        scale = lax.rsqrt(spread + eps_norm)
        row = lax.broadcasted_iota(jnp.int32, scale.shape, 0) + first
        scale = jnp.where(row < live, scale, 0.0)
        message = (center * scale * gain).astype(BF16)
        msgs[at, :] = message
        out_ref[at, :] = edge_ref[at, :] + message

    def segment(at, first):
        shape = (2 * TILE, ROWS)
        spot = lax.broadcasted_iota(jnp.int32, shape, 0).astype(I16)
        here = jnp.broadcast_to(recv_ref[:, at].astype(I16), shape)
        hot = jnp.where(here == spot, jnp.ones(shape, BF16), jnp.zeros(shape, BF16))
        part = mm(hot, msgs[at, :])
        sums[...] = part if first else sums[...] + part

    for k in range(count + 2):
        if k >= 2:
            segment(pl.ds((k - 2) * ROWS, ROWS), k == 2)
        if 1 <= k <= count:
            norm(pl.ds((k - 1) * ROWS, ROWS), (k - 1) * ROWS)
        if k < count:
            gather(pl.ds(k * ROWS, ROWS))
    if split:
        core = lax.axis_index("edge")
        keep_ref[...] = sums[dyn(core * TILE, TILE), :].astype(BF16)
        give_ref[...] = sums[dyn((1 - core) * TILE, TILE), :].astype(BF16)
    else:
        part_ref[...] = sums[...].astype(BF16)


def updated(layer, nodes, first, second, w1_ref, b1_ref, w2_ref, gain_ref):
    total = (first.astype(F32) + second.astype(F32)).astype(BF16)
    pre = mm(nodes, w1_ref[layer, 0:TILE, :]) + mm(total, w1_ref[layer, TILE:, :])
    hidden = jnp.maximum(pre + b1_ref[layer : layer + 1, :], 0.0).astype(BF16)
    step = layer_norm(mm(hidden, w2_ref[layer]), gain_ref[layer : layer + 1, :])
    return (nodes.astype(F32) + step).astype(BF16)


def node_kernel(
    stride, layer, own_ref, peer_ref, first, second, list_own, list_peer, w1, b1, w2, gain, out, far, near, old
):
    core = lax.axis_index("edge")
    old[dyn(core * TILE, TILE), :] = own_ref[...]
    old[dyn((1 - core) * TILE, TILE), :] = peer_ref[...]
    nodes = updated(layer, old[...], first[...], second[...], w1, b1, w2, gain)
    out[...] = nodes
    for face, ref in zip(faces(stride), (far, near)):
        for n, (owner, lists) in enumerate(((core, list_own), (1 - core, list_peer))):
            hot = one_hot_rows(lists[0, pl.ds(face, 1), :] + owner * TILE, 2 * TILE)
            ref[n * HALF : (n + 1) * HALF, :] = mm(hot, nodes).astype(BF16)


def last_kernel(layer, nodes_ref, first, second, w1, b1, w2, gain, out):
    core = lax.axis_index("edge")
    nodes = nodes_ref[dyn(core * TILE, TILE), :]
    out[...] = updated(layer, nodes, first[...], second[...], w1, b1, w2, gain)


def met(count, stride, odd):
    pairs = []
    for dom in range(count):
        ahead = (dom // stride) % 2 == odd
        pairs.append((dom + (stride if ahead else -stride)) % count)
    return pairs


def swapped(value):
    return lax.ppermute(value, "edge", [(0, 1), (1, 0)])


def fast_shards(
    node_lat,
    edge_lat,
    senders,
    receivers,
    live_edges,
    send_rows,
    edge_w1,
    edge_b1,
    edge_w2,
    edge_gain,
    node_w1,
    node_b1,
    node_w2,
    node_gain,
):
    domains = lax.axis_size("dom")
    stride = domains // 4
    edges, width = edge_lat.shape
    nodes = node_lat.shape[0]
    near_d, far_d = met(domains, 1, 0), met(domains, 1, 1)
    near_s, far_s = met(domains, stride, 0), met(domains, stride, 1)

    def sent_by_core(value, partner_d, partner_s):
        pairs = [(2 * d, 2 * p) for d, p in enumerate(partner_d)]
        pairs += [(2 * d + 1, 2 * p + 1) for d, p in enumerate(partner_s)]
        return lax.ppermute(value, ("dom", "edge"), pairs)

    table = pltpu.VMEM((2 * TILE, width), BF16)
    messages = pltpu.VMEM((edges, width), BF16)
    pre_shape = shaped((edges, width), F32)
    rows_out = shaped((TILE, width), BF16)
    pass_flops = 2 * edges * TILE * width

    peer_nodes = swapped(node_lat)
    peer_lists = swapped(send_rows)
    send_at, recv_at = senders[None], receivers[None]
    first = (node_lat, send_rows, send_at, recv_at, edge_w1, edge_b1)
    node_lat, send_rows, send_at, recv_at, edge_w1, edge_b1 = call(
        functools.partial(load_kernel, len(first)),
        [shaped(a.shape, a.dtype) for a in first],
        in_hbm(first),
        scratch=[pltpu.SemaphoreType.DMA((len(first),))],
        stay=range(len(first)),
        name="load",
    )
    far_rows, near_rows = call(
        functools.partial(pick_kernel, stride),
        [rows_out, rows_out],
        (node_lat, peer_nodes, send_rows, peer_lists),
        name="pick",
    )
    for layer in range(LAYERS):
        last = layer == LAYERS - 1
        near = sent_by_core(near_rows, near_d, near_s)
        far = sent_by_core(far_rows, far_d, far_s)
        if layer == 0:
            loads = (edge_lat, edge_w2, node_w1, node_w2, edge_gain, node_b1, node_gain)
            pre, cols, edge_rows, edge_w2, node_w1, node_w2, edge_gain, node_b1, node_gain = call(
                functools.partial(first_kernel, stride, len(loads)),
                [pre_shape, shaped((2, edges, HALF), I16)]
                + [shaped(a.shape, a.dtype) for a in loads],
                (send_at, recv_at, node_lat, peer_nodes, edge_w1, edge_b1, *in_hbm(loads)),
                scratch=[
                    pltpu.VMEM((4 * TILE, width), BF16),
                    pltpu.SemaphoreType.DMA((edges // LOCAL_ROWS + len(loads) - 1,)),
                ],
                stay=range(6, 6 + len(loads)),
                flops=5 * pass_flops,
                name="first",
            )
        else:
            pre = call(
                functools.partial(local_kernel, layer),
                pre_shape,
                (edge_rows, cols, all_nodes, edge_w1, edge_b1),
                scratch=[pltpu.VMEM((4 * TILE, width), BF16)],
                flops=5 * pass_flops,
                name="local",
            )
        pre, near, live_edges = lax.optimization_barrier((pre, near, live_edges))
        near_other = swapped(near)
        add = functools.partial(
            call, outs=pre_shape, flops=pass_flops, name="near"
        )
        pre = add(functools.partial(near_kernel, layer, False), args=(pre, cols, edge_w1, near))
        pre, far = lax.optimization_barrier((pre, far))
        far_other = swapped(far)
        pre = add(functools.partial(near_kernel, layer, True), args=(pre, cols, edge_w1, near_other))
        if last:
            outs = [shaped((nodes, width), BF16)] * 2
        else:
            outs = [shaped((2 * nodes, width), BF16)]
        edge_rows, *partial = call(
            functools.partial(edge_kernel, layer, last),
            [shaped((edges, width), BF16)] + outs,
            (live_edges, pre, cols, recv_at, edge_rows, edge_w1, edge_w2, edge_gain, far, far_other),
            scratch=[
                table,
                pltpu.VMEM((edges, width), F32),
                messages,
                pltpu.VMEM((2 * nodes, width), F32),
            ],
            smem=(0,),
            flops=5 * pass_flops,
            name="far",
        )
        other = swapped(partial[-1])
        weights = (node_w1, node_b1, node_w2, node_gain)
        if last:
            (edge_out,) = call(
                functools.partial(load_kernel, 1),
                [shaped((edges, width), BF16)],
                (edge_rows,),
                scratch=[pltpu.SemaphoreType.DMA((1,))],
                leave=(0,),
                name="store",
            )
            out = call(
                functools.partial(last_kernel, layer),
                shaped((nodes, width), BF16),
                (all_nodes, partial[0], other, *weights),
                name="last",
            )
        else:
            all_nodes, far_rows, near_rows = call(
                functools.partial(node_kernel, stride, layer),
                [shaped((2 * nodes, width), BF16), rows_out, rows_out],
                (node_lat, peer_nodes, partial[0], other, send_rows, peer_lists, *weights),
                scratch=[table],
                name="nodes",
            )
    return out, edge_out


def shards(*args):
    node_lat, edge_lat, _, _, _, send_rows = args[:6]
    domains = lax.axis_size("dom")
    fits = (
        lax.axis_size("edge") == 2
        and domains % 8 == 0
        and node_lat.shape == (TILE, TILE)
        and edge_lat.shape[0] % LOCAL_ROWS == 0
        and send_rows.shape[1:] == (4, HALF)
        and args[6].shape == (LAYERS, 3 * TILE, TILE)
    )
    return (fast_shards if fits else general_shards)(*args)


def general_shards(
    node_lat,
    edge_lat,
    senders,
    receivers,
    live_edges,
    send_rows,
    edge_w1,
    edge_b1,
    edge_w2,
    edge_gain,
    node_w1,
    node_b1,
    node_w2,
    node_gain,
):
    rank_count = lax.axis_size("edge")
    domains = lax.axis_size("dom")
    stride = domains // 4
    offsets = (1, -1, stride, -stride)
    node_count = node_lat.shape[0]
    face_count = send_rows.shape[1]
    latent = node_lat.shape[1]
    live_rows = lax.broadcasted_iota(jnp.int32, (edge_lat.shape[0],), 0) < live_edges[0, 0]
    lists_all = None
    lists_all = lax.all_gather(send_rows, "edge", axis=0, tiled=True)
    lists_all = lists_all + (jnp.arange(rank_count, dtype=jnp.int32) * node_count)[:, None, None]
    owned_rows = node_lat
    edge_rows = edge_lat
    for layer_index in range(LAYERS):
        received = []
        domain_rows = lax.all_gather(owned_rows, "edge", axis=0, tiled=True)
        face_rows = jnp.take(domain_rows, lists_all, axis=0)
        for face_index in range(face_count):
            received.append(passed_along(face_rows[:, face_index], "dom", offsets[face_index]))
        halo_all = jnp.stack(received, axis=1).reshape(-1, latent)
        node_table = jnp.concatenate([domain_rows, halo_all], axis=0)
        sender_rows = jnp.take(node_table, senders, axis=0)
        receiver_rows = jnp.take(domain_rows, receivers, axis=0)
        edge_rows, messages = edge_update(
            edge_rows,
            sender_rows,
            receiver_rows,
            edge_w1[layer_index],
            edge_b1[layer_index],
            edge_w2[layer_index],
            edge_gain[layer_index],
            live_rows,
        )
        summed = lax.psum_scatter(
            jax.ops.segment_sum(
                messages, receivers, num_segments=lax.axis_size("edge") * node_count
            ).astype(jnp.bfloat16),
            "edge",
            scatter_dimension=0,
            tiled=True,
        )
        owned_rows = node_update(
            owned_rows,
            summed,
            node_w1[layer_index],
            node_b1[layer_index],
            node_w2[layer_index],
            node_gain[layer_index],
        )
    return (owned_rows, edge_rows)


def solution(mesh):
    in_specs = (
        P(("dom", "edge"), None),
        P(("dom", "edge"), None),
        P(("dom", "edge")),
        P(("dom", "edge")),
        P("dom", "edge"),
        P(("dom", "edge"), None, None),
        P(),
        P(),
        P(),
        P(),
        P(),
        P(),
        P(),
        P(),
    )
    out_specs = (P(("dom", "edge"), None), P(("dom", "edge"), None))
    return jax.shard_map(shards, mesh=mesh, in_specs=in_specs, out_specs=out_specs, check_vma=False)
```

```python
import functools

import jax
import jax.numpy as jnp
from jax import lax
from jax.experimental import pallas as pl
from jax.experimental.pallas import tpu as pltpu
from jax.sharding import PartitionSpec as P

LAYERS = 2


eps_norm = 1e-05


def passed_along(value, axis, steps):
    count = lax.axis_size(axis)
    pairs = [(source, (source + steps) % count) for source in range(count)]
    return lax.ppermute(value, axis, pairs)


def layer_norm(values, norm_gain):
    center = values - jnp.mean(values, axis=-1, keepdims=True)
    spread = jnp.mean(center * center, axis=-1, keepdims=True)
    return center * lax.rsqrt(spread + eps_norm) * norm_gain


def edge_update(
    edge_rows, sender_rows, receiver_rows, weight_in, bias_in, weight_out, norm_gain, live_rows
):
    feature_width = edge_rows.shape[1]
    pre_act = jnp.dot(edge_rows, weight_in[:feature_width], preferred_element_type=jnp.float32)
    pre_act = pre_act + jnp.dot(
        sender_rows,
        weight_in[feature_width : 2 * feature_width],
        preferred_element_type=jnp.float32,
    )
    pre_act = pre_act + jnp.dot(
        receiver_rows, weight_in[2 * feature_width :], preferred_element_type=jnp.float32
    )
    hidden_rows = jax.nn.relu(pre_act + bias_in).astype(jnp.bfloat16)
    messages = layer_norm(
        jnp.dot(hidden_rows, weight_out, preferred_element_type=jnp.float32), norm_gain
    )
    messages = jnp.where(live_rows[:, None], messages, jnp.float32(0.0))
    return ((edge_rows.astype(jnp.float32) + messages).astype(jnp.bfloat16), messages)


def node_update(node_rows, aggregate, weight_in, bias_in, weight_out, norm_gain):
    feature_width = node_rows.shape[1]
    pre_act = jnp.dot(node_rows, weight_in[:feature_width], preferred_element_type=jnp.float32)
    pre_act = pre_act + jnp.dot(
        aggregate, weight_in[feature_width:], preferred_element_type=jnp.float32
    )
    hidden_rows = jax.nn.relu(pre_act + bias_in).astype(jnp.bfloat16)
    update = layer_norm(
        jnp.dot(hidden_rows, weight_out, preferred_element_type=jnp.float32), norm_gain
    )
    return (node_rows.astype(jnp.float32) + update).astype(jnp.bfloat16)


F32 = jnp.float32
BF16 = jnp.bfloat16
TILE = 256
HALF = 128
ROWS = 512
LOCAL_ROWS = 1024
I16 = jnp.int16
IN_VMEM = pl.BlockSpec(memory_space=pltpu.VMEM)
IN_SMEM = pl.BlockSpec(memory_space=pltpu.SMEM)
IN_HBM = pl.BlockSpec(memory_space=pltpu.HBM)


def shaped(shape, dtype):
    return jax.ShapeDtypeStruct(shape, dtype)


def call(kernel, outs, args, scratch=(), smem=(), stay=(), leave=(), flops=0, limit=24):
    nbytes = sum(a.size * a.dtype.itemsize for a in args)
    return pl.pallas_call(
        kernel,
        out_shape=outs,
        in_specs=[
            IN_SMEM if k in smem else IN_HBM if k in stay else IN_VMEM for k in range(len(args))
        ],
        out_specs=[IN_HBM if k in leave else IN_VMEM for k in range(len(outs))]
        if isinstance(outs, list)
        else IN_VMEM,
        scratch_shapes=scratch,
        compiler_params=pltpu.CompilerParams(vmem_limit_bytes=limit << 20),
        cost_estimate=pl.CostEstimate(flops=flops, transcendentals=0, bytes_accessed=nbytes),
    )(*args)


def place(stride):
    dom = lax.axis_index("dom")
    core = lax.axis_index("edge")
    return core, lax.rem(dom, 2), lax.rem(lax.div(dom, stride), 2)


def mm(a, b):
    return jnp.dot(a, b, preferred_element_type=F32)


def column(row):
    return jnp.transpose(jnp.broadcast_to(row, (HALF, HALF)))


def one_hot_rows(row, width):
    col = column(row)
    lane = lax.broadcasted_iota(jnp.int32, (HALF, HALF), 1)
    parts = [jnp.where(col == lane + k, 1.0, 0.0) for k in range(0, width, HALF)]
    return jnp.concatenate(parts, axis=1).astype(BF16)


def dyn(start, size, unit=None):
    return pl.ds(pl.multiple_of(start, unit or size), size)


def faces(stride):
    core, par_d, par_s = place(stride)
    par = jnp.where(core == 0, par_d, par_s)
    return 2 * core + 1 - par, 2 * core + par


def face_hits(stride, lists):
    rows = [one_hot_rows(lists[0, pl.ds(face, 1), :], TILE) for face in faces(stride)]
    return jnp.concatenate(rows, axis=0)


def pick_kernel(stride, own_ref, peer_ref, list_own, list_peer, far, near):
    for n, (lists, nodes) in enumerate(((list_own, own_ref), (list_peer, peer_ref))):
        picked = mm(face_hits(stride, lists), nodes[...]).astype(BF16)
        far[n * HALF : (n + 1) * HALF, :] = picked[:HALF]
        near[n * HALF : (n + 1) * HALF, :] = picked[HALF:]


def load_kernel(count, *refs):
    hbm, vmem, sems = refs[:count], refs[count:-1], refs[-1]
    copies = [
        pltpu.make_async_copy(src if len(src.shape) == len(dst.shape) else src.at[0], dst, sems.at[k])
        for k, (src, dst) in enumerate(zip(hbm, vmem))
    ]
    for copy in copies:
        copy.start()
    for copy in copies:
        copy.wait()


def in_hbm(arrays):
    return [pltpu.with_memory_space_constraint(a, pltpu.HBM) for a in arrays]


def columns(stride, send_ref, recv_ref, cols, at):
    _, par_d, par_s = place(stride)
    v = send_ref[:, at]
    j = v - 2 * TILE
    owner = lax.shift_right_arithmetic(j, 9)
    face = lax.shift_right_arithmetic(j, 7) & 3
    core = lax.shift_right_arithmetic(face, 1)
    par = jnp.where(core == 0, par_d, par_s)
    near = (face & 1) != par
    tile = jnp.where(near, 2, 4) + core
    at_tile = ((owner ^ core) & 1) * HALF + (j & (HALF - 1))
    spot = jnp.where(v < 2 * TILE, v, tile * TILE + at_tile)
    cols[0, at, :] = column(spot).astype(I16)
    cols[1, at, :] = column(recv_ref[:, at]).astype(I16)


def hits(spots, first, tiles):
    one = jnp.ones(spots.shape, BF16)
    zero = jnp.zeros(spots.shape, BF16)
    lane = lax.broadcasted_iota(jnp.int32, spots.shape, 1)
    parts = [
        jnp.where(spots == (lane + (first * TILE + k * HALF)).astype(I16), one, zero)
        for k in range(2 * tiles)
    ]
    return jnp.concatenate(parts, axis=1)


def project(parts, w1_ref, table):
    for k in (1, 2):
        for start, size, ref in parts:
            table[dyn((2 * k - 2) * TILE + start, size, TILE), :] = mm(
                ref[...], w1_ref[k * TILE : (k + 1) * TILE, :]
            ).astype(BF16)


def local_block(layer, at, edge_ref, cols, w1_ref, b1_ref, table, pre_ref):
    acc = mm(edge_ref[at, :], w1_ref[0:TILE, :])
    acc = acc + mm(hits(cols[0, at, :], 0, 2), table[0 : 2 * TILE, :])
    acc = acc + mm(hits(cols[1, at, :], 0, 2), table[2 * TILE :, :])
    pre_ref[at, :] = acc + b1_ref[layer : layer + 1, :]


def first_kernel(stride, loads, send_ref, recv_ref, own_ref, peer_ref, w1_ref, b1_ref, *refs):
    hbm, (pre_ref, cols), refs = refs[:loads], refs[loads : loads + 2], refs[loads + 2 :]
    vmem, (table, sems) = refs[:loads], refs[loads:]
    edge_hbm, edge_ref = hbm[0], vmem[0]
    blocks = [pl.ds(start, LOCAL_ROWS) for start in range(0, edge_ref.shape[0], LOCAL_ROWS)]
    copies = [(edge_hbm.at[at, :], edge_ref.at[at, :]) for at in blocks]
    copies += [(hbm[1].at[1], vmem[1])] + list(zip(hbm[2:], vmem[2:]))
    copies = [pltpu.make_async_copy(*ends, sems.at[k]) for k, ends in enumerate(copies)]
    copies[0].start()
    core = lax.axis_index("edge")
    parts = ((core * TILE, TILE, own_ref), ((1 - core) * TILE, TILE, peer_ref))

    def make(k):
        for start in range(k * LOCAL_ROWS, (k + 1) * LOCAL_ROWS, HALF):
            columns(stride, send_ref, recv_ref, cols, pl.ds(start, HALF))

    make(0)
    project(parts, w1_ref, table)
    for k, at in enumerate(blocks):
        copies[k].wait()
        if k + 1 < len(blocks):
            copies[k + 1].start()
            make(k + 1)
        else:
            for copy in copies[len(blocks) :]:
                copy.start()
        local_block(0, at, edge_ref, cols, w1_ref, b1_ref, table, pre_ref)
    for copy in copies[len(blocks) :]:
        copy.wait()


def local_kernel(layer, edge_ref, cols, dom_ref, w1_ref, b1_ref, pre_ref, table):
    project(((0, 2 * TILE, dom_ref),), w1_ref, table)

    def step(k, carry):
        at = dyn(k * LOCAL_ROWS, LOCAL_ROWS)
        local_block(layer, at, edge_ref, cols, w1_ref, b1_ref, table, pre_ref)
        return carry

    lax.fori_loop(0, edge_ref.shape[0] // LOCAL_ROWS, step, 0)


def halo_tables(own, peer, w1_ref, table):
    core = lax.axis_index("edge")
    w_s = w1_ref[TILE : 2 * TILE, :]
    for axis, ref in ((core, own), (1 - core, peer)):
        table[dyn(axis * TILE, TILE), :] = mm(ref[...], w_s).astype(BF16)


def tile_kernel(first, peer, pre_ref, cols, w1_ref, rows_ref, out_ref):
    core = lax.axis_index("edge")
    tile = first + (1 - core if peer else core)
    table = mm(rows_ref[...], w1_ref[TILE : 2 * TILE, :]).astype(BF16)
    half = pre_ref.shape[0] // 2

    def step(k, carry):
        at = dyn(k * half, half)
        out_ref[at, :] = pre_ref[at, :] + mm(hits(cols[0, at, :], tile, 1), table)
        return carry

    lax.fori_loop(0, 2, step, 0)


def edge_kernel(
    layer, split, live_ref, pre_ref, cols, recv_ref, edge_ref, w1_ref, w2_ref, gain_ref, *refs
):
    own, peer, refs = (None, *refs[:1], refs[1:]) if split else (*refs[:2], refs[2:])
    out_ref, refs = refs[0], refs[1:]
    if split:
        keep_ref, give_ref, table, raw, msgs, sums = refs
    else:
        part_ref, table, raw, msgs, sums = refs
    if split:
        first, tiles = 5 - lax.axis_index("edge"), 1
        table[0:TILE, :] = mm(peer[...], w1_ref[TILE : 2 * TILE, :]).astype(BF16)
    else:
        first, tiles = 4, 2
        halo_tables(own, peer, w1_ref, table)
    gain = gain_ref[layer : layer + 1, :]
    live = live_ref[0, 0]
    count = edge_ref.shape[0] // ROWS

    def gather(at):
        acc = pre_ref[at, :] + mm(hits(cols[0, at, :], first, tiles), table[0 : tiles * TILE, :])
        hidden = jnp.maximum(acc.astype(BF16), jnp.asarray(0, BF16))
        raw[at, :] = mm(hidden, w2_ref[layer])

    def norm(at, start):
        values = raw[at, :]
        center = values - jnp.mean(values, axis=-1, keepdims=True)
        spread = jnp.mean(center * center, axis=-1, keepdims=True)
        scale = lax.rsqrt(spread + eps_norm)
        row = lax.broadcasted_iota(jnp.int32, scale.shape, 0) + start
        scale = jnp.where(row < live, scale, 0.0)
        message = (center * scale * gain).astype(BF16)
        msgs[at, :] = message
        out_ref[at, :] = edge_ref[at, :] + message

    def segment(at, new):
        shape = (2 * TILE, ROWS)
        spot = lax.broadcasted_iota(jnp.int32, shape, 0).astype(I16)
        here = jnp.broadcast_to(recv_ref[:, at].astype(I16), shape)
        hot = jnp.where(here == spot, jnp.ones(shape, BF16), jnp.zeros(shape, BF16))
        part = mm(hot, msgs[at, :])
        sums[...] = part if new else sums[...] + part

    for k in range(count + 2):
        if k >= 2:
            segment(pl.ds((k - 2) * ROWS, ROWS), k == 2)
        if 1 <= k <= count:
            norm(pl.ds((k - 1) * ROWS, ROWS), (k - 1) * ROWS)
        if k < count:
            gather(pl.ds(k * ROWS, ROWS))
    if split:
        core = lax.axis_index("edge")
        keep_ref[...] = sums[dyn(core * TILE, TILE), :].astype(BF16)
        give_ref[...] = sums[dyn((1 - core) * TILE, TILE), :].astype(BF16)
    else:
        part_ref[...] = sums[...].astype(BF16)


def updated(layer, nodes, first, second, w1_ref, b1_ref, w2_ref, gain_ref):
    total = (first.astype(F32) + second.astype(F32)).astype(BF16)
    pre = mm(nodes, w1_ref[layer, 0:TILE, :]) + mm(total, w1_ref[layer, TILE:, :])
    hidden = jnp.maximum(pre + b1_ref[layer : layer + 1, :], 0.0).astype(BF16)
    step = layer_norm(mm(hidden, w2_ref[layer]), gain_ref[layer : layer + 1, :])
    return (nodes.astype(F32) + step).astype(BF16)


def node_kernel(
    stride, layer, own_ref, peer_ref, first, second, list_own, list_peer, w1, b1, w2, gain, out, far, near
):
    core = lax.axis_index("edge")
    hot = [face_hits(stride, lists) for lists in (list_own, list_peer)]
    for n, (owner, ref) in enumerate(((core, own_ref), (1 - core, peer_ref))):
        at = dyn(owner * TILE, TILE)
        nodes = updated(layer, ref[...], first[at, :], second[at, :], w1, b1, w2, gain)
        out[at, :] = nodes
        picked = mm(hot[n], nodes).astype(BF16)
        far[n * HALF : (n + 1) * HALF, :] = picked[:HALF]
        near[n * HALF : (n + 1) * HALF, :] = picked[HALF:]


def last_kernel(layer, nodes_ref, first, second, w1, b1, w2, gain, out):
    core = lax.axis_index("edge")
    nodes = nodes_ref[dyn(core * TILE, TILE), :]
    out[...] = updated(layer, nodes, first[...], second[...], w1, b1, w2, gain)


def met(count, stride, odd):
    pairs = []
    for dom in range(count):
        ahead = (dom // stride) % 2 == odd
        pairs.append((dom + (stride if ahead else -stride)) % count)
    return pairs


def swapped(value):
    return lax.ppermute(value, "edge", [(0, 1), (1, 0)])


def fast_shards(
    node_lat,
    edge_lat,
    senders,
    receivers,
    live_edges,
    send_rows,
    edge_w1,
    edge_b1,
    edge_w2,
    edge_gain,
    node_w1,
    node_b1,
    node_w2,
    node_gain,
):
    domains = lax.axis_size("dom")
    stride = domains // 4
    edges, width = edge_lat.shape
    nodes = node_lat.shape[0]
    near_d, far_d = met(domains, 1, 0), met(domains, 1, 1)
    near_s, far_s = met(domains, stride, 0), met(domains, stride, 1)

    def sent_by_core(value, partner_d, partner_s):
        pairs = [(2 * d, 2 * p) for d, p in enumerate(partner_d)]
        pairs += [(2 * d + 1, 2 * p + 1) for d, p in enumerate(partner_s)]
        return lax.ppermute(value, ("dom", "edge"), pairs)

    table = pltpu.VMEM((2 * TILE, width), BF16)
    messages = pltpu.VMEM((edges, width), BF16)
    pre_shape = shaped((edges, width), F32)
    rows_out = shaped((TILE, width), BF16)
    pass_flops = 2 * edges * TILE * width

    peer_nodes = swapped(node_lat)
    peer_lists = swapped(send_rows)
    send_at, recv_at = senders[None], receivers[None]
    first = (node_lat, send_rows, send_at, recv_at, edge_b1, edge_w1)
    node_lat, send_rows, send_at, recv_at, edge_b1, first_w1 = call(
        functools.partial(load_kernel, len(first)),
        [shaped(a.shape, a.dtype) for a in first[:-1]] + [shaped(edge_w1.shape[1:], BF16)],
        in_hbm(first),
        scratch=[pltpu.SemaphoreType.DMA((len(first),))],
        stay=range(len(first)),
    )
    far_rows, near_rows = call(
        functools.partial(pick_kernel, stride),
        [rows_out, rows_out],
        (node_lat, peer_nodes, send_rows, peer_lists),
    )
    for layer in range(LAYERS):
        last = layer == LAYERS - 1
        near = sent_by_core(near_rows, near_d, near_s)
        far = sent_by_core(far_rows, far_d, far_s)
        if layer == 0:
            loads = (edge_lat, edge_w1, edge_w2, node_w1, node_w2, edge_gain, node_b1, node_gain)
            pre, cols, edge_rows, next_w1, edge_w2, node_w1, node_w2, edge_gain, node_b1, node_gain = call(
                functools.partial(first_kernel, stride, len(loads)),
                [pre_shape, shaped((2, edges, HALF), I16)]
                + [shaped(a.shape[1:] if a is edge_w1 else a.shape, a.dtype) for a in loads],
                (send_at, recv_at, node_lat, peer_nodes, first_w1, edge_b1, *in_hbm(loads)),
                scratch=[
                    pltpu.VMEM((4 * TILE, width), BF16),
                    pltpu.SemaphoreType.DMA((edges // LOCAL_ROWS + len(loads) - 1,)),
                ],
                stay=range(6, 6 + len(loads)),
                flops=5 * pass_flops,
            )
        else:
            pre = call(
                functools.partial(local_kernel, layer),
                pre_shape,
                (edge_rows, cols, all_nodes, next_w1, edge_b1),
                scratch=[pltpu.VMEM((4 * TILE, width), BF16)],
                flops=5 * pass_flops,
            )
        w1 = next_w1 if layer else first_w1

        def add(first, peer, pre, rows):
            return call(
                functools.partial(tile_kernel, first, peer),
                pre_shape,
                (pre, cols, w1, rows),
                flops=pass_flops,
            )

        pre, near, live_edges = lax.optimization_barrier((pre, near, live_edges))
        near_other = swapped(near)
        if last:
            pre = add(2, False, pre, near)
            pre = add(2, True, pre, near_other)
            pre, far = lax.optimization_barrier((pre, far))
            far_other = (swapped(far),)
            pre = add(4, False, pre, far)
        else:
            pre = add(2, False, pre, near)
            pre, far = lax.optimization_barrier((pre, far))
            far_other = (far, swapped(far))
            pre = add(2, True, pre, near_other)
        if last:
            outs = [shaped((nodes, width), BF16)] * 2
        else:
            outs = [shaped((2 * nodes, width), BF16)]
        edge_rows, *partial = call(
            functools.partial(edge_kernel, layer, last),
            [shaped((edges, width), BF16)] + outs,
            (live_edges, pre, cols, recv_at, edge_rows, w1, edge_w2, edge_gain, *far_other),
            scratch=[
                table,
                pltpu.VMEM((edges, width), F32),
                messages,
                pltpu.VMEM((2 * nodes, width), F32),
            ],
            smem=(0,),
            flops=5 * pass_flops,
        )
        other = swapped(partial[-1])
        weights = (node_w1, node_b1, node_w2, node_gain)
        if last:
            (edge_out,) = call(
                functools.partial(load_kernel, 1),
                [shaped((edges, width), BF16)],
                (edge_rows,),
                scratch=[pltpu.SemaphoreType.DMA((1,))],
                leave=(0,),
            )
            out = call(
                functools.partial(last_kernel, layer),
                shaped((nodes, width), BF16),
                (all_nodes, partial[0], other, *weights),
            )
        else:
            all_nodes, far_rows, near_rows = call(
                functools.partial(node_kernel, stride, layer),
                [shaped((2 * nodes, width), BF16), rows_out, rows_out],
                (node_lat, peer_nodes, partial[0], other, send_rows, peer_lists, *weights),
            )
    return out, edge_out


def shards(*args):
    node_lat, edge_lat, _, _, _, send_rows = args[:6]
    domains = lax.axis_size("dom")
    fits = (
        lax.axis_size("edge") == 2
        and domains % 8 == 0
        and node_lat.shape == (TILE, TILE)
        and edge_lat.shape[0] % LOCAL_ROWS == 0
        and send_rows.shape[1:] == (4, HALF)
        and args[6].shape == (LAYERS, 3 * TILE, TILE)
    )
    return (fast_shards if fits else general_shards)(*args)


def general_shards(
    node_lat,
    edge_lat,
    senders,
    receivers,
    live_edges,
    send_rows,
    edge_w1,
    edge_b1,
    edge_w2,
    edge_gain,
    node_w1,
    node_b1,
    node_w2,
    node_gain,
):
    rank_count = lax.axis_size("edge")
    domains = lax.axis_size("dom")
    stride = domains // 4
    offsets = (1, -1, stride, -stride)
    node_count = node_lat.shape[0]
    face_count = send_rows.shape[1]
    latent = node_lat.shape[1]
    live_rows = lax.broadcasted_iota(jnp.int32, (edge_lat.shape[0],), 0) < live_edges[0, 0]
    lists_all = None
    lists_all = lax.all_gather(send_rows, "edge", axis=0, tiled=True)
    lists_all = lists_all + (jnp.arange(rank_count, dtype=jnp.int32) * node_count)[:, None, None]
    owned_rows = node_lat
    edge_rows = edge_lat
    for layer_index in range(LAYERS):
        received = []
        domain_rows = lax.all_gather(owned_rows, "edge", axis=0, tiled=True)
        face_rows = jnp.take(domain_rows, lists_all, axis=0)
        for face_index in range(face_count):
            received.append(passed_along(face_rows[:, face_index], "dom", offsets[face_index]))
        halo_all = jnp.stack(received, axis=1).reshape(-1, latent)
        node_table = jnp.concatenate([domain_rows, halo_all], axis=0)
        sender_rows = jnp.take(node_table, senders, axis=0)
        receiver_rows = jnp.take(domain_rows, receivers, axis=0)
        edge_rows, messages = edge_update(
            edge_rows,
            sender_rows,
            receiver_rows,
            edge_w1[layer_index],
            edge_b1[layer_index],
            edge_w2[layer_index],
            edge_gain[layer_index],
            live_rows,
        )
        summed = lax.psum_scatter(
            jax.ops.segment_sum(
                messages, receivers, num_segments=lax.axis_size("edge") * node_count
            ).astype(jnp.bfloat16),
            "edge",
            scatter_dimension=0,
            tiled=True,
        )
        owned_rows = node_update(
            owned_rows,
            summed,
            node_w1[layer_index],
            node_b1[layer_index],
            node_w2[layer_index],
            node_gain[layer_index],
        )
    return (owned_rows, edge_rows)


def solution(mesh):
    in_specs = (
        P(("dom", "edge"), None),
        P(("dom", "edge"), None),
        P(("dom", "edge")),
        P(("dom", "edge")),
        P("dom", "edge"),
        P(("dom", "edge"), None, None),
        P(),
        P(),
        P(),
        P(),
        P(),
        P(),
        P(),
        P(),
    )
    out_specs = (P(("dom", "edge"), None), P(("dom", "edge"), None))
    return jax.shard_map(shards, mesh=mesh, in_specs=in_specs, out_specs=out_specs, check_vma=False)
```

```python
import functools

import jax
import jax.numpy as jnp
from jax import lax
from jax.experimental import pallas as pl
from jax.experimental.pallas import tpu as pltpu
from jax.sharding import PartitionSpec as P

LAYERS = 2


eps_norm = 1e-05


def passed_along(value, axis, steps):
    count = lax.axis_size(axis)
    pairs = [(source, (source + steps) % count) for source in range(count)]
    return lax.ppermute(value, axis, pairs)


def layer_norm(values, norm_gain):
    center = values - jnp.mean(values, axis=-1, keepdims=True)
    spread = jnp.mean(center * center, axis=-1, keepdims=True)
    return center * lax.rsqrt(spread + eps_norm) * norm_gain


def edge_update(
    edge_rows, sender_rows, receiver_rows, weight_in, bias_in, weight_out, norm_gain, live_rows
):
    feature_width = edge_rows.shape[1]
    pre_act = jnp.dot(edge_rows, weight_in[:feature_width], preferred_element_type=jnp.float32)
    pre_act = pre_act + jnp.dot(
        sender_rows,
        weight_in[feature_width : 2 * feature_width],
        preferred_element_type=jnp.float32,
    )
    pre_act = pre_act + jnp.dot(
        receiver_rows, weight_in[2 * feature_width :], preferred_element_type=jnp.float32
    )
    hidden_rows = jax.nn.relu(pre_act + bias_in).astype(jnp.bfloat16)
    messages = layer_norm(
        jnp.dot(hidden_rows, weight_out, preferred_element_type=jnp.float32), norm_gain
    )
    messages = jnp.where(live_rows[:, None], messages, jnp.float32(0.0))
    return ((edge_rows.astype(jnp.float32) + messages).astype(jnp.bfloat16), messages)


def node_update(node_rows, aggregate, weight_in, bias_in, weight_out, norm_gain):
    feature_width = node_rows.shape[1]
    pre_act = jnp.dot(node_rows, weight_in[:feature_width], preferred_element_type=jnp.float32)
    pre_act = pre_act + jnp.dot(
        aggregate, weight_in[feature_width:], preferred_element_type=jnp.float32
    )
    hidden_rows = jax.nn.relu(pre_act + bias_in).astype(jnp.bfloat16)
    update = layer_norm(
        jnp.dot(hidden_rows, weight_out, preferred_element_type=jnp.float32), norm_gain
    )
    return (node_rows.astype(jnp.float32) + update).astype(jnp.bfloat16)


F32 = jnp.float32
BF16 = jnp.bfloat16
TILE = 256
HALF = 128
ROWS = 512
LOCAL_ROWS = 1024
I16 = jnp.int16
IN_VMEM = pl.BlockSpec(memory_space=pltpu.VMEM)
IN_SMEM = pl.BlockSpec(memory_space=pltpu.SMEM)
IN_HBM = pl.BlockSpec(memory_space=pltpu.HBM)


def shaped(shape, dtype):
    return jax.ShapeDtypeStruct(shape, dtype)


def call(kernel, outs, args, scratch=(), smem=(), stay=(), leave=(), flops=0, limit=24):
    nbytes = sum(a.size * a.dtype.itemsize for a in args)
    return pl.pallas_call(
        kernel,
        out_shape=outs,
        in_specs=[
            IN_SMEM if k in smem else IN_HBM if k in stay else IN_VMEM for k in range(len(args))
        ],
        out_specs=[IN_HBM if k in leave else IN_VMEM for k in range(len(outs))]
        if isinstance(outs, list)
        else IN_VMEM,
        scratch_shapes=scratch,
        compiler_params=pltpu.CompilerParams(vmem_limit_bytes=limit << 20),
        cost_estimate=pl.CostEstimate(flops=flops, transcendentals=0, bytes_accessed=nbytes),
    )(*args)


def place(stride):
    dom = lax.axis_index("dom")
    core = lax.axis_index("edge")
    return core, lax.rem(dom, 2), lax.rem(lax.div(dom, stride), 2)


def mm(a, b):
    return jnp.dot(a, b, preferred_element_type=F32)


def column(row):
    return jnp.transpose(jnp.broadcast_to(row, (HALF, HALF)))


def one_hot_rows(row, width):
    col = column(row)
    lane = lax.broadcasted_iota(jnp.int32, (HALF, HALF), 1)
    parts = [jnp.where(col == lane + k, 1.0, 0.0) for k in range(0, width, HALF)]
    return jnp.concatenate(parts, axis=1).astype(BF16)


def dyn(start, size, unit=None):
    return pl.ds(pl.multiple_of(start, unit or size), size)


def faces(stride):
    core, par_d, par_s = place(stride)
    par = jnp.where(core == 0, par_d, par_s)
    return 2 * core + 1 - par, 2 * core + par


def face_hits(stride, lists):
    return [one_hot_rows(lists[0, pl.ds(face, 1), :], TILE) for face in faces(stride)]


def pick_kernel(stride, own_ref, peer_ref, list_own, list_peer, far, near):
    for n, (lists, nodes) in enumerate(((list_own, own_ref), (list_peer, peer_ref))):
        for rows, out_rows in zip(face_hits(stride, lists), (far, near)):
            out_rows[n * HALF : (n + 1) * HALF, :] = mm(rows, nodes[...]).astype(BF16)


def load_kernel(count, *refs):
    hbm, vmem, sems = refs[:count], refs[count:-1], refs[-1]
    copies = [
        pltpu.make_async_copy(src if len(src.shape) == len(dst.shape) else src.at[0], dst, sems.at[k])
        for k, (src, dst) in enumerate(zip(hbm, vmem))
    ]
    for copy in copies:
        copy.start()
    for copy in copies:
        copy.wait()


def in_hbm(arrays):
    return [pltpu.with_memory_space_constraint(a, pltpu.HBM) for a in arrays]


def columns(stride, send_ref, recv_ref, cols, at):
    _, par_d, par_s = place(stride)
    v = send_ref[:, at]
    j = v - 2 * TILE
    owner = lax.shift_right_arithmetic(j, 9)
    face = lax.shift_right_arithmetic(j, 7) & 3
    core = lax.shift_right_arithmetic(face, 1)
    par = jnp.where(core == 0, par_d, par_s)
    near = (face & 1) != par
    tile = jnp.where(near, 2, 4) + core
    at_tile = ((owner ^ core) & 1) * HALF + (j & (HALF - 1))
    spot = jnp.where(v < 2 * TILE, v, tile * TILE + at_tile)
    cols[0, at, :] = column(spot).astype(I16)
    cols[1, at, :] = column(recv_ref[:, at]).astype(I16)


def hits(spots, first, tiles):
    one = jnp.ones(spots.shape, BF16)
    zero = jnp.zeros(spots.shape, BF16)
    lane = lax.broadcasted_iota(jnp.int32, spots.shape, 1)
    parts = [
        jnp.where(spots == (lane + (first * TILE + k * HALF)).astype(I16), one, zero)
        for k in range(2 * tiles)
    ]
    return jnp.concatenate(parts, axis=1)


def project(parts, w1_ref, table):
    for k in (1, 2):
        for start, size, ref in parts:
            table[dyn((2 * k - 2) * TILE + start, size, TILE), :] = mm(
                ref[...], w1_ref[k * TILE : (k + 1) * TILE, :]
            ).astype(BF16)


def local_block(layer, at, cols, b1_ref, table, pre_ref, edges=None):
    acc = 0.0 if edges is None else mm(*edges)
    acc = acc + mm(hits(cols[0, at, :], 0, 2), table[0 : 2 * TILE, :])
    acc = acc + mm(hits(cols[1, at, :], 0, 2), table[2 * TILE :, :])
    pre_ref[at, :] = acc + b1_ref[layer : layer + 1, :]


def first_kernel(stride, loads, send_ref, recv_ref, own_ref, peer_ref, w1_ref, b1_ref, *refs):
    hbm, (pre_ref, cols), refs = refs[:loads], refs[loads : loads + 2], refs[loads + 2 :]
    vmem, (table, sems) = refs[:loads], refs[loads:]
    ends = [(hbm[0].at[1], vmem[0])] + list(zip(hbm[1:], vmem[1:]))
    copies = [pltpu.make_async_copy(*pair, sems.at[k]) for k, pair in enumerate(ends)]
    for copy in copies:
        copy.start()
    blocks = [pl.ds(start, LOCAL_ROWS) for start in range(0, pre_ref.shape[0], LOCAL_ROWS)]
    core = lax.axis_index("edge")
    parts = ((core * TILE, TILE, own_ref), ((1 - core) * TILE, TILE, peer_ref))

    def make(k):
        for start in range(k * LOCAL_ROWS, (k + 1) * LOCAL_ROWS, HALF):
            columns(stride, send_ref, recv_ref, cols, pl.ds(start, HALF))

    make(0)
    project(parts, w1_ref, table)
    for k, at in enumerate(blocks):
        if k + 1 < len(blocks):
            make(k + 1)
        local_block(0, at, cols, b1_ref, table, pre_ref)
    for copy in copies:
        copy.wait()


def local_kernel(layer, edge_ref, cols, dom_ref, w1_ref, b1_ref, pre_ref, table):
    project(((0, 2 * TILE, dom_ref),), w1_ref, table)

    def step(k, carry):
        at = dyn(k * LOCAL_ROWS, LOCAL_ROWS)
        edges = (edge_ref[at, :], w1_ref[0:TILE, :])
        local_block(layer, at, cols, b1_ref, table, pre_ref, edges)
        return carry

    lax.fori_loop(0, edge_ref.shape[0] // LOCAL_ROWS, step, 0)


def halo_tables(own, peer, w1_ref, table):
    core = lax.axis_index("edge")
    w_s = w1_ref[TILE : 2 * TILE, :]
    for axis, ref in ((core, own), (1 - core, peer)):
        table[dyn(axis * TILE, TILE), :] = mm(ref[...], w_s).astype(BF16)


def tile_kernel(first, peer, pre_ref, cols, w1_ref, rows_ref, *refs):
    out_ref = refs[-1]
    core = lax.axis_index("edge")
    tile = first + (1 - core if peer else core)
    table = mm(rows_ref[...], w1_ref[TILE : 2 * TILE, :]).astype(BF16)
    half = pre_ref.shape[0] // 2

    def step(k, carry):
        at = dyn(k * half, half)
        acc = pre_ref[at, :] + mm(hits(cols[0, at, :], tile, 1), table)
        if len(refs) == 2:
            acc = acc + mm(refs[0][at, :], w1_ref[0:TILE, :])
        out_ref[at, :] = acc
        return carry

    lax.fori_loop(0, 2, step, 0)


def edge_kernel(
    layer, split, live_ref, pre_ref, cols, recv_ref, edge_ref, w1_ref, w2_ref, gain_ref, *refs
):
    own, peer, refs = (None, *refs[:1], refs[1:]) if split else (*refs[:2], refs[2:])
    out_ref, refs = refs[0], refs[1:]
    if split:
        keep_ref, give_ref, table, raw, msgs, sums = refs
    else:
        part_ref, table, raw, msgs, sums = refs
    if split:
        first, tiles = 5 - lax.axis_index("edge"), 1
        table[0:TILE, :] = mm(peer[...], w1_ref[TILE : 2 * TILE, :]).astype(BF16)
    else:
        first, tiles = 4, 2
        halo_tables(own, peer, w1_ref, table)
    gain = gain_ref[layer : layer + 1, :]
    live = live_ref[0, 0]
    count = edge_ref.shape[0] // ROWS

    def gather(at):
        acc = pre_ref[at, :] + mm(hits(cols[0, at, :], first, tiles), table[0 : tiles * TILE, :])
        hidden = jnp.maximum(acc.astype(BF16), jnp.asarray(0, BF16))
        raw[at, :] = mm(hidden, w2_ref[layer])

    def norm(at, start):
        values = raw[at, :]
        center = values - jnp.mean(values, axis=-1, keepdims=True)
        spread = jnp.mean(center * center, axis=-1, keepdims=True)
        scale = lax.rsqrt(spread + eps_norm)
        row = lax.broadcasted_iota(jnp.int32, scale.shape, 0) + start
        scale = jnp.where(row < live, scale, 0.0)
        message = (center * scale * gain).astype(BF16)
        msgs[at, :] = message
        out_ref[at, :] = edge_ref[at, :] + message

    def segment(at, new):
        shape = (2 * TILE, ROWS)
        spot = lax.broadcasted_iota(jnp.int32, shape, 0).astype(I16)
        here = jnp.broadcast_to(recv_ref[:, at].astype(I16), shape)
        hot = jnp.where(here == spot, jnp.ones(shape, BF16), jnp.zeros(shape, BF16))
        part = mm(hot, msgs[at, :])
        sums[...] = part if new else sums[...] + part

    for k in range(count + 2):
        if k >= 2:
            segment(pl.ds((k - 2) * ROWS, ROWS), k == 2)
        if 1 <= k <= count:
            norm(pl.ds((k - 1) * ROWS, ROWS), (k - 1) * ROWS)
        if k < count:
            gather(pl.ds(k * ROWS, ROWS))
    if split:
        core = lax.axis_index("edge")
        keep_ref[...] = sums[dyn(core * TILE, TILE), :].astype(BF16)
        give_ref[...] = sums[dyn((1 - core) * TILE, TILE), :].astype(BF16)
    else:
        part_ref[...] = sums[...].astype(BF16)


def updated(layer, nodes, first, second, w1_ref, b1_ref, w2_ref, gain_ref):
    total = (first.astype(F32) + second.astype(F32)).astype(BF16)
    pre = mm(nodes, w1_ref[layer, 0:TILE, :]) + mm(total, w1_ref[layer, TILE:, :])
    hidden = jnp.maximum(pre + b1_ref[layer : layer + 1, :], 0.0).astype(BF16)
    step = layer_norm(mm(hidden, w2_ref[layer]), gain_ref[layer : layer + 1, :])
    return (nodes.astype(F32) + step).astype(BF16)


def node_kernel(
    stride, layer, own_ref, peer_ref, first, second, list_own, list_peer, w1, b1, w2, gain, out, far, near
):
    core = lax.axis_index("edge")
    nodes = []
    for owner, ref in ((core, own_ref), (1 - core, peer_ref)):
        at = dyn(owner * TILE, TILE)
        nodes.append(updated(layer, ref[...], first[at, :], second[at, :], w1, b1, w2, gain))
        out[at, :] = nodes[-1]
    for face, ref in zip(faces(stride), (far, near)):
        for n, lists in enumerate((list_own, list_peer)):
            rows = one_hot_rows(lists[0, pl.ds(face, 1), :], TILE)
            ref[n * HALF : (n + 1) * HALF, :] = mm(rows, nodes[n]).astype(BF16)


def last_kernel(layer, nodes_ref, first, second, w1, b1, w2, gain, out):
    core = lax.axis_index("edge")
    nodes = nodes_ref[dyn(core * TILE, TILE), :]
    out[...] = updated(layer, nodes, first[...], second[...], w1, b1, w2, gain)


def met(count, stride, odd):
    pairs = []
    for dom in range(count):
        ahead = (dom // stride) % 2 == odd
        pairs.append((dom + (stride if ahead else -stride)) % count)
    return pairs


def swapped(value):
    return lax.ppermute(value, "edge", [(0, 1), (1, 0)])


def fast_shards(
    node_lat,
    edge_lat,
    senders,
    receivers,
    live_edges,
    send_rows,
    edge_w1,
    edge_b1,
    edge_w2,
    edge_gain,
    node_w1,
    node_b1,
    node_w2,
    node_gain,
):
    domains = lax.axis_size("dom")
    stride = domains // 4
    edges, width = edge_lat.shape
    nodes = node_lat.shape[0]
    near_d, far_d = met(domains, 1, 0), met(domains, 1, 1)
    near_s, far_s = met(domains, stride, 0), met(domains, stride, 1)

    def sent_by_core(value, partner_d, partner_s):
        pairs = [(2 * d, 2 * p) for d, p in enumerate(partner_d)]
        pairs += [(2 * d + 1, 2 * p + 1) for d, p in enumerate(partner_s)]
        return lax.ppermute(value, ("dom", "edge"), pairs)

    table = pltpu.VMEM((2 * TILE, width), BF16)
    messages = pltpu.VMEM((edges, width), BF16)
    pre_shape = shaped((edges, width), F32)
    rows_out = shaped((TILE, width), BF16)
    pass_flops = 2 * edges * TILE * width

    peer_nodes = swapped(node_lat)
    peer_lists = swapped(send_rows)
    send_at, recv_at = senders[None], receivers[None]
    first = (node_lat, send_rows, send_at, recv_at, edge_b1, edge_w1)
    node_lat, send_rows, send_at, recv_at, edge_b1, first_w1 = call(
        functools.partial(load_kernel, len(first)),
        [shaped(a.shape, a.dtype) for a in first[:-1]] + [shaped(edge_w1.shape[1:], BF16)],
        in_hbm(first),
        scratch=[pltpu.SemaphoreType.DMA((len(first),))],
        stay=range(len(first)),
    )
    far_rows, near_rows = call(
        functools.partial(pick_kernel, stride),
        [rows_out, rows_out],
        (node_lat, peer_nodes, send_rows, peer_lists),
    )
    for layer in range(LAYERS):
        last = layer == LAYERS - 1
        near = sent_by_core(near_rows, near_d, near_s)
        far = sent_by_core(far_rows, far_d, far_s)
        if layer == 0:
            loads = (edge_w1, edge_lat, edge_w2, node_w1, node_w2, edge_gain, node_b1, node_gain)
            pre, cols, next_w1, edge_rows, edge_w2, node_w1, node_w2, edge_gain, node_b1, node_gain = call(
                functools.partial(first_kernel, stride, len(loads)),
                [pre_shape, shaped((2, edges, HALF), I16)]
                + [shaped(a.shape[1:] if a is edge_w1 else a.shape, a.dtype) for a in loads],
                (send_at, recv_at, node_lat, peer_nodes, first_w1, edge_b1, *in_hbm(loads)),
                scratch=[
                    pltpu.VMEM((4 * TILE, width), BF16),
                    pltpu.SemaphoreType.DMA((len(loads),)),
                ],
                stay=range(6, 6 + len(loads)),
                flops=5 * pass_flops,
            )
        else:
            pre = call(
                functools.partial(local_kernel, layer),
                pre_shape,
                (edge_rows, cols, all_nodes, next_w1, edge_b1),
                scratch=[pltpu.VMEM((4 * TILE, width), BF16)],
                flops=5 * pass_flops,
            )
        w1 = next_w1 if layer else first_w1

        def add(first, peer, pre, rows, *edges):
            return call(
                functools.partial(tile_kernel, first, peer),
                pre_shape,
                (pre, cols, w1, rows, *edges),
                flops=pass_flops,
            )

        pre, near, live_edges = lax.optimization_barrier((pre, near, live_edges))
        near_other = swapped(near)
        if last:
            pre = add(2, False, pre, near)
            pre = add(2, True, pre, near_other)
            pre, far = lax.optimization_barrier((pre, far))
            far_other = (swapped(far),)
            pre = add(4, False, pre, far)
        else:
            pre = add(2, False, pre, near, edge_rows)
            pre, far = lax.optimization_barrier((pre, far))
            far_other = (far, swapped(far))
            pre = add(2, True, pre, near_other)
        if last:
            outs = [shaped((nodes, width), BF16)] * 2
        else:
            outs = [shaped((2 * nodes, width), BF16)]
        edge_rows, *partial = call(
            functools.partial(edge_kernel, layer, last),
            [shaped((edges, width), BF16)] + outs,
            (live_edges, pre, cols, recv_at, edge_rows, w1, edge_w2, edge_gain, *far_other),
            scratch=[
                table,
                pltpu.VMEM((edges, width), F32),
                messages,
                pltpu.VMEM((2 * nodes, width), F32),
            ],
            smem=(0,),
            flops=5 * pass_flops,
        )
        other = swapped(partial[-1])
        weights = (node_w1, node_b1, node_w2, node_gain)
        if last:
            (edge_out,) = call(
                functools.partial(load_kernel, 1),
                [shaped((edges, width), BF16)],
                (edge_rows,),
                scratch=[pltpu.SemaphoreType.DMA((1,))],
                leave=(0,),
            )
            out = call(
                functools.partial(last_kernel, layer),
                shaped((nodes, width), BF16),
                (all_nodes, partial[0], other, *weights),
            )
        else:
            all_nodes, far_rows, near_rows = call(
                functools.partial(node_kernel, stride, layer),
                [shaped((2 * nodes, width), BF16), rows_out, rows_out],
                (node_lat, peer_nodes, partial[0], other, send_rows, peer_lists, *weights),
            )
    return out, edge_out


def shards(*args):
    node_lat, edge_lat, _, _, _, send_rows = args[:6]
    domains = lax.axis_size("dom")
    fits = (
        lax.axis_size("edge") == 2
        and domains % 8 == 0
        and node_lat.shape == (TILE, TILE)
        and edge_lat.shape[0] % LOCAL_ROWS == 0
        and send_rows.shape[1:] == (4, HALF)
        and args[6].shape == (LAYERS, 3 * TILE, TILE)
    )
    return (fast_shards if fits else general_shards)(*args)


def general_shards(
    node_lat,
    edge_lat,
    senders,
    receivers,
    live_edges,
    send_rows,
    edge_w1,
    edge_b1,
    edge_w2,
    edge_gain,
    node_w1,
    node_b1,
    node_w2,
    node_gain,
):
    rank_count = lax.axis_size("edge")
    domains = lax.axis_size("dom")
    stride = domains // 4
    offsets = (1, -1, stride, -stride)
    node_count = node_lat.shape[0]
    face_count = send_rows.shape[1]
    latent = node_lat.shape[1]
    live_rows = lax.broadcasted_iota(jnp.int32, (edge_lat.shape[0],), 0) < live_edges[0, 0]
    lists_all = None
    lists_all = lax.all_gather(send_rows, "edge", axis=0, tiled=True)
    lists_all = lists_all + (jnp.arange(rank_count, dtype=jnp.int32) * node_count)[:, None, None]
    owned_rows = node_lat
    edge_rows = edge_lat
    for layer_index in range(LAYERS):
        received = []
        domain_rows = lax.all_gather(owned_rows, "edge", axis=0, tiled=True)
        face_rows = jnp.take(domain_rows, lists_all, axis=0)
        for face_index in range(face_count):
            received.append(passed_along(face_rows[:, face_index], "dom", offsets[face_index]))
        halo_all = jnp.stack(received, axis=1).reshape(-1, latent)
        node_table = jnp.concatenate([domain_rows, halo_all], axis=0)
        sender_rows = jnp.take(node_table, senders, axis=0)
        receiver_rows = jnp.take(domain_rows, receivers, axis=0)
        edge_rows, messages = edge_update(
            edge_rows,
            sender_rows,
            receiver_rows,
            edge_w1[layer_index],
            edge_b1[layer_index],
            edge_w2[layer_index],
            edge_gain[layer_index],
            live_rows,
        )
        summed = lax.psum_scatter(
            jax.ops.segment_sum(
                messages, receivers, num_segments=lax.axis_size("edge") * node_count
            ).astype(jnp.bfloat16),
            "edge",
            scatter_dimension=0,
            tiled=True,
        )
        owned_rows = node_update(
            owned_rows,
            summed,
            node_w1[layer_index],
            node_b1[layer_index],
            node_w2[layer_index],
            node_gain[layer_index],
        )
    return (owned_rows, edge_rows)


def solution(mesh):
    in_specs = (
        P(("dom", "edge"), None),
        P(("dom", "edge"), None),
        P(("dom", "edge")),
        P(("dom", "edge")),
        P("dom", "edge"),
        P(("dom", "edge"), None, None),
        P(),
        P(),
        P(),
        P(),
        P(),
        P(),
        P(),
        P(),
    )
    out_specs = (P(("dom", "edge"), None), P(("dom", "edge"), None))
    return jax.shard_map(shards, mesh=mesh, in_specs=in_specs, out_specs=out_specs, check_vma=False)
```

```python
import functools

import jax
import jax.numpy as jnp
from jax import lax
from jax.experimental import pallas as pl
from jax.experimental.pallas import tpu as pltpu
from jax.sharding import PartitionSpec as P

LAYERS = 2


eps_norm = 1e-05


def passed_along(value, axis, steps):
    count = lax.axis_size(axis)
    pairs = [(source, (source + steps) % count) for source in range(count)]
    return lax.ppermute(value, axis, pairs)


def layer_norm(values, norm_gain):
    center = values - jnp.mean(values, axis=-1, keepdims=True)
    spread = jnp.mean(center * center, axis=-1, keepdims=True)
    return center * lax.rsqrt(spread + eps_norm) * norm_gain


def edge_update(
    edge_rows, sender_rows, receiver_rows, weight_in, bias_in, weight_out, norm_gain, live_rows
):
    feature_width = edge_rows.shape[1]
    pre_act = jnp.dot(edge_rows, weight_in[:feature_width], preferred_element_type=jnp.float32)
    pre_act = pre_act + jnp.dot(
        sender_rows,
        weight_in[feature_width : 2 * feature_width],
        preferred_element_type=jnp.float32,
    )
    pre_act = pre_act + jnp.dot(
        receiver_rows, weight_in[2 * feature_width :], preferred_element_type=jnp.float32
    )
    hidden_rows = jax.nn.relu(pre_act + bias_in).astype(jnp.bfloat16)
    messages = layer_norm(
        jnp.dot(hidden_rows, weight_out, preferred_element_type=jnp.float32), norm_gain
    )
    messages = jnp.where(live_rows[:, None], messages, jnp.float32(0.0))
    return ((edge_rows.astype(jnp.float32) + messages).astype(jnp.bfloat16), messages)


def node_update(node_rows, aggregate, weight_in, bias_in, weight_out, norm_gain):
    feature_width = node_rows.shape[1]
    pre_act = jnp.dot(node_rows, weight_in[:feature_width], preferred_element_type=jnp.float32)
    pre_act = pre_act + jnp.dot(
        aggregate, weight_in[feature_width:], preferred_element_type=jnp.float32
    )
    hidden_rows = jax.nn.relu(pre_act + bias_in).astype(jnp.bfloat16)
    update = layer_norm(
        jnp.dot(hidden_rows, weight_out, preferred_element_type=jnp.float32), norm_gain
    )
    return (node_rows.astype(jnp.float32) + update).astype(jnp.bfloat16)


F32 = jnp.float32
BF16 = jnp.bfloat16
TILE = 256
HALF = 128
ROWS = 512
LOCAL_ROWS = 1024
I16 = jnp.int16
IN_VMEM = pl.BlockSpec(memory_space=pltpu.VMEM)
IN_SMEM = pl.BlockSpec(memory_space=pltpu.SMEM)
IN_HBM = pl.BlockSpec(memory_space=pltpu.HBM)


def shaped(shape, dtype):
    return jax.ShapeDtypeStruct(shape, dtype)


def call(kernel, outs, args, scratch=(), smem=(), stay=(), leave=(), flops=0, limit=24):
    nbytes = sum(a.size * a.dtype.itemsize for a in args)
    return pl.pallas_call(
        kernel,
        out_shape=outs,
        in_specs=[
            IN_SMEM if k in smem else IN_HBM if k in stay else IN_VMEM for k in range(len(args))
        ],
        out_specs=[IN_HBM if k in leave else IN_VMEM for k in range(len(outs))]
        if isinstance(outs, list)
        else IN_VMEM,
        scratch_shapes=scratch,
        compiler_params=pltpu.CompilerParams(vmem_limit_bytes=limit << 20),
        cost_estimate=pl.CostEstimate(flops=flops, transcendentals=0, bytes_accessed=nbytes),
    )(*args)


def place(stride):
    dom = lax.axis_index("dom")
    core = lax.axis_index("edge")
    return core, lax.rem(dom, 2), lax.rem(lax.div(dom, stride), 2)


def mm(a, b):
    return jnp.dot(a, b, preferred_element_type=F32)


def column(row):
    return jnp.transpose(jnp.broadcast_to(row, (HALF, HALF)))


def one_hot_rows(row, width):
    col = column(row)
    lane = lax.broadcasted_iota(jnp.int32, (HALF, HALF), 1)
    parts = [jnp.where(col == lane + k, 1.0, 0.0) for k in range(0, width, HALF)]
    return jnp.concatenate(parts, axis=1).astype(BF16)


def dyn(start, size, unit=None):
    return pl.ds(pl.multiple_of(start, unit or size), size)


def faces(stride):
    core, par_d, par_s = place(stride)
    par = jnp.where(core == 0, par_d, par_s)
    return 2 * core + 1 - par, 2 * core + par


def face_hits(stride, lists):
    return [one_hot_rows(lists[0, pl.ds(face, 1), :], TILE) for face in faces(stride)]


def pick_kernel(stride, own_ref, peer_ref, list_own, list_peer, far, near):
    for n, (lists, nodes) in enumerate(((list_own, own_ref), (list_peer, peer_ref))):
        for rows, out_rows in zip(face_hits(stride, lists), (far, near)):
            out_rows[n * HALF : (n + 1) * HALF, :] = mm(rows, nodes[...]).astype(BF16)


def load_kernel(count, *refs):
    hbm, vmem, sems = refs[:count], refs[count:-1], refs[-1]
    copies = [
        pltpu.make_async_copy(src if len(src.shape) == len(dst.shape) else src.at[0], dst, sems.at[k])
        for k, (src, dst) in enumerate(zip(hbm, vmem))
    ]
    for copy in copies:
        copy.start()
    for copy in copies:
        copy.wait()


def in_hbm(arrays):
    return [pltpu.with_memory_space_constraint(a, pltpu.HBM) for a in arrays]


def columns(stride, send_ref, recv_ref, cols, at):
    _, par_d, par_s = place(stride)
    v = send_ref[:, at]
    j = v - 2 * TILE
    owner = lax.shift_right_arithmetic(j, 9)
    face = lax.shift_right_arithmetic(j, 7) & 3
    core = lax.shift_right_arithmetic(face, 1)
    par = jnp.where(core == 0, par_d, par_s)
    near = (face & 1) != par
    tile = jnp.where(near, 2, 4) + core
    at_tile = ((owner ^ core) & 1) * HALF + (j & (HALF - 1))
    spot = jnp.where(v < 2 * TILE, v, tile * TILE + at_tile)
    cols[0, at, :] = column(spot).astype(I16)
    cols[1, at, :] = column(recv_ref[:, at]).astype(I16)


def hits(spots, first, tiles):
    one = jnp.ones(spots.shape, BF16)
    zero = jnp.zeros(spots.shape, BF16)
    lane = lax.broadcasted_iota(jnp.int32, spots.shape, 1)
    parts = [
        jnp.where(spots == (lane + (first * TILE + k * HALF)).astype(I16), one, zero)
        for k in range(2 * tiles)
    ]
    return jnp.concatenate(parts, axis=1)


def project(parts, w1_ref, table):
    for k in (1, 2):
        for start, size, ref in parts:
            table[dyn((2 * k - 2) * TILE + start, size, TILE), :] = mm(
                ref[...], w1_ref[k * TILE : (k + 1) * TILE, :]
            ).astype(BF16)


def local_block(layer, at, cols, b1_ref, table, pre_ref, edges=None):
    acc = 0.0 if edges is None else mm(*edges)
    acc = acc + mm(hits(cols[0, at, :], 0, 2), table[0 : 2 * TILE, :])
    acc = acc + mm(hits(cols[1, at, :], 0, 2), table[2 * TILE :, :])
    pre_ref[at, :] = acc + b1_ref[layer : layer + 1, :]


def first_kernel(stride, loads, send_ref, recv_ref, own_ref, peer_ref, w1_ref, b1_ref, *refs):
    hbm, (pre_ref, cols), refs = refs[:loads], refs[loads : loads + 2], refs[loads + 2 :]
    vmem, (table, sems) = refs[:loads], refs[loads:]
    ends = [(hbm[0].at[1], vmem[0])] + list(zip(hbm[1:], vmem[1:]))
    copies = [pltpu.make_async_copy(*pair, sems.at[k]) for k, pair in enumerate(ends)]
    for copy in copies:
        copy.start()
    blocks = [pl.ds(start, LOCAL_ROWS) for start in range(0, pre_ref.shape[0], LOCAL_ROWS)]
    core = lax.axis_index("edge")
    parts = ((core * TILE, TILE, own_ref), ((1 - core) * TILE, TILE, peer_ref))

    def make(k):
        for start in range(k * LOCAL_ROWS, (k + 1) * LOCAL_ROWS, HALF):
            columns(stride, send_ref, recv_ref, cols, pl.ds(start, HALF))

    make(0)
    project(parts, w1_ref, table)
    for k, at in enumerate(blocks):
        if k + 1 < len(blocks):
            make(k + 1)
        local_block(0, at, cols, b1_ref, table, pre_ref)
    for copy in copies:
        copy.wait()


def local_kernel(layer, edge_ref, cols, dom_ref, w1_ref, b1_ref, pre_ref, table):
    project(((0, 2 * TILE, dom_ref),), w1_ref, table)

    def step(k, carry):
        at = dyn(k * LOCAL_ROWS, LOCAL_ROWS)
        edges = (edge_ref[at, :], w1_ref[0:TILE, :])
        local_block(layer, at, cols, b1_ref, table, pre_ref, edges)
        return carry

    lax.fori_loop(0, edge_ref.shape[0] // LOCAL_ROWS, step, 0)


def tile_kernel(first, peer, pre_ref, cols, w1_ref, rows_ref, *refs):
    out_ref = refs[-1]
    core = lax.axis_index("edge")
    tile = first + (1 - core if peer else core)
    table = mm(rows_ref[...], w1_ref[TILE : 2 * TILE, :]).astype(BF16)
    half = pre_ref.shape[0] // 2

    def step(k, carry):
        at = dyn(k * half, half)
        acc = pre_ref[at, :] + mm(hits(cols[0, at, :], tile, 1), table)
        if len(refs) == 2:
            acc = acc + mm(refs[0][at, :], w1_ref[0:TILE, :])
        out_ref[at, :] = acc
        return carry

    lax.fori_loop(0, 2, step, 0)


def edge_kernel(
    layer, split, live_ref, pre_ref, cols, recv_ref, edge_ref, w1_ref, w2_ref, gain_ref, peer, out_ref, *refs
):
    if split:
        keep_ref, give_ref, table, raw, msgs, sums = refs
    else:
        part_ref, table, raw, msgs, sums = refs
    tile = 5 - lax.axis_index("edge")
    table[...] = mm(peer[...], w1_ref[TILE : 2 * TILE, :]).astype(BF16)
    gain = gain_ref[layer : layer + 1, :]
    live = live_ref[0, 0]
    count = edge_ref.shape[0] // ROWS

    def gather(at):
        acc = pre_ref[at, :] + mm(hits(cols[0, at, :], tile, 1), table[...])
        hidden = jnp.maximum(acc.astype(BF16), jnp.asarray(0, BF16))
        raw[at, :] = mm(hidden, w2_ref[layer])

    def norm(at, start):
        values = raw[at, :]
        center = values - jnp.mean(values, axis=-1, keepdims=True)
        spread = jnp.mean(center * center, axis=-1, keepdims=True)
        scale = lax.rsqrt(spread + eps_norm)
        row = lax.broadcasted_iota(jnp.int32, scale.shape, 0) + start
        scale = jnp.where(row < live, scale, 0.0)
        message = (center * scale * gain).astype(BF16)
        msgs[at, :] = message
        out_ref[at, :] = edge_ref[at, :] + message

    def segment(at, new):
        shape = (2 * TILE, ROWS)
        spot = lax.broadcasted_iota(jnp.int32, shape, 0).astype(I16)
        here = jnp.broadcast_to(recv_ref[:, at].astype(I16), shape)
        hot = jnp.where(here == spot, jnp.ones(shape, BF16), jnp.zeros(shape, BF16))
        part = mm(hot, msgs[at, :])
        sums[...] = part if new else sums[...] + part

    for k in range(count + 2):
        if k >= 2:
            segment(pl.ds((k - 2) * ROWS, ROWS), k == 2)
        if 1 <= k <= count:
            norm(pl.ds((k - 1) * ROWS, ROWS), (k - 1) * ROWS)
        if k < count:
            gather(pl.ds(k * ROWS, ROWS))
    if split:
        core = lax.axis_index("edge")
        keep_ref[...] = sums[dyn(core * TILE, TILE), :].astype(BF16)
        give_ref[...] = sums[dyn((1 - core) * TILE, TILE), :].astype(BF16)
    else:
        part_ref[...] = sums[...].astype(BF16)


def updated(layer, nodes, first, second, w1_ref, b1_ref, w2_ref, gain_ref):
    total = (first.astype(F32) + second.astype(F32)).astype(BF16)
    pre = mm(nodes, w1_ref[layer, 0:TILE, :]) + mm(total, w1_ref[layer, TILE:, :])
    hidden = jnp.maximum(pre + b1_ref[layer : layer + 1, :], 0.0).astype(BF16)
    step = layer_norm(mm(hidden, w2_ref[layer]), gain_ref[layer : layer + 1, :])
    return (nodes.astype(F32) + step).astype(BF16)


def node_kernel(
    stride, layer, own_ref, peer_ref, first, second, list_own, list_peer, w1, b1, w2, gain, out, far, near
):
    core = lax.axis_index("edge")
    nodes = []
    for owner, ref in ((core, own_ref), (1 - core, peer_ref)):
        at = dyn(owner * TILE, TILE)
        nodes.append(updated(layer, ref[...], first[at, :], second[at, :], w1, b1, w2, gain))
        out[at, :] = nodes[-1]
    for face, ref in zip(faces(stride), (far, near)):
        for n, lists in enumerate((list_own, list_peer)):
            rows = one_hot_rows(lists[0, pl.ds(face, 1), :], TILE)
            ref[n * HALF : (n + 1) * HALF, :] = mm(rows, nodes[n]).astype(BF16)


def last_kernel(layer, nodes_ref, first, second, w1, b1, w2, gain, out):
    core = lax.axis_index("edge")
    nodes = nodes_ref[dyn(core * TILE, TILE), :]
    out[...] = updated(layer, nodes, first[...], second[...], w1, b1, w2, gain)


def met(count, stride, odd):
    pairs = []
    for dom in range(count):
        ahead = (dom // stride) % 2 == odd
        pairs.append((dom + (stride if ahead else -stride)) % count)
    return pairs


def swapped(value):
    return lax.ppermute(value, "edge", [(0, 1), (1, 0)])


def fast_shards(
    node_lat,
    edge_lat,
    senders,
    receivers,
    live_edges,
    send_rows,
    edge_w1,
    edge_b1,
    edge_w2,
    edge_gain,
    node_w1,
    node_b1,
    node_w2,
    node_gain,
):
    domains = lax.axis_size("dom")
    stride = domains // 4
    edges, width = edge_lat.shape
    nodes = node_lat.shape[0]
    near_d, far_d = met(domains, 1, 0), met(domains, 1, 1)
    near_s, far_s = met(domains, stride, 0), met(domains, stride, 1)

    def sent_by_core(value, partner_d, partner_s):
        pairs = [(2 * d, 2 * p) for d, p in enumerate(partner_d)]
        pairs += [(2 * d + 1, 2 * p + 1) for d, p in enumerate(partner_s)]
        return lax.ppermute(value, ("dom", "edge"), pairs)

    table = pltpu.VMEM((TILE, width), BF16)
    messages = pltpu.VMEM((edges, width), BF16)
    pre_shape = shaped((edges, width), F32)
    rows_out = shaped((TILE, width), BF16)
    pass_flops = 2 * edges * TILE * width

    peer_nodes = swapped(node_lat)
    peer_lists = swapped(send_rows)
    send_at, recv_at = senders[None], receivers[None]
    first = (node_lat, send_rows, send_at, recv_at, edge_b1, edge_w1)
    node_lat, send_rows, send_at, recv_at, edge_b1, first_w1 = call(
        functools.partial(load_kernel, len(first)),
        [shaped(a.shape, a.dtype) for a in first[:-1]] + [shaped(edge_w1.shape[1:], BF16)],
        in_hbm(first),
        scratch=[pltpu.SemaphoreType.DMA((len(first),))],
        stay=range(len(first)),
    )
    far_rows, near_rows = call(
        functools.partial(pick_kernel, stride),
        [rows_out, rows_out],
        (node_lat, peer_nodes, send_rows, peer_lists),
    )
    for layer in range(LAYERS):
        last = layer == LAYERS - 1
        near = sent_by_core(near_rows, near_d, near_s)
        far = sent_by_core(far_rows, far_d, far_s)
        if layer == 0:
            loads = (edge_w1, edge_lat, edge_w2, node_w1, node_w2, edge_gain, node_b1, node_gain)
            pre, cols, next_w1, edge_rows, edge_w2, node_w1, node_w2, edge_gain, node_b1, node_gain = call(
                functools.partial(first_kernel, stride, len(loads)),
                [pre_shape, shaped((2, edges, HALF), I16)]
                + [shaped(a.shape[1:] if a is edge_w1 else a.shape, a.dtype) for a in loads],
                (send_at, recv_at, node_lat, peer_nodes, first_w1, edge_b1, *in_hbm(loads)),
                scratch=[
                    pltpu.VMEM((4 * TILE, width), BF16),
                    pltpu.SemaphoreType.DMA((len(loads),)),
                ],
                stay=range(6, 6 + len(loads)),
                flops=5 * pass_flops,
            )
        else:
            pre = call(
                functools.partial(local_kernel, layer),
                pre_shape,
                (edge_rows, cols, all_nodes, next_w1, edge_b1),
                scratch=[pltpu.VMEM((4 * TILE, width), BF16)],
                flops=5 * pass_flops,
            )
        w1 = next_w1 if layer else first_w1

        def add(first, peer, pre, rows, *edges):
            return call(
                functools.partial(tile_kernel, first, peer),
                pre_shape,
                (pre, cols, w1, rows, *edges),
                flops=pass_flops,
            )

        pre, near, live_edges = lax.optimization_barrier((pre, near, live_edges))
        near_other = swapped(near)
        pre = add(2, False, pre, near, *(() if layer else (edge_rows,)))
        pre = add(2, True, pre, near_other)
        pre, far = lax.optimization_barrier((pre, far))
        far_other = swapped(far)
        pre = add(4, False, pre, far)
        if last:
            outs = [shaped((nodes, width), BF16)] * 2
        else:
            outs = [shaped((2 * nodes, width), BF16)]
        edge_rows, *partial = call(
            functools.partial(edge_kernel, layer, last),
            [shaped((edges, width), BF16)] + outs,
            (live_edges, pre, cols, recv_at, edge_rows, w1, edge_w2, edge_gain, far_other),
            scratch=[
                table,
                pltpu.VMEM((edges, width), F32),
                messages,
                pltpu.VMEM((2 * nodes, width), F32),
            ],
            smem=(0,),
            flops=5 * pass_flops,
        )
        other = swapped(partial[-1])
        weights = (node_w1, node_b1, node_w2, node_gain)
        if last:
            (edge_out,) = call(
                functools.partial(load_kernel, 1),
                [shaped((edges, width), BF16)],
                (edge_rows,),
                scratch=[pltpu.SemaphoreType.DMA((1,))],
                leave=(0,),
            )
            out = call(
                functools.partial(last_kernel, layer),
                shaped((nodes, width), BF16),
                (all_nodes, partial[0], other, *weights),
            )
        else:
            all_nodes, far_rows, near_rows = call(
                functools.partial(node_kernel, stride, layer),
                [shaped((2 * nodes, width), BF16), rows_out, rows_out],
                (node_lat, peer_nodes, partial[0], other, send_rows, peer_lists, *weights),
            )
    return out, edge_out


def shards(*args):
    node_lat, edge_lat, _, _, _, send_rows = args[:6]
    domains = lax.axis_size("dom")
    fits = (
        lax.axis_size("edge") == 2
        and domains % 8 == 0
        and node_lat.shape == (TILE, TILE)
        and edge_lat.shape[0] % LOCAL_ROWS == 0
        and send_rows.shape[1:] == (4, HALF)
        and args[6].shape == (LAYERS, 3 * TILE, TILE)
    )
    return (fast_shards if fits else general_shards)(*args)


def general_shards(
    node_lat,
    edge_lat,
    senders,
    receivers,
    live_edges,
    send_rows,
    edge_w1,
    edge_b1,
    edge_w2,
    edge_gain,
    node_w1,
    node_b1,
    node_w2,
    node_gain,
):
    rank_count = lax.axis_size("edge")
    domains = lax.axis_size("dom")
    stride = domains // 4
    offsets = (1, -1, stride, -stride)
    node_count = node_lat.shape[0]
    face_count = send_rows.shape[1]
    latent = node_lat.shape[1]
    live_rows = lax.broadcasted_iota(jnp.int32, (edge_lat.shape[0],), 0) < live_edges[0, 0]
    lists_all = None
    lists_all = lax.all_gather(send_rows, "edge", axis=0, tiled=True)
    lists_all = lists_all + (jnp.arange(rank_count, dtype=jnp.int32) * node_count)[:, None, None]
    owned_rows = node_lat
    edge_rows = edge_lat
    for layer_index in range(LAYERS):
        received = []
        domain_rows = lax.all_gather(owned_rows, "edge", axis=0, tiled=True)
        face_rows = jnp.take(domain_rows, lists_all, axis=0)
        for face_index in range(face_count):
            received.append(passed_along(face_rows[:, face_index], "dom", offsets[face_index]))
        halo_all = jnp.stack(received, axis=1).reshape(-1, latent)
        node_table = jnp.concatenate([domain_rows, halo_all], axis=0)
        sender_rows = jnp.take(node_table, senders, axis=0)
        receiver_rows = jnp.take(domain_rows, receivers, axis=0)
        edge_rows, messages = edge_update(
            edge_rows,
            sender_rows,
            receiver_rows,
            edge_w1[layer_index],
            edge_b1[layer_index],
            edge_w2[layer_index],
            edge_gain[layer_index],
            live_rows,
        )
        summed = lax.psum_scatter(
            jax.ops.segment_sum(
                messages, receivers, num_segments=lax.axis_size("edge") * node_count
            ).astype(jnp.bfloat16),
            "edge",
            scatter_dimension=0,
            tiled=True,
        )
        owned_rows = node_update(
            owned_rows,
            summed,
            node_w1[layer_index],
            node_b1[layer_index],
            node_w2[layer_index],
            node_gain[layer_index],
        )
    return (owned_rows, edge_rows)


def solution(mesh):
    in_specs = (
        P(("dom", "edge"), None),
        P(("dom", "edge"), None),
        P(("dom", "edge")),
        P(("dom", "edge")),
        P("dom", "edge"),
        P(("dom", "edge"), None, None),
        P(),
        P(),
        P(),
        P(),
        P(),
        P(),
        P(),
        P(),
    )
    out_specs = (P(("dom", "edge"), None), P(("dom", "edge"), None))
    return jax.shard_map(shards, mesh=mesh, in_specs=in_specs, out_specs=out_specs, check_vma=False)
```

```python
import functools

import jax
import jax.numpy as jnp
from jax import lax
from jax.experimental import pallas as pl
from jax.experimental.pallas import tpu as pltpu
from jax.sharding import PartitionSpec as P

LAYERS = 2


eps_norm = 1e-05


def passed_along(value, axis, steps):
    count = lax.axis_size(axis)
    pairs = [(source, (source + steps) % count) for source in range(count)]
    return lax.ppermute(value, axis, pairs)


def layer_norm(values, norm_gain):
    center = values - jnp.mean(values, axis=-1, keepdims=True)
    spread = jnp.mean(center * center, axis=-1, keepdims=True)
    return center * lax.rsqrt(spread + eps_norm) * norm_gain


def edge_update(
    edge_rows, sender_rows, receiver_rows, weight_in, bias_in, weight_out, norm_gain, live_rows
):
    feature_width = edge_rows.shape[1]
    pre_act = jnp.dot(edge_rows, weight_in[:feature_width], preferred_element_type=jnp.float32)
    pre_act = pre_act + jnp.dot(
        sender_rows,
        weight_in[feature_width : 2 * feature_width],
        preferred_element_type=jnp.float32,
    )
    pre_act = pre_act + jnp.dot(
        receiver_rows, weight_in[2 * feature_width :], preferred_element_type=jnp.float32
    )
    hidden_rows = jax.nn.relu(pre_act + bias_in).astype(jnp.bfloat16)
    messages = layer_norm(
        jnp.dot(hidden_rows, weight_out, preferred_element_type=jnp.float32), norm_gain
    )
    messages = jnp.where(live_rows[:, None], messages, jnp.float32(0.0))
    return ((edge_rows.astype(jnp.float32) + messages).astype(jnp.bfloat16), messages)


def node_update(node_rows, aggregate, weight_in, bias_in, weight_out, norm_gain):
    feature_width = node_rows.shape[1]
    pre_act = jnp.dot(node_rows, weight_in[:feature_width], preferred_element_type=jnp.float32)
    pre_act = pre_act + jnp.dot(
        aggregate, weight_in[feature_width:], preferred_element_type=jnp.float32
    )
    hidden_rows = jax.nn.relu(pre_act + bias_in).astype(jnp.bfloat16)
    update = layer_norm(
        jnp.dot(hidden_rows, weight_out, preferred_element_type=jnp.float32), norm_gain
    )
    return (node_rows.astype(jnp.float32) + update).astype(jnp.bfloat16)


F32 = jnp.float32
BF16 = jnp.bfloat16
TILE = 256
HALF = 128
ROWS = 512
LOCAL_ROWS = 1024
I16 = jnp.int16
IN_VMEM = pl.BlockSpec(memory_space=pltpu.VMEM)
IN_SMEM = pl.BlockSpec(memory_space=pltpu.SMEM)
IN_HBM = pl.BlockSpec(memory_space=pltpu.HBM)


def shaped(shape, dtype):
    return jax.ShapeDtypeStruct(shape, dtype)


def call(kernel, outs, args, scratch=(), smem=(), stay=(), leave=(), flops=0, limit=24):
    nbytes = sum(a.size * a.dtype.itemsize for a in args)
    return pl.pallas_call(
        kernel,
        out_shape=outs,
        in_specs=[
            IN_SMEM if k in smem else IN_HBM if k in stay else IN_VMEM for k in range(len(args))
        ],
        out_specs=[IN_HBM if k in leave else IN_VMEM for k in range(len(outs))]
        if isinstance(outs, list)
        else IN_VMEM,
        scratch_shapes=scratch,
        compiler_params=pltpu.CompilerParams(vmem_limit_bytes=limit << 20),
        cost_estimate=pl.CostEstimate(flops=flops, transcendentals=0, bytes_accessed=nbytes),
    )(*args)


def place(stride):
    dom = lax.axis_index("dom")
    core = lax.axis_index("edge")
    return core, lax.rem(dom, 2), lax.rem(lax.div(dom, stride), 2)


def mm(a, b):
    return jnp.dot(a, b, preferred_element_type=F32)


def column(row):
    return jnp.transpose(jnp.broadcast_to(row, (HALF, HALF)))


def one_hot_rows(row, width):
    col = column(row)
    lane = lax.broadcasted_iota(jnp.int32, (HALF, HALF), 1)
    parts = [jnp.where(col == lane + k, 1.0, 0.0) for k in range(0, width, HALF)]
    return jnp.concatenate(parts, axis=1).astype(BF16)


def dyn(start, size, unit=None):
    return pl.ds(pl.multiple_of(start, unit or size), size)


def faces(stride):
    core, par_d, par_s = place(stride)
    par = jnp.where(core == 0, par_d, par_s)
    return 2 * core + 1 - par, 2 * core + par


def face_hits(stride, lists):
    return [one_hot_rows(lists[0, pl.ds(face, 1), :], TILE) for face in faces(stride)]


def pick_kernel(stride, own_ref, peer_ref, list_own, list_peer, far, near, hot):
    for n, (lists, nodes) in enumerate(((list_own, own_ref), (list_peer, peer_ref))):
        for k, (rows, out_rows) in enumerate(zip(face_hits(stride, lists), (far, near))):
            hot[2 * n + k] = rows
            out_rows[n * HALF : (n + 1) * HALF, :] = mm(rows, nodes[...]).astype(BF16)


def load_kernel(count, *refs):
    hbm, vmem, sems = refs[:count], refs[count:-1], refs[-1]
    copies = [
        pltpu.make_async_copy(src if len(src.shape) == len(dst.shape) else src.at[0], dst, sems.at[k])
        for k, (src, dst) in enumerate(zip(hbm, vmem))
    ]
    for copy in copies:
        copy.start()
    for copy in copies:
        copy.wait()


def store_kernel(rows, vmem, hbm, sems):
    blocks = [pl.ds(start, rows) for start in range(0, hbm.shape[0], rows)]
    copies = [
        pltpu.make_async_copy(vmem.at[at, :], hbm.at[at, :], sems.at[k])
        for k, at in enumerate(blocks)
    ]
    for copy in copies:
        copy.start()
    for copy in copies:
        copy.wait()


def in_hbm(arrays):
    return [pltpu.with_memory_space_constraint(a, pltpu.HBM) for a in arrays]


def columns(stride, send_ref, recv_ref, cols, at):
    _, par_d, par_s = place(stride)
    v = send_ref[:, at]
    j = v - 2 * TILE
    owner = lax.shift_right_arithmetic(j, 9)
    face = lax.shift_right_arithmetic(j, 7) & 3
    core = lax.shift_right_arithmetic(face, 1)
    par = jnp.where(core == 0, par_d, par_s)
    near = (face & 1) != par
    tile = jnp.where(near, 2, 4) + core
    at_tile = ((owner ^ core) & 1) * HALF + (j & (HALF - 1))
    spot = jnp.where(v < 2 * TILE, v, tile * TILE + at_tile)
    cols[0, at, :] = column(spot).astype(I16)
    cols[1, at, :] = column(recv_ref[:, at]).astype(I16)


def hits(spots, first, tiles):
    one = jnp.ones(spots.shape, BF16)
    zero = jnp.zeros(spots.shape, BF16)
    lane = lax.broadcasted_iota(jnp.int32, spots.shape, 1)
    parts = [
        jnp.where(spots == (lane + (first * TILE + k * HALF)).astype(I16), one, zero)
        for k in range(2 * tiles)
    ]
    return jnp.concatenate(parts, axis=1)


def project(parts, w1_ref, table):
    for k in (1, 2):
        for start, size, ref in parts:
            table[dyn((2 * k - 2) * TILE + start, size, TILE), :] = mm(
                ref[...], w1_ref[k * TILE : (k + 1) * TILE, :]
            ).astype(BF16)


def local_block(layer, at, cols, b1_ref, table, pre_ref, edges=None):
    acc = 0.0 if edges is None else mm(*edges)
    acc = acc + mm(hits(cols[0, at, :], 0, 2), table[0 : 2 * TILE, :])
    acc = acc + mm(hits(cols[1, at, :], 0, 2), table[2 * TILE :, :])
    pre_ref[at, :] = acc + b1_ref[layer : layer + 1, :]


def first_kernel(stride, loads, send_ref, recv_ref, own_ref, peer_ref, w1_ref, b1_ref, *refs):
    hbm, (pre_ref, cols), refs = refs[:loads], refs[loads : loads + 2], refs[loads + 2 :]
    vmem, (table, sems) = refs[:loads], refs[loads:]
    ends = [(hbm[0].at[1], vmem[0])] + list(zip(hbm[1:], vmem[1:]))
    copies = [pltpu.make_async_copy(*pair, sems.at[k]) for k, pair in enumerate(ends)]
    for copy in copies:
        copy.start()
    blocks = [pl.ds(start, LOCAL_ROWS) for start in range(0, pre_ref.shape[0], LOCAL_ROWS)]
    core = lax.axis_index("edge")
    parts = ((core * TILE, TILE, own_ref), ((1 - core) * TILE, TILE, peer_ref))

    def make(k):
        for start in range(k * LOCAL_ROWS, (k + 1) * LOCAL_ROWS, HALF):
            columns(stride, send_ref, recv_ref, cols, pl.ds(start, HALF))

    make(0)
    project(parts, w1_ref, table)
    for k, at in enumerate(blocks):
        if k + 1 < len(blocks):
            make(k + 1)
        local_block(0, at, cols, b1_ref, table, pre_ref)
    for copy in copies:
        copy.wait()


def local_kernel(layer, edge_ref, cols, dom_ref, w1_ref, b1_ref, pre_ref, table):
    project(((0, 2 * TILE, dom_ref),), w1_ref, table)

    def step(k, carry):
        at = dyn(k * LOCAL_ROWS, LOCAL_ROWS)
        edges = (edge_ref[at, :], w1_ref[0:TILE, :])
        local_block(layer, at, cols, b1_ref, table, pre_ref, edges)
        return carry

    lax.fori_loop(0, edge_ref.shape[0] // LOCAL_ROWS, step, 0)


def tile_kernel(first, peer, pre_ref, cols, w1_ref, rows_ref, *refs):
    out_ref = refs[-1]
    core = lax.axis_index("edge")
    tile = first + (1 - core if peer else core)
    table = mm(rows_ref[...], w1_ref[TILE : 2 * TILE, :]).astype(BF16)
    half = pre_ref.shape[0] // 2

    def step(k, carry):
        at = dyn(k * half, half)
        acc = pre_ref[at, :] + mm(hits(cols[0, at, :], tile, 1), table)
        if len(refs) == 2:
            acc = acc + mm(refs[0][at, :], w1_ref[0:TILE, :])
        out_ref[at, :] = acc
        return carry

    lax.fori_loop(0, 2, step, 0)


def edge_kernel(
    layer, split, live_ref, pre_ref, cols, recv_ref, edge_ref, w1_ref, w2_ref, gain_ref, peer, out_ref, *refs
):
    if split:
        keep_ref, give_ref, table, raw, msgs, sums = refs
    else:
        part_ref, table, raw, msgs, sums = refs
    tile = 5 - lax.axis_index("edge")
    table[...] = mm(peer[...], w1_ref[TILE : 2 * TILE, :]).astype(BF16)
    gain = gain_ref[layer : layer + 1, :]
    live = live_ref[0, 0]
    count = edge_ref.shape[0] // ROWS

    def gather(at):
        acc = pre_ref[at, :] + mm(hits(cols[0, at, :], tile, 1), table[...])
        hidden = jnp.maximum(acc.astype(BF16), jnp.asarray(0, BF16))
        raw[at, :] = mm(hidden, w2_ref[layer])

    def norm(at, start):
        values = raw[at, :]
        center = values - jnp.mean(values, axis=-1, keepdims=True)
        spread = jnp.mean(center * center, axis=-1, keepdims=True)
        scale = lax.rsqrt(spread + eps_norm)
        row = lax.broadcasted_iota(jnp.int32, scale.shape, 0) + start
        scale = jnp.where(row < live, scale, 0.0)
        message = (center * scale * gain).astype(BF16)
        msgs[at, :] = message
        out_ref[at, :] = edge_ref[at, :] + message

    def segment(at, new):
        shape = (2 * TILE, ROWS)
        spot = lax.broadcasted_iota(jnp.int32, shape, 0).astype(I16)
        here = jnp.broadcast_to(recv_ref[:, at].astype(I16), shape)
        hot = jnp.where(here == spot, jnp.ones(shape, BF16), jnp.zeros(shape, BF16))
        part = mm(hot, msgs[at, :])
        sums[...] = part if new else sums[...] + part

    for k in range(count + 2):
        if k >= 2:
            segment(pl.ds((k - 2) * ROWS, ROWS), k == 2)
        if 1 <= k <= count:
            norm(pl.ds((k - 1) * ROWS, ROWS), (k - 1) * ROWS)
        if k < count:
            gather(pl.ds(k * ROWS, ROWS))
    if split:
        core = lax.axis_index("edge")
        keep_ref[...] = sums[dyn(core * TILE, TILE), :].astype(BF16)
        give_ref[...] = sums[dyn((1 - core) * TILE, TILE), :].astype(BF16)
    else:
        part_ref[...] = sums[...].astype(BF16)


def updated(layer, nodes, first, second, w1_ref, b1_ref, w2_ref, gain_ref):
    total = (first.astype(F32) + second.astype(F32)).astype(BF16)
    pre = mm(nodes, w1_ref[layer, 0:TILE, :]) + mm(total, w1_ref[layer, TILE:, :])
    hidden = jnp.maximum(pre + b1_ref[layer : layer + 1, :], 0.0).astype(BF16)
    step = layer_norm(mm(hidden, w2_ref[layer]), gain_ref[layer : layer + 1, :])
    return (nodes.astype(F32) + step).astype(BF16)


def node_kernel(layer, own_ref, peer_ref, first, second, hot, w1, b1, w2, gain, out, far, near):
    core = lax.axis_index("edge")
    nodes = []
    for owner, ref in ((core, own_ref), (1 - core, peer_ref)):
        at = dyn(owner * TILE, TILE)
        nodes.append(updated(layer, ref[...], first[at, :], second[at, :], w1, b1, w2, gain))
        out[at, :] = nodes[-1]
    for n in range(2):
        for k, ref in enumerate((far, near)):
            ref[n * HALF : (n + 1) * HALF, :] = mm(hot[2 * n + k], nodes[n]).astype(BF16)


def last_kernel(layer, nodes_ref, first, second, w1, b1, w2, gain, out):
    core = lax.axis_index("edge")
    nodes = nodes_ref[dyn(core * TILE, TILE), :]
    out[...] = updated(layer, nodes, first[...], second[...], w1, b1, w2, gain)


def met(count, stride, odd):
    pairs = []
    for dom in range(count):
        ahead = (dom // stride) % 2 == odd
        pairs.append((dom + (stride if ahead else -stride)) % count)
    return pairs


def swapped(value):
    return lax.ppermute(value, "edge", [(0, 1), (1, 0)])


def fast_shards(
    node_lat,
    edge_lat,
    senders,
    receivers,
    live_edges,
    send_rows,
    edge_w1,
    edge_b1,
    edge_w2,
    edge_gain,
    node_w1,
    node_b1,
    node_w2,
    node_gain,
):
    domains = lax.axis_size("dom")
    stride = domains // 4
    edges, width = edge_lat.shape
    nodes = node_lat.shape[0]
    near_d, far_d = met(domains, 1, 0), met(domains, 1, 1)
    near_s, far_s = met(domains, stride, 0), met(domains, stride, 1)

    def sent_by_core(value, partner_d, partner_s):
        pairs = [(2 * d, 2 * p) for d, p in enumerate(partner_d)]
        pairs += [(2 * d + 1, 2 * p + 1) for d, p in enumerate(partner_s)]
        return lax.ppermute(value, ("dom", "edge"), pairs)

    table = pltpu.VMEM((TILE, width), BF16)
    messages = pltpu.VMEM((edges, width), BF16)
    pre_shape = shaped((edges, width), F32)
    rows_out = shaped((TILE, width), BF16)
    pass_flops = 2 * edges * TILE * width

    peer_nodes = swapped(node_lat)
    peer_lists = swapped(send_rows)
    send_at, recv_at = senders[None], receivers[None]
    first = (node_lat, send_rows, send_at, recv_at, edge_b1, edge_w1)
    node_lat, send_rows, send_at, recv_at, edge_b1, first_w1 = call(
        functools.partial(load_kernel, len(first)),
        [shaped(a.shape, a.dtype) for a in first[:-1]] + [shaped(edge_w1.shape[1:], BF16)],
        in_hbm(first),
        scratch=[pltpu.SemaphoreType.DMA((len(first),))],
        stay=range(len(first)),
    )
    far_rows, near_rows, hot = call(
        functools.partial(pick_kernel, stride),
        [rows_out, rows_out, shaped((4, HALF, TILE), BF16)],
        (node_lat, peer_nodes, send_rows, peer_lists),
    )
    for layer in range(LAYERS):
        last = layer == LAYERS - 1
        near = sent_by_core(near_rows, near_d, near_s)
        far = sent_by_core(far_rows, far_d, far_s)
        if layer == 0:
            loads = (edge_w1, edge_lat, edge_w2, node_w1, node_w2, edge_gain, node_b1, node_gain)
            pre, cols, next_w1, edge_rows, edge_w2, node_w1, node_w2, edge_gain, node_b1, node_gain = call(
                functools.partial(first_kernel, stride, len(loads)),
                [pre_shape, shaped((2, edges, HALF), I16)]
                + [shaped(a.shape[1:] if a is edge_w1 else a.shape, a.dtype) for a in loads],
                (send_at, recv_at, node_lat, peer_nodes, first_w1, edge_b1, *in_hbm(loads)),
                scratch=[
                    pltpu.VMEM((4 * TILE, width), BF16),
                    pltpu.SemaphoreType.DMA((len(loads),)),
                ],
                stay=range(6, 6 + len(loads)),
                flops=5 * pass_flops,
            )
        else:
            pre = call(
                functools.partial(local_kernel, layer),
                pre_shape,
                (edge_rows, cols, all_nodes, next_w1, edge_b1),
                scratch=[pltpu.VMEM((4 * TILE, width), BF16)],
                flops=5 * pass_flops,
            )
        w1 = next_w1 if layer else first_w1

        def add(first, peer, pre, rows, *edges):
            return call(
                functools.partial(tile_kernel, first, peer),
                pre_shape,
                (pre, cols, w1, rows, *edges),
                flops=pass_flops,
            )

        pre, near, live_edges = lax.optimization_barrier((pre, near, live_edges))
        near_other = swapped(near)
        pre = add(2, False, pre, near, *(() if layer else (edge_rows,)))
        pre = add(2, True, pre, near_other)
        pre, far = lax.optimization_barrier((pre, far))
        far_other = swapped(far)
        pre = add(4, False, pre, far)
        if last:
            outs = [shaped((nodes, width), BF16)] * 2
        else:
            outs = [shaped((2 * nodes, width), BF16)]
        edge_rows, *partial = call(
            functools.partial(edge_kernel, layer, last),
            [shaped((edges, width), BF16)] + outs,
            (live_edges, pre, cols, recv_at, edge_rows, w1, edge_w2, edge_gain, far_other),
            scratch=[
                table,
                pltpu.VMEM((edges, width), F32),
                messages,
                pltpu.VMEM((2 * nodes, width), F32),
            ],
            smem=(0,),
            flops=5 * pass_flops,
        )
        other = swapped(partial[-1])
        weights = (node_w1, node_b1, node_w2, node_gain)
        if last:
            (edge_out,) = call(
                functools.partial(store_kernel, ROWS),
                [shaped((edges, width), BF16)],
                (edge_rows,),
                scratch=[pltpu.SemaphoreType.DMA((edges // ROWS,))],
                leave=(0,),
            )
            out = call(
                functools.partial(last_kernel, layer),
                shaped((nodes, width), BF16),
                (all_nodes, partial[0], other, *weights),
            )
        else:
            all_nodes, far_rows, near_rows = call(
                functools.partial(node_kernel, layer),
                [shaped((2 * nodes, width), BF16), rows_out, rows_out],
                (node_lat, peer_nodes, partial[0], other, hot, *weights),
            )
    return out, edge_out


def shards(*args):
    node_lat, edge_lat, _, _, _, send_rows = args[:6]
    domains = lax.axis_size("dom")
    fits = (
        lax.axis_size("edge") == 2
        and domains % 8 == 0
        and node_lat.shape == (TILE, TILE)
        and edge_lat.shape[0] % LOCAL_ROWS == 0
        and send_rows.shape[1:] == (4, HALF)
        and args[6].shape == (LAYERS, 3 * TILE, TILE)
    )
    return (fast_shards if fits else general_shards)(*args)


def general_shards(
    node_lat,
    edge_lat,
    senders,
    receivers,
    live_edges,
    send_rows,
    edge_w1,
    edge_b1,
    edge_w2,
    edge_gain,
    node_w1,
    node_b1,
    node_w2,
    node_gain,
):
    rank_count = lax.axis_size("edge")
    domains = lax.axis_size("dom")
    stride = domains // 4
    offsets = (1, -1, stride, -stride)
    node_count = node_lat.shape[0]
    face_count = send_rows.shape[1]
    latent = node_lat.shape[1]
    live_rows = lax.broadcasted_iota(jnp.int32, (edge_lat.shape[0],), 0) < live_edges[0, 0]
    lists_all = None
    lists_all = lax.all_gather(send_rows, "edge", axis=0, tiled=True)
    lists_all = lists_all + (jnp.arange(rank_count, dtype=jnp.int32) * node_count)[:, None, None]
    owned_rows = node_lat
    edge_rows = edge_lat
    for layer_index in range(LAYERS):
        received = []
        domain_rows = lax.all_gather(owned_rows, "edge", axis=0, tiled=True)
        face_rows = jnp.take(domain_rows, lists_all, axis=0)
        for face_index in range(face_count):
            received.append(passed_along(face_rows[:, face_index], "dom", offsets[face_index]))
        halo_all = jnp.stack(received, axis=1).reshape(-1, latent)
        node_table = jnp.concatenate([domain_rows, halo_all], axis=0)
        sender_rows = jnp.take(node_table, senders, axis=0)
        receiver_rows = jnp.take(domain_rows, receivers, axis=0)
        edge_rows, messages = edge_update(
            edge_rows,
            sender_rows,
            receiver_rows,
            edge_w1[layer_index],
            edge_b1[layer_index],
            edge_w2[layer_index],
            edge_gain[layer_index],
            live_rows,
        )
        summed = lax.psum_scatter(
            jax.ops.segment_sum(
                messages, receivers, num_segments=lax.axis_size("edge") * node_count
            ).astype(jnp.bfloat16),
            "edge",
            scatter_dimension=0,
            tiled=True,
        )
        owned_rows = node_update(
            owned_rows,
            summed,
            node_w1[layer_index],
            node_b1[layer_index],
            node_w2[layer_index],
            node_gain[layer_index],
        )
    return (owned_rows, edge_rows)


def solution(mesh):
    in_specs = (
        P(("dom", "edge"), None),
        P(("dom", "edge"), None),
        P(("dom", "edge")),
        P(("dom", "edge")),
        P("dom", "edge"),
        P(("dom", "edge"), None, None),
        P(),
        P(),
        P(),
        P(),
        P(),
        P(),
        P(),
        P(),
    )
    out_specs = (P(("dom", "edge"), None), P(("dom", "edge"), None))
    return jax.shard_map(shards, mesh=mesh, in_specs=in_specs, out_specs=out_specs, check_vma=False)
```

```python
import functools

import jax
import jax.numpy as jnp
from jax import lax
from jax.experimental import pallas as pl
from jax.experimental.pallas import tpu as pltpu
from jax.sharding import PartitionSpec as P

LAYERS = 2


eps_norm = 1e-05


def passed_along(value, axis, steps):
    count = lax.axis_size(axis)
    pairs = [(source, (source + steps) % count) for source in range(count)]
    return lax.ppermute(value, axis, pairs)


def layer_norm(values, norm_gain):
    center = values - jnp.mean(values, axis=-1, keepdims=True)
    spread = jnp.mean(center * center, axis=-1, keepdims=True)
    return center * lax.rsqrt(spread + eps_norm) * norm_gain


def edge_update(
    edge_rows, sender_rows, receiver_rows, weight_in, bias_in, weight_out, norm_gain, live_rows
):
    feature_width = edge_rows.shape[1]
    pre_act = jnp.dot(edge_rows, weight_in[:feature_width], preferred_element_type=jnp.float32)
    pre_act = pre_act + jnp.dot(
        sender_rows,
        weight_in[feature_width : 2 * feature_width],
        preferred_element_type=jnp.float32,
    )
    pre_act = pre_act + jnp.dot(
        receiver_rows, weight_in[2 * feature_width :], preferred_element_type=jnp.float32
    )
    hidden_rows = jax.nn.relu(pre_act + bias_in).astype(jnp.bfloat16)
    messages = layer_norm(
        jnp.dot(hidden_rows, weight_out, preferred_element_type=jnp.float32), norm_gain
    )
    messages = jnp.where(live_rows[:, None], messages, jnp.float32(0.0))
    return ((edge_rows.astype(jnp.float32) + messages).astype(jnp.bfloat16), messages)


def node_update(node_rows, aggregate, weight_in, bias_in, weight_out, norm_gain):
    feature_width = node_rows.shape[1]
    pre_act = jnp.dot(node_rows, weight_in[:feature_width], preferred_element_type=jnp.float32)
    pre_act = pre_act + jnp.dot(
        aggregate, weight_in[feature_width:], preferred_element_type=jnp.float32
    )
    hidden_rows = jax.nn.relu(pre_act + bias_in).astype(jnp.bfloat16)
    update = layer_norm(
        jnp.dot(hidden_rows, weight_out, preferred_element_type=jnp.float32), norm_gain
    )
    return (node_rows.astype(jnp.float32) + update).astype(jnp.bfloat16)


F32 = jnp.float32
BF16 = jnp.bfloat16
TILE = 256
HALF = 128
ROWS = 512
LOCAL_ROWS = 1024
I16 = jnp.int16
IN_VMEM = pl.BlockSpec(memory_space=pltpu.VMEM)
IN_SMEM = pl.BlockSpec(memory_space=pltpu.SMEM)
IN_HBM = pl.BlockSpec(memory_space=pltpu.HBM)


def shaped(shape, dtype):
    return jax.ShapeDtypeStruct(shape, dtype)


def call(kernel, outs, args, scratch=(), smem=(), stay=(), leave=(), aliases=None, flops=0, limit=24):
    nbytes = sum(a.size * a.dtype.itemsize for a in args)
    return pl.pallas_call(
        kernel,
        out_shape=outs,
        in_specs=[
            IN_SMEM if k in smem else IN_HBM if k in stay else IN_VMEM for k in range(len(args))
        ],
        out_specs=[IN_HBM if k in leave else IN_VMEM for k in range(len(outs))]
        if isinstance(outs, list)
        else IN_VMEM,
        scratch_shapes=scratch,
        input_output_aliases=aliases or {},
        compiler_params=pltpu.CompilerParams(vmem_limit_bytes=limit << 20),
        cost_estimate=pl.CostEstimate(flops=flops, transcendentals=0, bytes_accessed=nbytes),
    )(*args)


def place(stride):
    dom = lax.axis_index("dom")
    core = lax.axis_index("edge")
    return core, lax.rem(dom, 2), lax.rem(lax.div(dom, stride), 2)


def mm(a, b):
    return jnp.dot(a, b, preferred_element_type=F32)


def column(row):
    return jnp.transpose(jnp.broadcast_to(row, (HALF, HALF)))


def one_hot_rows(row, width):
    col = column(row)
    lane = lax.broadcasted_iota(jnp.int32, (HALF, HALF), 1)
    parts = [jnp.where(col == lane + k, 1.0, 0.0) for k in range(0, width, HALF)]
    return jnp.concatenate(parts, axis=1).astype(BF16)


def dyn(start, size, unit=None):
    return pl.ds(pl.multiple_of(start, unit or size), size)


def faces(stride):
    core, par_d, par_s = place(stride)
    par = jnp.where(core == 0, par_d, par_s)
    return 2 * core + 1 - par, 2 * core + par


def face_hits(stride, lists):
    return [one_hot_rows(lists[0, pl.ds(face, 1), :], TILE) for face in faces(stride)]


def pick_kernel(stride, own_ref, peer_ref, list_own, list_peer, far, near, hot):
    for n, (lists, nodes) in enumerate(((list_own, own_ref), (list_peer, peer_ref))):
        for k, (rows, out_rows) in enumerate(zip(face_hits(stride, lists), (far, near))):
            hot[2 * n + k] = rows
            out_rows[n * HALF : (n + 1) * HALF, :] = mm(rows, nodes[...]).astype(BF16)


def load_kernel(count, *refs):
    hbm, vmem, sems = refs[:count], refs[count:-1], refs[-1]
    copies = [
        pltpu.make_async_copy(src if len(src.shape) == len(dst.shape) else src.at[0], dst, sems.at[k])
        for k, (src, dst) in enumerate(zip(hbm, vmem))
    ]
    for copy in copies:
        copy.start()
    for copy in copies:
        copy.wait()


def in_hbm(arrays):
    return [pltpu.with_memory_space_constraint(a, pltpu.HBM) for a in arrays]


def columns(stride, send_ref, recv_ref, cols, at):
    _, par_d, par_s = place(stride)
    v = send_ref[:, at]
    j = v - 2 * TILE
    owner = lax.shift_right_arithmetic(j, 9)
    face = lax.shift_right_arithmetic(j, 7) & 3
    core = lax.shift_right_arithmetic(face, 1)
    par = jnp.where(core == 0, par_d, par_s)
    near = (face & 1) != par
    tile = jnp.where(near, 2, 4) + core
    at_tile = ((owner ^ core) & 1) * HALF + (j & (HALF - 1))
    spot = jnp.where(v < 2 * TILE, v, tile * TILE + at_tile)
    cols[0, at, :] = column(spot).astype(I16)
    cols[1, at, :] = column(recv_ref[:, at]).astype(I16)


def hits(spots, first, tiles):
    one = jnp.ones(spots.shape, BF16)
    zero = jnp.zeros(spots.shape, BF16)
    lane = lax.broadcasted_iota(jnp.int32, spots.shape, 1)
    parts = [
        jnp.where(spots == (lane + (first * TILE + k * HALF)).astype(I16), one, zero)
        for k in range(2 * tiles)
    ]
    return jnp.concatenate(parts, axis=1)


def project(parts, w1_ref, table):
    for k in (1, 2):
        for start, size, ref in parts:
            table[dyn((2 * k - 2) * TILE + start, size, TILE), :] = mm(
                ref[...], w1_ref[k * TILE : (k + 1) * TILE, :]
            ).astype(BF16)


def local_block(layer, at, cols, b1_ref, table, pre_ref, edges=None):
    acc = 0.0 if edges is None else mm(*edges)
    acc = acc + mm(hits(cols[0, at, :], 0, 2), table[0 : 2 * TILE, :])
    acc = acc + mm(hits(cols[1, at, :], 0, 2), table[2 * TILE :, :])
    pre_ref[at, :] = acc + b1_ref[layer : layer + 1, :]


def first_kernel(stride, loads, send_ref, recv_ref, own_ref, peer_ref, w1_ref, b1_ref, *refs):
    hbm, (pre_ref, cols), refs = refs[:loads], refs[loads : loads + 2], refs[loads + 2 :]
    vmem, (table, sems) = refs[:loads], refs[loads:]
    ends = [(hbm[0].at[1], vmem[0])] + list(zip(hbm[1:], vmem[1:]))
    copies = [pltpu.make_async_copy(*pair, sems.at[k]) for k, pair in enumerate(ends)]
    for copy in copies:
        copy.start()
    blocks = [pl.ds(start, LOCAL_ROWS) for start in range(0, pre_ref.shape[0], LOCAL_ROWS)]
    core = lax.axis_index("edge")
    parts = ((core * TILE, TILE, own_ref), ((1 - core) * TILE, TILE, peer_ref))

    def make(k):
        for start in range(k * LOCAL_ROWS, (k + 1) * LOCAL_ROWS, HALF):
            columns(stride, send_ref, recv_ref, cols, pl.ds(start, HALF))

    make(0)
    project(parts, w1_ref, table)
    for k, at in enumerate(blocks):
        if k + 1 < len(blocks):
            make(k + 1)
        local_block(0, at, cols, b1_ref, table, pre_ref)
    for copy in copies:
        copy.wait()


def local_kernel(layer, edge_ref, cols, dom_ref, w1_ref, b1_ref, pre_ref, table):
    project(((0, 2 * TILE, dom_ref),), w1_ref, table)

    def step(k, carry):
        at = dyn(k * LOCAL_ROWS, LOCAL_ROWS)
        edges = (edge_ref[at, :], w1_ref[0:TILE, :])
        local_block(layer, at, cols, b1_ref, table, pre_ref, edges)
        return carry

    lax.fori_loop(0, edge_ref.shape[0] // LOCAL_ROWS, step, 0)


def tile_kernel(first, peer, pre_ref, cols, w1_ref, rows_ref, *refs):
    out_ref = refs[-1]
    core = lax.axis_index("edge")
    tile = first + (1 - core if peer else core)
    table = mm(rows_ref[...], w1_ref[TILE : 2 * TILE, :]).astype(BF16)
    half = pre_ref.shape[0] // 2

    def step(k, carry):
        at = dyn(k * half, half)
        acc = pre_ref[at, :] + mm(hits(cols[0, at, :], tile, 1), table)
        if len(refs) == 2:
            acc = acc + mm(refs[0][at, :], w1_ref[0:TILE, :])
        out_ref[at, :] = acc
        return carry

    lax.fori_loop(0, 2, step, 0)


def receiver_hits(recv_ref, at, node, nodes):
    shape = (nodes, ROWS)
    spot = (lax.broadcasted_iota(jnp.int32, shape, 0) + node).astype(I16)
    here = jnp.broadcast_to(recv_ref[:, at].astype(I16), shape)
    return jnp.where(here == spot, jnp.ones(shape, BF16), jnp.zeros(shape, BF16))


def edge_kernel(
    layer, split, live_ref, pre_ref, cols, recv_ref, edge_ref, w1_ref, w2_ref, gain_ref, peer, out_ref, *refs
):
    core = lax.axis_index("edge")
    if split:
        give_ref, msgs, table, raw, sums = refs
        node, nodes = (1 - core) * TILE, TILE
    else:
        node, nodes = 0, 2 * TILE
        part_ref, table, raw, msgs, sums = refs
    tile = 5 - core
    table[...] = mm(peer[...], w1_ref[TILE : 2 * TILE, :]).astype(BF16)
    gain = gain_ref[layer : layer + 1, :]
    live = live_ref[0, 0]
    count = edge_ref.shape[0] // ROWS

    def gather(at):
        acc = pre_ref[at, :] + mm(hits(cols[0, at, :], tile, 1), table[...])
        hidden = jnp.maximum(acc.astype(BF16), jnp.asarray(0, BF16))
        raw[at, :] = mm(hidden, w2_ref[layer])

    def norm(at, start):
        values = raw[at, :]
        center = values - jnp.mean(values, axis=-1, keepdims=True)
        spread = jnp.mean(center * center, axis=-1, keepdims=True)
        scale = lax.rsqrt(spread + eps_norm)
        row = lax.broadcasted_iota(jnp.int32, scale.shape, 0) + start
        scale = jnp.where(row < live, scale, 0.0)
        message = (center * scale * gain).astype(BF16)
        msgs[at, :] = message
        out_ref[at, :] = edge_ref[at, :] + message

    def segment(at, new):
        part = mm(receiver_hits(recv_ref, at, node, nodes), msgs[at, :])
        sums[...] = part if new else sums[...] + part

    for k in range(count + 2):
        if k >= 2:
            segment(pl.ds((k - 2) * ROWS, ROWS), k == 2)
        if 1 <= k <= count:
            norm(pl.ds((k - 1) * ROWS, ROWS), (k - 1) * ROWS)
        if k < count:
            gather(pl.ds(k * ROWS, ROWS))
    (give_ref if split else part_ref)[...] = sums[...].astype(BF16)


def output_copies(edge_ref, hbm, sems, half):
    rows = edge_ref.shape[0] // 2
    blocks = [pl.ds(half * rows + start, ROWS) for start in range(0, rows, ROWS)]
    return [
        pltpu.make_async_copy(edge_ref.at[at, :], hbm.at[at, :], sems.at[k])
        for k, at in enumerate(blocks)
    ]


def keep_kernel(recv_ref, msgs, edge_ref, keep_ref, hbm, sems):
    copies = output_copies(edge_ref, hbm, sems, 0)
    for copy in copies:
        copy.start()
    node = lax.axis_index("edge") * TILE
    total = 0.0
    for start in range(0, edge_ref.shape[0], ROWS):
        at = pl.ds(start, ROWS)
        total = total + mm(receiver_hits(recv_ref, at, node, TILE), msgs[at, :])
    keep_ref[...] = total.astype(BF16)
    for copy in copies:
        copy.wait()


def updated(layer, nodes, first, second, w1_ref, b1_ref, w2_ref, gain_ref):
    total = (first.astype(F32) + second.astype(F32)).astype(BF16)
    pre = mm(nodes, w1_ref[layer, 0:TILE, :]) + mm(total, w1_ref[layer, TILE:, :])
    hidden = jnp.maximum(pre + b1_ref[layer : layer + 1, :], 0.0).astype(BF16)
    step = layer_norm(mm(hidden, w2_ref[layer]), gain_ref[layer : layer + 1, :])
    return (nodes.astype(F32) + step).astype(BF16)


def node_kernel(layer, own_ref, peer_ref, first, second, hot, w1, b1, w2, gain, out, far, near):
    core = lax.axis_index("edge")
    nodes = []
    for owner, ref in ((core, own_ref), (1 - core, peer_ref)):
        at = dyn(owner * TILE, TILE)
        nodes.append(updated(layer, ref[...], first[at, :], second[at, :], w1, b1, w2, gain))
        out[at, :] = nodes[-1]
    for n in range(2):
        for k, ref in enumerate((far, near)):
            ref[n * HALF : (n + 1) * HALF, :] = mm(hot[2 * n + k], nodes[n]).astype(BF16)


def last_kernel(layer, nodes_ref, first, second, edge_ref, _, w1, b1, w2, gain, out, hbm, sems):
    copies = output_copies(edge_ref, hbm, sems, 1)
    for copy in copies:
        copy.start()
    core = lax.axis_index("edge")
    nodes = nodes_ref[dyn(core * TILE, TILE), :]
    out[...] = updated(layer, nodes, first[...], second[...], w1, b1, w2, gain)
    for copy in copies:
        copy.wait()


def met(count, stride, odd):
    pairs = []
    for dom in range(count):
        ahead = (dom // stride) % 2 == odd
        pairs.append((dom + (stride if ahead else -stride)) % count)
    return pairs


def swapped(value):
    return lax.ppermute(value, "edge", [(0, 1), (1, 0)])


def fast_shards(
    node_lat,
    edge_lat,
    senders,
    receivers,
    live_edges,
    send_rows,
    edge_w1,
    edge_b1,
    edge_w2,
    edge_gain,
    node_w1,
    node_b1,
    node_w2,
    node_gain,
):
    domains = lax.axis_size("dom")
    stride = domains // 4
    edges, width = edge_lat.shape
    nodes = node_lat.shape[0]
    near_d, far_d = met(domains, 1, 0), met(domains, 1, 1)
    near_s, far_s = met(domains, stride, 0), met(domains, stride, 1)

    def sent_by_core(value, partner_d, partner_s):
        pairs = [(2 * d, 2 * p) for d, p in enumerate(partner_d)]
        pairs += [(2 * d + 1, 2 * p + 1) for d, p in enumerate(partner_s)]
        return lax.ppermute(value, ("dom", "edge"), pairs)

    table = pltpu.VMEM((TILE, width), BF16)
    messages = pltpu.VMEM((edges, width), BF16)
    pre_shape = shaped((edges, width), F32)
    rows_out = shaped((TILE, width), BF16)
    pass_flops = 2 * edges * TILE * width

    peer_nodes = swapped(node_lat)
    peer_lists = swapped(send_rows)
    send_at, recv_at = senders[None], receivers[None]
    first = (node_lat, send_rows, send_at, recv_at, edge_b1, edge_w1)
    node_lat, send_rows, send_at, recv_at, edge_b1, first_w1 = call(
        functools.partial(load_kernel, len(first)),
        [shaped(a.shape, a.dtype) for a in first[:-1]] + [shaped(edge_w1.shape[1:], BF16)],
        in_hbm(first),
        scratch=[pltpu.SemaphoreType.DMA((len(first),))],
        stay=range(len(first)),
    )
    far_rows, near_rows, hot = call(
        functools.partial(pick_kernel, stride),
        [rows_out, rows_out, shaped((4, HALF, TILE), BF16)],
        (node_lat, peer_nodes, send_rows, peer_lists),
    )
    for layer in range(LAYERS):
        last = layer == LAYERS - 1
        near = sent_by_core(near_rows, near_d, near_s)
        far = sent_by_core(far_rows, far_d, far_s)
        if layer == 0:
            loads = (edge_w1, edge_lat, edge_w2, node_w1, node_w2, edge_gain, node_b1, node_gain)
            pre, cols, next_w1, edge_rows, edge_w2, node_w1, node_w2, edge_gain, node_b1, node_gain = call(
                functools.partial(first_kernel, stride, len(loads)),
                [pre_shape, shaped((2, edges, HALF), I16)]
                + [shaped(a.shape[1:] if a is edge_w1 else a.shape, a.dtype) for a in loads],
                (send_at, recv_at, node_lat, peer_nodes, first_w1, edge_b1, *in_hbm(loads)),
                scratch=[
                    pltpu.VMEM((4 * TILE, width), BF16),
                    pltpu.SemaphoreType.DMA((len(loads),)),
                ],
                stay=range(6, 6 + len(loads)),
                flops=5 * pass_flops,
            )
        else:
            pre = call(
                functools.partial(local_kernel, layer),
                pre_shape,
                (edge_rows, cols, all_nodes, next_w1, edge_b1),
                scratch=[pltpu.VMEM((4 * TILE, width), BF16)],
                flops=5 * pass_flops,
            )
        w1 = next_w1 if layer else first_w1

        def add(first, peer, pre, rows, *edges):
            return call(
                functools.partial(tile_kernel, first, peer),
                pre_shape,
                (pre, cols, w1, rows, *edges),
                flops=pass_flops,
            )

        pre, near, live_edges = lax.optimization_barrier((pre, near, live_edges))
        near_other = swapped(near)
        pre = add(2, False, pre, near, *(() if layer else (edge_rows,)))
        pre = add(2, True, pre, near_other)
        pre, far = lax.optimization_barrier((pre, far))
        far_other = swapped(far)
        pre = add(4, False, pre, far)
        if last:
            outs = [shaped((nodes, width), BF16), shaped((edges, width), BF16)]
        else:
            outs = [shaped((2 * nodes, width), BF16)]
        edge_rows, *partial = call(
            functools.partial(edge_kernel, layer, last),
            [shaped((edges, width), BF16)] + outs,
            (live_edges, pre, cols, recv_at, edge_rows, w1, edge_w2, edge_gain, far_other),
            scratch=[table, pltpu.VMEM((edges, width), F32)]
            + ([pltpu.VMEM((nodes, width), F32)] if last else [messages, pltpu.VMEM((2 * nodes, width), F32)]),
            smem=(0,),
            flops=5 * pass_flops,
        )
        other = swapped(partial[0])
        weights = (node_w1, node_b1, node_w2, node_gain)
        if last:
            sems = [pltpu.SemaphoreType.DMA((edges // ROWS // 2,))]
            edge_out = shaped((edges, width), BF16)
            keep, half_out = call(
                keep_kernel,
                [shaped((nodes, width), BF16), edge_out],
                (recv_at, partial[1], edge_rows),
                scratch=sems,
                leave=(1,),
            )
            out, edge_out = call(
                functools.partial(last_kernel, layer),
                [shaped((nodes, width), BF16), edge_out],
                (all_nodes, keep, other, edge_rows, *in_hbm([half_out]), *weights),
                scratch=sems,
                stay=(4,),
                leave=(1,),
                aliases={4: 1},
            )
        else:
            all_nodes, far_rows, near_rows = call(
                functools.partial(node_kernel, layer),
                [shaped((2 * nodes, width), BF16), rows_out, rows_out],
                (node_lat, peer_nodes, partial[0], other, hot, *weights),
            )
    return out, edge_out


def shards(*args):
    node_lat, edge_lat, _, _, _, send_rows = args[:6]
    domains = lax.axis_size("dom")
    fits = (
        lax.axis_size("edge") == 2
        and domains % 8 == 0
        and node_lat.shape == (TILE, TILE)
        and edge_lat.shape[0] % LOCAL_ROWS == 0
        and send_rows.shape[1:] == (4, HALF)
        and args[6].shape == (LAYERS, 3 * TILE, TILE)
    )
    return (fast_shards if fits else general_shards)(*args)


def general_shards(
    node_lat,
    edge_lat,
    senders,
    receivers,
    live_edges,
    send_rows,
    edge_w1,
    edge_b1,
    edge_w2,
    edge_gain,
    node_w1,
    node_b1,
    node_w2,
    node_gain,
):
    rank_count = lax.axis_size("edge")
    domains = lax.axis_size("dom")
    stride = domains // 4
    offsets = (1, -1, stride, -stride)
    node_count = node_lat.shape[0]
    face_count = send_rows.shape[1]
    latent = node_lat.shape[1]
    live_rows = lax.broadcasted_iota(jnp.int32, (edge_lat.shape[0],), 0) < live_edges[0, 0]
    lists_all = None
    lists_all = lax.all_gather(send_rows, "edge", axis=0, tiled=True)
    lists_all = lists_all + (jnp.arange(rank_count, dtype=jnp.int32) * node_count)[:, None, None]
    owned_rows = node_lat
    edge_rows = edge_lat
    for layer_index in range(LAYERS):
        received = []
        domain_rows = lax.all_gather(owned_rows, "edge", axis=0, tiled=True)
        face_rows = jnp.take(domain_rows, lists_all, axis=0)
        for face_index in range(face_count):
            received.append(passed_along(face_rows[:, face_index], "dom", offsets[face_index]))
        halo_all = jnp.stack(received, axis=1).reshape(-1, latent)
        node_table = jnp.concatenate([domain_rows, halo_all], axis=0)
        sender_rows = jnp.take(node_table, senders, axis=0)
        receiver_rows = jnp.take(domain_rows, receivers, axis=0)
        edge_rows, messages = edge_update(
            edge_rows,
            sender_rows,
            receiver_rows,
            edge_w1[layer_index],
            edge_b1[layer_index],
            edge_w2[layer_index],
            edge_gain[layer_index],
            live_rows,
        )
        summed = lax.psum_scatter(
            jax.ops.segment_sum(
                messages, receivers, num_segments=lax.axis_size("edge") * node_count
            ).astype(jnp.bfloat16),
            "edge",
            scatter_dimension=0,
            tiled=True,
        )
        owned_rows = node_update(
            owned_rows,
            summed,
            node_w1[layer_index],
            node_b1[layer_index],
            node_w2[layer_index],
            node_gain[layer_index],
        )
    return (owned_rows, edge_rows)


def solution(mesh):
    in_specs = (
        P(("dom", "edge"), None),
        P(("dom", "edge"), None),
        P(("dom", "edge")),
        P(("dom", "edge")),
        P("dom", "edge"),
        P(("dom", "edge"), None, None),
        P(),
        P(),
        P(),
        P(),
        P(),
        P(),
        P(),
        P(),
    )
    out_specs = (P(("dom", "edge"), None), P(("dom", "edge"), None))
    return jax.shard_map(shards, mesh=mesh, in_specs=in_specs, out_specs=out_specs, check_vma=False)
```

```python
import functools

import jax
import jax.numpy as jnp
from jax import lax
from jax.experimental import pallas as pl
from jax.experimental.pallas import tpu as pltpu
from jax.sharding import PartitionSpec as P

LAYERS = 2


eps_norm = 1e-05


def passed_along(value, axis, steps):
    count = lax.axis_size(axis)
    pairs = [(source, (source + steps) % count) for source in range(count)]
    return lax.ppermute(value, axis, pairs)


def layer_norm(values, norm_gain):
    center = values - jnp.mean(values, axis=-1, keepdims=True)
    spread = jnp.mean(center * center, axis=-1, keepdims=True)
    return center * lax.rsqrt(spread + eps_norm) * norm_gain


def edge_update(
    edge_rows, sender_rows, receiver_rows, weight_in, bias_in, weight_out, norm_gain, live_rows
):
    feature_width = edge_rows.shape[1]
    pre_act = jnp.dot(edge_rows, weight_in[:feature_width], preferred_element_type=jnp.float32)
    pre_act = pre_act + jnp.dot(
        sender_rows,
        weight_in[feature_width : 2 * feature_width],
        preferred_element_type=jnp.float32,
    )
    pre_act = pre_act + jnp.dot(
        receiver_rows, weight_in[2 * feature_width :], preferred_element_type=jnp.float32
    )
    hidden_rows = jax.nn.relu(pre_act + bias_in).astype(jnp.bfloat16)
    messages = layer_norm(
        jnp.dot(hidden_rows, weight_out, preferred_element_type=jnp.float32), norm_gain
    )
    messages = jnp.where(live_rows[:, None], messages, jnp.float32(0.0))
    return ((edge_rows.astype(jnp.float32) + messages).astype(jnp.bfloat16), messages)


def node_update(node_rows, aggregate, weight_in, bias_in, weight_out, norm_gain):
    feature_width = node_rows.shape[1]
    pre_act = jnp.dot(node_rows, weight_in[:feature_width], preferred_element_type=jnp.float32)
    pre_act = pre_act + jnp.dot(
        aggregate, weight_in[feature_width:], preferred_element_type=jnp.float32
    )
    hidden_rows = jax.nn.relu(pre_act + bias_in).astype(jnp.bfloat16)
    update = layer_norm(
        jnp.dot(hidden_rows, weight_out, preferred_element_type=jnp.float32), norm_gain
    )
    return (node_rows.astype(jnp.float32) + update).astype(jnp.bfloat16)


F32 = jnp.float32
BF16 = jnp.bfloat16
TILE = 256
HALF = 128
ROWS = 512
LOCAL_ROWS = 1024
I16 = jnp.int16
IN_VMEM = pl.BlockSpec(memory_space=pltpu.VMEM)
IN_SMEM = pl.BlockSpec(memory_space=pltpu.SMEM)
IN_HBM = pl.BlockSpec(memory_space=pltpu.HBM)


def shaped(shape, dtype):
    return jax.ShapeDtypeStruct(shape, dtype)


def call(kernel, outs, args, scratch=(), smem=(), stay=(), leave=(), flops=0, limit=24):
    nbytes = sum(a.size * a.dtype.itemsize for a in args)
    return pl.pallas_call(
        kernel,
        out_shape=outs,
        in_specs=[
            IN_SMEM if k in smem else IN_HBM if k in stay else IN_VMEM for k in range(len(args))
        ],
        out_specs=[IN_HBM if k in leave else IN_VMEM for k in range(len(outs))]
        if isinstance(outs, list)
        else IN_VMEM,
        scratch_shapes=scratch,
        compiler_params=pltpu.CompilerParams(vmem_limit_bytes=limit << 20),
        cost_estimate=pl.CostEstimate(flops=flops, transcendentals=0, bytes_accessed=nbytes),
    )(*args)


def place(stride):
    dom = lax.axis_index("dom")
    core = lax.axis_index("edge")
    return core, lax.rem(dom, 2), lax.rem(lax.div(dom, stride), 2)


def mm(a, b):
    return jnp.dot(a, b, preferred_element_type=F32)


def column(row):
    return jnp.transpose(jnp.broadcast_to(row, (HALF, HALF)))


def one_hot_rows(row, width):
    col = column(row)
    lane = lax.broadcasted_iota(jnp.int32, (HALF, HALF), 1)
    parts = [jnp.where(col == lane + k, 1.0, 0.0) for k in range(0, width, HALF)]
    return jnp.concatenate(parts, axis=1).astype(BF16)


def dyn(start, size, unit=None):
    return pl.ds(pl.multiple_of(start, unit or size), size)


def faces(stride):
    core, par_d, par_s = place(stride)
    par = jnp.where(core == 0, par_d, par_s)
    return 2 * core + 1 - par, 2 * core + par


def face_hits(stride, lists):
    return [one_hot_rows(lists[0, pl.ds(face, 1), :], TILE) for face in faces(stride)]


def pick_kernel(stride, own_ref, peer_ref, list_own, list_peer, far, near, hot):
    for n, (lists, nodes) in enumerate(((list_own, own_ref), (list_peer, peer_ref))):
        for k, (rows, out_rows) in enumerate(zip(face_hits(stride, lists), (far, near))):
            hot[2 * n + k] = rows
            out_rows[n * HALF : (n + 1) * HALF, :] = mm(rows, nodes[...]).astype(BF16)


def load_kernel(count, *refs):
    hbm, vmem, sems = refs[:count], refs[count:-1], refs[-1]
    copies = [
        pltpu.make_async_copy(src if len(src.shape) == len(dst.shape) else src.at[0], dst, sems.at[k])
        for k, (src, dst) in enumerate(zip(hbm, vmem))
    ]
    for copy in copies:
        copy.start()
    for copy in copies:
        copy.wait()


def in_hbm(arrays):
    return [pltpu.with_memory_space_constraint(a, pltpu.HBM) for a in arrays]


def columns(stride, send_ref, recv_ref, cols, at):
    _, par_d, par_s = place(stride)
    v = send_ref[:, at]
    j = v - 2 * TILE
    owner = lax.shift_right_arithmetic(j, 9)
    face = lax.shift_right_arithmetic(j, 7) & 3
    core = lax.shift_right_arithmetic(face, 1)
    par = jnp.where(core == 0, par_d, par_s)
    near = (face & 1) != par
    tile = jnp.where(near, 2, 4) + core
    at_tile = ((owner ^ core) & 1) * HALF + (j & (HALF - 1))
    spot = jnp.where(v < 2 * TILE, v, tile * TILE + at_tile)
    cols[0, at, :] = column(spot).astype(I16)
    cols[1, at, :] = column(recv_ref[:, at]).astype(I16)


def hits(spots, first, tiles):
    one = jnp.ones(spots.shape, BF16)
    zero = jnp.zeros(spots.shape, BF16)
    lane = lax.broadcasted_iota(jnp.int32, spots.shape, 1)
    parts = [
        jnp.where(spots == (lane + (first * TILE + k * HALF)).astype(I16), one, zero)
        for k in range(2 * tiles)
    ]
    return jnp.concatenate(parts, axis=1)


def project(parts, w1_ref, table):
    for k in (1, 2):
        for start, size, ref in parts:
            table[dyn((2 * k - 2) * TILE + start, size, TILE), :] = mm(
                ref[...], w1_ref[k * TILE : (k + 1) * TILE, :]
            ).astype(BF16)


def local_block(layer, at, cols, b1_ref, table, pre_ref, edges=None):
    acc = 0.0 if edges is None else mm(*edges)
    acc = acc + mm(hits(cols[0, at, :], 0, 2), table[0 : 2 * TILE, :])
    acc = acc + mm(hits(cols[1, at, :], 0, 2), table[2 * TILE :, :])
    pre_ref[at, :] = acc + b1_ref[layer : layer + 1, :]


def first_kernel(stride, loads, send_ref, recv_ref, own_ref, peer_ref, w1_ref, b1_ref, *refs):
    hbm, (pre_ref, cols), refs = refs[:loads], refs[loads : loads + 2], refs[loads + 2 :]
    vmem, (table, sems) = refs[:loads], refs[loads:]
    ends = [(hbm[0].at[1], vmem[0])] + list(zip(hbm[1:], vmem[1:]))
    copies = [pltpu.make_async_copy(*pair, sems.at[k]) for k, pair in enumerate(ends)]
    for copy in copies:
        copy.start()
    blocks = [pl.ds(start, LOCAL_ROWS) for start in range(0, pre_ref.shape[0], LOCAL_ROWS)]
    core = lax.axis_index("edge")
    parts = ((core * TILE, TILE, own_ref), ((1 - core) * TILE, TILE, peer_ref))

    def make(k):
        for start in range(k * LOCAL_ROWS, (k + 1) * LOCAL_ROWS, HALF):
            columns(stride, send_ref, recv_ref, cols, pl.ds(start, HALF))

    make(0)
    project(parts, w1_ref, table)
    for k, at in enumerate(blocks):
        if k + 1 < len(blocks):
            make(k + 1)
        local_block(0, at, cols, b1_ref, table, pre_ref)
    for copy in copies:
        copy.wait()


def local_kernel(layer, edge_ref, cols, dom_ref, w1_ref, b1_ref, pre_ref, table):
    project(((0, 2 * TILE, dom_ref),), w1_ref, table)

    def step(k, carry):
        at = dyn(k * LOCAL_ROWS, LOCAL_ROWS)
        edges = (edge_ref[at, :], w1_ref[0:TILE, :])
        local_block(layer, at, cols, b1_ref, table, pre_ref, edges)
        return carry

    lax.fori_loop(0, edge_ref.shape[0] // LOCAL_ROWS, step, 0)


def tile_kernel(first, peer, pre_ref, cols, w1_ref, rows_ref, *refs):
    out_ref = refs[-1]
    core = lax.axis_index("edge")
    tile = first + (1 - core if peer else core)
    table = mm(rows_ref[...], w1_ref[TILE : 2 * TILE, :]).astype(BF16)
    half = pre_ref.shape[0] // 2

    def step(k, carry):
        at = dyn(k * half, half)
        acc = pre_ref[at, :] + mm(hits(cols[0, at, :], tile, 1), table)
        if len(refs) == 2:
            acc = acc + mm(refs[0][at, :], w1_ref[0:TILE, :])
        out_ref[at, :] = acc
        return carry

    lax.fori_loop(0, 2, step, 0)


def receiver_hits(recv_ref, at, node, nodes):
    shape = (nodes, ROWS)
    spot = (lax.broadcasted_iota(jnp.int32, shape, 0) + node).astype(I16)
    here = jnp.broadcast_to(recv_ref[:, at].astype(I16), shape)
    return jnp.where(here == spot, jnp.ones(shape, BF16), jnp.zeros(shape, BF16))


def edge_kernel(
    layer, split, live_ref, pre_ref, cols, recv_ref, edge_ref, w1_ref, w2_ref, gain_ref, peer, out_ref, *refs
):
    core = lax.axis_index("edge")
    if split:
        give_ref, msgs, table, raw, sums = refs
        node, nodes = (1 - core) * TILE, TILE
    else:
        node, nodes = 0, 2 * TILE
        part_ref, table, raw, msgs, sums = refs
    tile = 5 - core
    table[...] = mm(peer[...], w1_ref[TILE : 2 * TILE, :]).astype(BF16)
    gain = gain_ref[layer : layer + 1, :]
    live = live_ref[0, 0]
    count = edge_ref.shape[0] // ROWS

    def gather(at):
        acc = pre_ref[at, :] + mm(hits(cols[0, at, :], tile, 1), table[...])
        hidden = jnp.maximum(acc.astype(BF16), jnp.asarray(0, BF16))
        raw[at, :] = mm(hidden, w2_ref[layer])

    def norm(at, start):
        values = raw[at, :]
        center = values - jnp.mean(values, axis=-1, keepdims=True)
        spread = jnp.mean(center * center, axis=-1, keepdims=True)
        scale = lax.rsqrt(spread + eps_norm)
        row = lax.broadcasted_iota(jnp.int32, scale.shape, 0) + start
        scale = jnp.where(row < live, scale, 0.0)
        message = (center * scale * gain).astype(BF16)
        msgs[at, :] = message
        out_ref[at, :] = edge_ref[at, :] + message

    def segment(at, new):
        part = mm(receiver_hits(recv_ref, at, node, nodes), msgs[at, :])
        sums[...] = part if new else sums[...] + part

    for k in range(count + 2):
        if k >= 2:
            segment(pl.ds((k - 2) * ROWS, ROWS), k == 2)
        if 1 <= k <= count:
            norm(pl.ds((k - 1) * ROWS, ROWS), (k - 1) * ROWS)
        if k < count:
            gather(pl.ds(k * ROWS, ROWS))
    (give_ref if split else part_ref)[...] = sums[...].astype(BF16)


def keep_kernel(recv_ref, msgs, edge_ref, keep_ref, hbm, sems):
    blocks = [pl.ds(start, ROWS) for start in range(0, edge_ref.shape[0], ROWS)]
    copies = [
        pltpu.make_async_copy(edge_ref.at[at, :], hbm.at[at, :], sems.at[k])
        for k, at in enumerate(blocks)
    ]
    for copy in copies:
        copy.start()
    node = lax.axis_index("edge") * TILE
    total = 0.0
    for at in blocks:
        total = total + mm(receiver_hits(recv_ref, at, node, TILE), msgs[at, :])
    keep_ref[...] = total.astype(BF16)
    for copy in copies:
        copy.wait()


def updated(layer, nodes, first, second, w1_ref, b1_ref, w2_ref, gain_ref):
    total = (first.astype(F32) + second.astype(F32)).astype(BF16)
    pre = mm(nodes, w1_ref[layer, 0:TILE, :]) + mm(total, w1_ref[layer, TILE:, :])
    hidden = jnp.maximum(pre + b1_ref[layer : layer + 1, :], 0.0).astype(BF16)
    step = layer_norm(mm(hidden, w2_ref[layer]), gain_ref[layer : layer + 1, :])
    return (nodes.astype(F32) + step).astype(BF16)


def node_kernel(layer, own_ref, peer_ref, first, second, hot, w1, b1, w2, gain, out, far, near):
    core = lax.axis_index("edge")
    nodes = []
    for owner, ref in ((core, own_ref), (1 - core, peer_ref)):
        at = dyn(owner * TILE, TILE)
        nodes.append(updated(layer, ref[...], first[at, :], second[at, :], w1, b1, w2, gain))
        out[at, :] = nodes[-1]
    for n in range(2):
        for k, ref in enumerate((far, near)):
            ref[n * HALF : (n + 1) * HALF, :] = mm(hot[2 * n + k], nodes[n]).astype(BF16)


def last_kernel(layer, nodes_ref, first, second, w1, b1, w2, gain, out):
    core = lax.axis_index("edge")
    nodes = nodes_ref[dyn(core * TILE, TILE), :]
    out[...] = updated(layer, nodes, first[...], second[...], w1, b1, w2, gain)


def met(count, stride, odd):
    pairs = []
    for dom in range(count):
        ahead = (dom // stride) % 2 == odd
        pairs.append((dom + (stride if ahead else -stride)) % count)
    return pairs


def swapped(value):
    return lax.ppermute(value, "edge", [(0, 1), (1, 0)])


def fast_shards(
    node_lat,
    edge_lat,
    senders,
    receivers,
    live_edges,
    send_rows,
    edge_w1,
    edge_b1,
    edge_w2,
    edge_gain,
    node_w1,
    node_b1,
    node_w2,
    node_gain,
):
    domains = lax.axis_size("dom")
    stride = domains // 4
    edges, width = edge_lat.shape
    nodes = node_lat.shape[0]
    near_d, far_d = met(domains, 1, 0), met(domains, 1, 1)
    near_s, far_s = met(domains, stride, 0), met(domains, stride, 1)

    def sent_by_core(value, partner_d, partner_s):
        pairs = [(2 * d, 2 * p) for d, p in enumerate(partner_d)]
        pairs += [(2 * d + 1, 2 * p + 1) for d, p in enumerate(partner_s)]
        return lax.ppermute(value, ("dom", "edge"), pairs)

    table = pltpu.VMEM((TILE, width), BF16)
    messages = pltpu.VMEM((edges, width), BF16)
    pre_shape = shaped((edges, width), F32)
    rows_out = shaped((TILE, width), BF16)
    pass_flops = 2 * edges * TILE * width

    peer_nodes = swapped(node_lat)
    peer_lists = swapped(send_rows)
    send_at, recv_at = senders[None], receivers[None]
    first = (node_lat, send_rows, send_at, recv_at, edge_b1, edge_w1)
    node_lat, send_rows, send_at, recv_at, edge_b1, first_w1 = call(
        functools.partial(load_kernel, len(first)),
        [shaped(a.shape, a.dtype) for a in first[:-1]] + [shaped(edge_w1.shape[1:], BF16)],
        in_hbm(first),
        scratch=[pltpu.SemaphoreType.DMA((len(first),))],
        stay=range(len(first)),
    )
    far_rows, near_rows, hot = call(
        functools.partial(pick_kernel, stride),
        [rows_out, rows_out, shaped((4, HALF, TILE), BF16)],
        (node_lat, peer_nodes, send_rows, peer_lists),
    )
    for layer in range(LAYERS):
        last = layer == LAYERS - 1
        near = sent_by_core(near_rows, near_d, near_s)
        far = sent_by_core(far_rows, far_d, far_s)
        if layer == 0:
            loads = (edge_w1, edge_lat, edge_w2, node_w1, node_w2, edge_gain, node_b1, node_gain)
            pre, cols, next_w1, edge_rows, edge_w2, node_w1, node_w2, edge_gain, node_b1, node_gain = call(
                functools.partial(first_kernel, stride, len(loads)),
                [pre_shape, shaped((2, edges, HALF), I16)]
                + [shaped(a.shape[1:] if a is edge_w1 else a.shape, a.dtype) for a in loads],
                (send_at, recv_at, node_lat, peer_nodes, first_w1, edge_b1, *in_hbm(loads)),
                scratch=[
                    pltpu.VMEM((4 * TILE, width), BF16),
                    pltpu.SemaphoreType.DMA((len(loads),)),
                ],
                stay=range(6, 6 + len(loads)),
                flops=5 * pass_flops,
            )
        else:
            pre = call(
                functools.partial(local_kernel, layer),
                pre_shape,
                (edge_rows, cols, all_nodes, next_w1, edge_b1),
                scratch=[pltpu.VMEM((4 * TILE, width), BF16)],
                flops=5 * pass_flops,
            )
        w1 = next_w1 if layer else first_w1

        def add(first, peer, pre, rows, *edges):
            return call(
                functools.partial(tile_kernel, first, peer),
                pre_shape,
                (pre, cols, w1, rows, *edges),
                flops=pass_flops,
            )

        pre, near, live_edges = lax.optimization_barrier((pre, near, live_edges))
        near_other = swapped(near)
        pre = add(2, False, pre, near, *(() if layer else (edge_rows,)))
        pre = add(2, True, pre, near_other)
        pre, far = lax.optimization_barrier((pre, far))
        far_other = swapped(far)
        pre = add(4, False, pre, far)
        if last:
            outs = [shaped((nodes, width), BF16), shaped((edges, width), BF16)]
        else:
            outs = [shaped((2 * nodes, width), BF16)]
        edge_rows, *partial = call(
            functools.partial(edge_kernel, layer, last),
            [shaped((edges, width), BF16)] + outs,
            (live_edges, pre, cols, recv_at, edge_rows, w1, edge_w2, edge_gain, far_other),
            scratch=[table, pltpu.VMEM((edges, width), F32)]
            + ([pltpu.VMEM((nodes, width), F32)] if last else [messages, pltpu.VMEM((2 * nodes, width), F32)]),
            smem=(0,),
            flops=5 * pass_flops,
        )
        other = swapped(partial[0])
        weights = (node_w1, node_b1, node_w2, node_gain)
        if last:
            keep, edge_out = call(
                keep_kernel,
                [shaped((nodes, width), BF16), shaped((edges, width), BF16)],
                (recv_at, partial[1], edge_rows),
                scratch=[pltpu.SemaphoreType.DMA((edges // ROWS,))],
                leave=(1,),
            )
            out = call(
                functools.partial(last_kernel, layer),
                shaped((nodes, width), BF16),
                (all_nodes, keep, other, *weights),
            )
        else:
            all_nodes, far_rows, near_rows = call(
                functools.partial(node_kernel, layer),
                [shaped((2 * nodes, width), BF16), rows_out, rows_out],
                (node_lat, peer_nodes, partial[0], other, hot, *weights),
            )
    return out, edge_out


def shards(*args):
    node_lat, edge_lat, _, _, _, send_rows = args[:6]
    domains = lax.axis_size("dom")
    fits = (
        lax.axis_size("edge") == 2
        and domains % 8 == 0
        and node_lat.shape == (TILE, TILE)
        and edge_lat.shape[0] % LOCAL_ROWS == 0
        and send_rows.shape[1:] == (4, HALF)
        and args[6].shape == (LAYERS, 3 * TILE, TILE)
    )
    return (fast_shards if fits else general_shards)(*args)


def general_shards(
    node_lat,
    edge_lat,
    senders,
    receivers,
    live_edges,
    send_rows,
    edge_w1,
    edge_b1,
    edge_w2,
    edge_gain,
    node_w1,
    node_b1,
    node_w2,
    node_gain,
):
    rank_count = lax.axis_size("edge")
    domains = lax.axis_size("dom")
    stride = domains // 4
    offsets = (1, -1, stride, -stride)
    node_count = node_lat.shape[0]
    face_count = send_rows.shape[1]
    latent = node_lat.shape[1]
    live_rows = lax.broadcasted_iota(jnp.int32, (edge_lat.shape[0],), 0) < live_edges[0, 0]
    lists_all = None
    lists_all = lax.all_gather(send_rows, "edge", axis=0, tiled=True)
    lists_all = lists_all + (jnp.arange(rank_count, dtype=jnp.int32) * node_count)[:, None, None]
    owned_rows = node_lat
    edge_rows = edge_lat
    for layer_index in range(LAYERS):
        received = []
        domain_rows = lax.all_gather(owned_rows, "edge", axis=0, tiled=True)
        face_rows = jnp.take(domain_rows, lists_all, axis=0)
        for face_index in range(face_count):
            received.append(passed_along(face_rows[:, face_index], "dom", offsets[face_index]))
        halo_all = jnp.stack(received, axis=1).reshape(-1, latent)
        node_table = jnp.concatenate([domain_rows, halo_all], axis=0)
        sender_rows = jnp.take(node_table, senders, axis=0)
        receiver_rows = jnp.take(domain_rows, receivers, axis=0)
        edge_rows, messages = edge_update(
            edge_rows,
            sender_rows,
            receiver_rows,
            edge_w1[layer_index],
            edge_b1[layer_index],
            edge_w2[layer_index],
            edge_gain[layer_index],
            live_rows,
        )
        summed = lax.psum_scatter(
            jax.ops.segment_sum(
                messages, receivers, num_segments=lax.axis_size("edge") * node_count
            ).astype(jnp.bfloat16),
            "edge",
            scatter_dimension=0,
            tiled=True,
        )
        owned_rows = node_update(
            owned_rows,
            summed,
            node_w1[layer_index],
            node_b1[layer_index],
            node_w2[layer_index],
            node_gain[layer_index],
        )
    return (owned_rows, edge_rows)


def solution(mesh):
    in_specs = (
        P(("dom", "edge"), None),
        P(("dom", "edge"), None),
        P(("dom", "edge")),
        P(("dom", "edge")),
        P("dom", "edge"),
        P(("dom", "edge"), None, None),
        P(),
        P(),
        P(),
        P(),
        P(),
        P(),
        P(),
        P(),
    )
    out_specs = (P(("dom", "edge"), None), P(("dom", "edge"), None))
    return jax.shard_map(shards, mesh=mesh, in_specs=in_specs, out_specs=out_specs, check_vma=False)
```

```python
import functools

import jax
import jax.numpy as jnp
from jax import lax
from jax.experimental import pallas as pl
from jax.experimental.pallas import tpu as pltpu
from jax.sharding import PartitionSpec as P

LAYERS = 2


eps_norm = 1e-05


def passed_along(value, axis, steps):
    count = lax.axis_size(axis)
    pairs = [(source, (source + steps) % count) for source in range(count)]
    return lax.ppermute(value, axis, pairs)


def layer_norm(values, norm_gain):
    center = values - jnp.mean(values, axis=-1, keepdims=True)
    spread = jnp.mean(center * center, axis=-1, keepdims=True)
    return center * lax.rsqrt(spread + eps_norm) * norm_gain


def edge_update(
    edge_rows, sender_rows, receiver_rows, weight_in, bias_in, weight_out, norm_gain, live_rows
):
    feature_width = edge_rows.shape[1]
    pre_act = jnp.dot(edge_rows, weight_in[:feature_width], preferred_element_type=jnp.float32)
    pre_act = pre_act + jnp.dot(
        sender_rows,
        weight_in[feature_width : 2 * feature_width],
        preferred_element_type=jnp.float32,
    )
    pre_act = pre_act + jnp.dot(
        receiver_rows, weight_in[2 * feature_width :], preferred_element_type=jnp.float32
    )
    hidden_rows = jax.nn.relu(pre_act + bias_in).astype(jnp.bfloat16)
    messages = layer_norm(
        jnp.dot(hidden_rows, weight_out, preferred_element_type=jnp.float32), norm_gain
    )
    messages = jnp.where(live_rows[:, None], messages, jnp.float32(0.0))
    return ((edge_rows.astype(jnp.float32) + messages).astype(jnp.bfloat16), messages)


def node_update(node_rows, aggregate, weight_in, bias_in, weight_out, norm_gain):
    feature_width = node_rows.shape[1]
    pre_act = jnp.dot(node_rows, weight_in[:feature_width], preferred_element_type=jnp.float32)
    pre_act = pre_act + jnp.dot(
        aggregate, weight_in[feature_width:], preferred_element_type=jnp.float32
    )
    hidden_rows = jax.nn.relu(pre_act + bias_in).astype(jnp.bfloat16)
    update = layer_norm(
        jnp.dot(hidden_rows, weight_out, preferred_element_type=jnp.float32), norm_gain
    )
    return (node_rows.astype(jnp.float32) + update).astype(jnp.bfloat16)


F32 = jnp.float32
BF16 = jnp.bfloat16
TILE = 256
HALF = 128
ROWS = 512
LOCAL_ROWS = 1024
I16 = jnp.int16
IN_VMEM = pl.BlockSpec(memory_space=pltpu.VMEM)
IN_SMEM = pl.BlockSpec(memory_space=pltpu.SMEM)
IN_HBM = pl.BlockSpec(memory_space=pltpu.HBM)


def shaped(shape, dtype):
    return jax.ShapeDtypeStruct(shape, dtype)


def call(kernel, outs, args, scratch=(), smem=(), stay=(), leave=(), flops=0, limit=24):
    nbytes = sum(a.size * a.dtype.itemsize for a in args)
    return pl.pallas_call(
        kernel,
        out_shape=outs,
        in_specs=[
            IN_SMEM if k in smem else IN_HBM if k in stay else IN_VMEM for k in range(len(args))
        ],
        out_specs=[IN_HBM if k in leave else IN_VMEM for k in range(len(outs))]
        if isinstance(outs, list)
        else IN_VMEM,
        scratch_shapes=scratch,
        compiler_params=pltpu.CompilerParams(vmem_limit_bytes=limit << 20),
        cost_estimate=pl.CostEstimate(flops=flops, transcendentals=0, bytes_accessed=nbytes),
    )(*args)


def place(stride):
    dom = lax.axis_index("dom")
    core = lax.axis_index("edge")
    return core, lax.rem(dom, 2), lax.rem(lax.div(dom, stride), 2)


def mm(a, b):
    return jnp.dot(a, b, preferred_element_type=F32)


def column(row):
    return jnp.transpose(jnp.broadcast_to(row, (HALF, HALF)))


def one_hot_rows(row, width):
    col = column(row)
    lane = lax.broadcasted_iota(jnp.int32, (HALF, HALF), 1)
    parts = [jnp.where(col == lane + k, 1.0, 0.0) for k in range(0, width, HALF)]
    return jnp.concatenate(parts, axis=1).astype(BF16)


def dyn(start, size, unit=None):
    return pl.ds(pl.multiple_of(start, unit or size), size)


def faces(stride):
    core, par_d, par_s = place(stride)
    par = jnp.where(core == 0, par_d, par_s)
    return 2 * core + 1 - par, 2 * core + par


def face_hits(stride, lists):
    return [one_hot_rows(lists[0, pl.ds(face, 1), :], TILE) for face in faces(stride)]


def pick_kernel(stride, own_ref, peer_ref, list_own, list_peer, far, near, hot):
    for n, (lists, nodes) in enumerate(((list_own, own_ref), (list_peer, peer_ref))):
        for k, (rows, out_rows) in enumerate(zip(face_hits(stride, lists), (far, near))):
            hot[2 * n + k] = rows
            out_rows[n * HALF : (n + 1) * HALF, :] = mm(rows, nodes[...]).astype(BF16)


def load_kernel(count, *refs):
    hbm, vmem, sems = refs[:count], refs[count:-1], refs[-1]
    copies = [
        pltpu.make_async_copy(src if len(src.shape) == len(dst.shape) else src.at[0], dst, sems.at[k])
        for k, (src, dst) in enumerate(zip(hbm, vmem))
    ]
    for copy in copies:
        copy.start()
    for copy in copies:
        copy.wait()


def in_hbm(arrays):
    return [pltpu.with_memory_space_constraint(a, pltpu.HBM) for a in arrays]


def columns(stride, send_ref, recv_ref, cols, at):
    _, par_d, par_s = place(stride)
    v = send_ref[:, at]
    j = v - 2 * TILE
    owner = lax.shift_right_arithmetic(j, 9)
    face = lax.shift_right_arithmetic(j, 7) & 3
    core = lax.shift_right_arithmetic(face, 1)
    par = jnp.where(core == 0, par_d, par_s)
    near = (face & 1) != par
    tile = jnp.where(near, 2, 4) + core
    at_tile = ((owner ^ core) & 1) * HALF + (j & (HALF - 1))
    spot = jnp.where(v < 2 * TILE, v, tile * TILE + at_tile)
    cols[0, at, :] = column(spot).astype(I16)
    cols[1, at, :] = column(recv_ref[:, at]).astype(I16)


def hits(spots, first, tiles):
    one = jnp.ones(spots.shape, BF16)
    zero = jnp.zeros(spots.shape, BF16)
    lane = lax.broadcasted_iota(jnp.int32, spots.shape, 1)
    parts = [
        jnp.where(spots == (lane + (first * TILE + k * HALF)).astype(I16), one, zero)
        for k in range(2 * tiles)
    ]
    return jnp.concatenate(parts, axis=1)


def project(parts, w1_ref, table):
    for k in (1, 2):
        for start, size, ref in parts:
            table[dyn((2 * k - 2) * TILE + start, size, TILE), :] = mm(
                ref[...], w1_ref[k * TILE : (k + 1) * TILE, :]
            ).astype(BF16)


def local_block(layer, at, cols, b1_ref, table, pre_ref, edges=None):
    acc = 0.0 if edges is None else mm(*edges)
    acc = acc + mm(hits(cols[0, at, :], 0, 2), table[0 : 2 * TILE, :])
    acc = acc + mm(hits(cols[1, at, :], 0, 2), table[2 * TILE :, :])
    pre_ref[at, :] = acc + b1_ref[layer : layer + 1, :]


def first_kernel(stride, loads, send_ref, recv_ref, own_ref, peer_ref, w1_ref, b1_ref, *refs):
    hbm, (pre_ref, cols), refs = refs[:loads], refs[loads : loads + 2], refs[loads + 2 :]
    vmem, (table, sems) = refs[:loads], refs[loads:]
    ends = [(hbm[0].at[1], vmem[0])] + list(zip(hbm[1:], vmem[1:]))
    copies = [pltpu.make_async_copy(*pair, sems.at[k]) for k, pair in enumerate(ends)]
    for copy in copies:
        copy.start()
    blocks = [pl.ds(start, ROWS) for start in range(0, pre_ref.shape[0], ROWS)]
    core = lax.axis_index("edge")
    parts = ((core * TILE, TILE, own_ref), ((1 - core) * TILE, TILE, peer_ref))

    def make(k):
        for start in range(k * ROWS, (k + 1) * ROWS, HALF):
            columns(stride, send_ref, recv_ref, cols, pl.ds(start, HALF))

    make(0)
    project(parts, w1_ref, table)
    for k, at in enumerate(blocks):
        if k + 1 < len(blocks):
            make(k + 1)
        local_block(0, at, cols, b1_ref, table, pre_ref)
    for copy in copies:
        copy.wait()


def local_kernel(layer, edge_ref, cols, dom_ref, w1_ref, b1_ref, pre_ref, table):
    project(((0, 2 * TILE, dom_ref),), w1_ref, table)

    def step(k, carry):
        at = dyn(k * LOCAL_ROWS, LOCAL_ROWS)
        edges = (edge_ref[at, :], w1_ref[0:TILE, :])
        local_block(layer, at, cols, b1_ref, table, pre_ref, edges)
        return carry

    lax.fori_loop(0, edge_ref.shape[0] // LOCAL_ROWS, step, 0)


def tile_kernel(first, peer, pre_ref, cols, w1_ref, rows_ref, *refs):
    out_ref = refs[-1]
    core = lax.axis_index("edge")
    tile = first + (1 - core if peer else core)
    table = mm(rows_ref[...], w1_ref[TILE : 2 * TILE, :]).astype(BF16)
    acc = pre_ref[...] + mm(hits(cols[0], tile, 1), table)
    if len(refs) == 2:
        acc = acc + mm(refs[0][...], w1_ref[0:TILE, :])
    out_ref[...] = acc


def receiver_hits(recv_ref, at, node, nodes):
    shape = (nodes, ROWS)
    spot = (lax.broadcasted_iota(jnp.int32, shape, 0) + node).astype(I16)
    here = jnp.broadcast_to(recv_ref[:, at].astype(I16), shape)
    return jnp.where(here == spot, jnp.ones(shape, BF16), jnp.zeros(shape, BF16))


def edge_kernel(
    layer, split, live_ref, pre_ref, cols, recv_ref, edge_ref, w1_ref, w2_ref, gain_ref, peer, out_ref, *refs
):
    core = lax.axis_index("edge")
    if split:
        give_ref, msgs, table, raw, sums = refs
        node, nodes = (1 - core) * TILE, TILE
    else:
        node, nodes = 0, 2 * TILE
        part_ref, table, raw, msgs, sums = refs
    tile = 5 - core
    table[...] = mm(peer[...], w1_ref[TILE : 2 * TILE, :]).astype(BF16)
    gain = gain_ref[layer : layer + 1, :]
    live = live_ref[0, 0]
    count = edge_ref.shape[0] // ROWS

    def gather(at):
        acc = pre_ref[at, :] + mm(hits(cols[0, at, :], tile, 1), table[...])
        hidden = jnp.maximum(acc.astype(BF16), jnp.asarray(0, BF16))
        raw[at, :] = mm(hidden, w2_ref[layer])

    def norm(at, start):
        values = raw[at, :]
        center = values - jnp.mean(values, axis=-1, keepdims=True)
        spread = jnp.mean(center * center, axis=-1, keepdims=True)
        scale = lax.rsqrt(spread + eps_norm)
        row = lax.broadcasted_iota(jnp.int32, scale.shape, 0) + start
        scale = jnp.where(row < live, scale, 0.0)
        message = (center * scale * gain).astype(BF16)
        msgs[at, :] = message
        out_ref[at, :] = edge_ref[at, :] + message

    def segment(at, new):
        part = mm(receiver_hits(recv_ref, at, node, nodes), msgs[at, :])
        sums[...] = part if new else sums[...] + part

    for k in range(count + 2):
        if k >= 2:
            segment(pl.ds((k - 2) * ROWS, ROWS), k == 2)
        if 1 <= k <= count:
            norm(pl.ds((k - 1) * ROWS, ROWS), (k - 1) * ROWS)
        if k < count:
            gather(pl.ds(k * ROWS, ROWS))
    (give_ref if split else part_ref)[...] = sums[...].astype(BF16)


def keep_kernel(recv_ref, msgs, edge_ref, keep_ref, hbm, sems):
    blocks = [pl.ds(start, ROWS) for start in range(0, edge_ref.shape[0], ROWS)]
    copies = [
        pltpu.make_async_copy(edge_ref.at[at, :], hbm.at[at, :], sems.at[k])
        for k, at in enumerate(blocks)
    ]
    for copy in copies:
        copy.start()
    node = lax.axis_index("edge") * TILE
    total = 0.0
    for at in blocks:
        total = total + mm(receiver_hits(recv_ref, at, node, TILE), msgs[at, :])
    keep_ref[...] = total.astype(BF16)
    for copy in copies:
        copy.wait()


def updated(layer, nodes, first, second, w1_ref, b1_ref, w2_ref, gain_ref):
    total = (first.astype(F32) + second.astype(F32)).astype(BF16)
    pre = mm(nodes, w1_ref[layer, 0:TILE, :]) + mm(total, w1_ref[layer, TILE:, :])
    hidden = jnp.maximum(pre + b1_ref[layer : layer + 1, :], 0.0).astype(BF16)
    step = layer_norm(mm(hidden, w2_ref[layer]), gain_ref[layer : layer + 1, :])
    return (nodes.astype(F32) + step).astype(BF16)


def node_kernel(layer, own_ref, peer_ref, first, second, hot, w1, b1, w2, gain, out, far, near):
    core = lax.axis_index("edge")
    nodes = []
    for owner, ref in ((core, own_ref), (1 - core, peer_ref)):
        at = dyn(owner * TILE, TILE)
        nodes.append(updated(layer, ref[...], first[at, :], second[at, :], w1, b1, w2, gain))
        out[at, :] = nodes[-1]
    for n in range(2):
        for k, ref in enumerate((far, near)):
            ref[n * HALF : (n + 1) * HALF, :] = mm(hot[2 * n + k], nodes[n]).astype(BF16)


def last_kernel(layer, nodes_ref, first, second, w1, b1, w2, gain, out):
    core = lax.axis_index("edge")
    nodes = nodes_ref[dyn(core * TILE, TILE), :]
    out[...] = updated(layer, nodes, first[...], second[...], w1, b1, w2, gain)


def met(count, stride, odd):
    pairs = []
    for dom in range(count):
        ahead = (dom // stride) % 2 == odd
        pairs.append((dom + (stride if ahead else -stride)) % count)
    return pairs


def swapped(value):
    return lax.ppermute(value, "edge", [(0, 1), (1, 0)])


def fast_shards(
    node_lat,
    edge_lat,
    senders,
    receivers,
    live_edges,
    send_rows,
    edge_w1,
    edge_b1,
    edge_w2,
    edge_gain,
    node_w1,
    node_b1,
    node_w2,
    node_gain,
):
    domains = lax.axis_size("dom")
    stride = domains // 4
    edges, width = edge_lat.shape
    nodes = node_lat.shape[0]
    near_d, far_d = met(domains, 1, 0), met(domains, 1, 1)
    near_s, far_s = met(domains, stride, 0), met(domains, stride, 1)

    def sent_by_core(value, partner_d, partner_s):
        pairs = [(2 * d, 2 * p) for d, p in enumerate(partner_d)]
        pairs += [(2 * d + 1, 2 * p + 1) for d, p in enumerate(partner_s)]
        return lax.ppermute(value, ("dom", "edge"), pairs)

    table = pltpu.VMEM((TILE, width), BF16)
    messages = pltpu.VMEM((edges, width), BF16)
    pre_shape = shaped((edges, width), F32)
    rows_out = shaped((TILE, width), BF16)
    pass_flops = 2 * edges * TILE * width

    peer_nodes = swapped(node_lat)
    peer_lists = swapped(send_rows)
    send_at, recv_at = senders[None], receivers[None]
    first = (node_lat, send_rows, send_at, recv_at, edge_b1, edge_w1)
    node_lat, send_rows, send_at, recv_at, edge_b1, first_w1 = call(
        functools.partial(load_kernel, len(first)),
        [shaped(a.shape, a.dtype) for a in first[:-1]] + [shaped(edge_w1.shape[1:], BF16)],
        in_hbm(first),
        scratch=[pltpu.SemaphoreType.DMA((len(first),))],
        stay=range(len(first)),
    )
    far_rows, near_rows, hot = call(
        functools.partial(pick_kernel, stride),
        [rows_out, rows_out, shaped((4, HALF, TILE), BF16)],
        (node_lat, peer_nodes, send_rows, peer_lists),
    )
    for layer in range(LAYERS):
        last = layer == LAYERS - 1
        near = sent_by_core(near_rows, near_d, near_s)
        far = sent_by_core(far_rows, far_d, far_s)
        if layer == 0:
            loads = (edge_w1, edge_lat, edge_w2, node_w1, node_w2, edge_gain, node_b1, node_gain)
            pre, cols, next_w1, edge_rows, edge_w2, node_w1, node_w2, edge_gain, node_b1, node_gain = call(
                functools.partial(first_kernel, stride, len(loads)),
                [pre_shape, shaped((2, edges, HALF), I16)]
                + [shaped(a.shape[1:] if a is edge_w1 else a.shape, a.dtype) for a in loads],
                (send_at, recv_at, node_lat, peer_nodes, first_w1, edge_b1, *in_hbm(loads)),
                scratch=[
                    pltpu.VMEM((4 * TILE, width), BF16),
                    pltpu.SemaphoreType.DMA((len(loads),)),
                ],
                stay=range(6, 6 + len(loads)),
                flops=5 * pass_flops,
            )
        else:
            pre = call(
                functools.partial(local_kernel, layer),
                pre_shape,
                (edge_rows, cols, all_nodes, next_w1, edge_b1),
                scratch=[pltpu.VMEM((4 * TILE, width), BF16)],
                flops=5 * pass_flops,
            )
        w1 = next_w1 if layer else first_w1

        def add(first, peer, pre, rows, *edges):
            return call(
                functools.partial(tile_kernel, first, peer),
                pre_shape,
                (pre, cols, w1, rows, *edges),
                flops=pass_flops,
            )

        pre, near, live_edges = lax.optimization_barrier((pre, near, live_edges))
        near_other = swapped(near)
        pre = add(2, False, pre, near, *(() if layer else (edge_rows,)))
        pre = add(2, True, pre, near_other)
        pre, far = lax.optimization_barrier((pre, far))
        far_other = swapped(far)
        pre = add(4, False, pre, far)
        if last:
            outs = [shaped((nodes, width), BF16), shaped((edges, width), BF16)]
        else:
            outs = [shaped((2 * nodes, width), BF16)]
        edge_rows, *partial = call(
            functools.partial(edge_kernel, layer, last),
            [shaped((edges, width), BF16)] + outs,
            (live_edges, pre, cols, recv_at, edge_rows, w1, edge_w2, edge_gain, far_other),
            scratch=[table, pltpu.VMEM((edges, width), F32)]
            + ([pltpu.VMEM((nodes, width), F32)] if last else [messages, pltpu.VMEM((2 * nodes, width), F32)]),
            smem=(0,),
            flops=5 * pass_flops,
        )
        other = swapped(partial[0])
        weights = (node_w1, node_b1, node_w2, node_gain)
        if last:
            keep, edge_out = call(
                keep_kernel,
                [shaped((nodes, width), BF16), shaped((edges, width), BF16)],
                (recv_at, partial[1], edge_rows),
                scratch=[pltpu.SemaphoreType.DMA((edges // ROWS,))],
                leave=(1,),
            )
            out = call(
                functools.partial(last_kernel, layer),
                shaped((nodes, width), BF16),
                (all_nodes, keep, other, *weights),
            )
        else:
            all_nodes, far_rows, near_rows = call(
                functools.partial(node_kernel, layer),
                [shaped((2 * nodes, width), BF16), rows_out, rows_out],
                (node_lat, peer_nodes, partial[0], other, hot, *weights),
            )
    return out, edge_out


def shards(*args):
    node_lat, edge_lat, _, _, _, send_rows = args[:6]
    domains = lax.axis_size("dom")
    fits = (
        lax.axis_size("edge") == 2
        and domains % 8 == 0
        and node_lat.shape == (TILE, TILE)
        and edge_lat.shape[0] % LOCAL_ROWS == 0
        and send_rows.shape[1:] == (4, HALF)
        and args[6].shape == (LAYERS, 3 * TILE, TILE)
    )
    return (fast_shards if fits else general_shards)(*args)


def general_shards(
    node_lat,
    edge_lat,
    senders,
    receivers,
    live_edges,
    send_rows,
    edge_w1,
    edge_b1,
    edge_w2,
    edge_gain,
    node_w1,
    node_b1,
    node_w2,
    node_gain,
):
    rank_count = lax.axis_size("edge")
    domains = lax.axis_size("dom")
    stride = domains // 4
    offsets = (1, -1, stride, -stride)
    node_count = node_lat.shape[0]
    face_count = send_rows.shape[1]
    latent = node_lat.shape[1]
    live_rows = lax.broadcasted_iota(jnp.int32, (edge_lat.shape[0],), 0) < live_edges[0, 0]
    lists_all = None
    lists_all = lax.all_gather(send_rows, "edge", axis=0, tiled=True)
    lists_all = lists_all + (jnp.arange(rank_count, dtype=jnp.int32) * node_count)[:, None, None]
    owned_rows = node_lat
    edge_rows = edge_lat
    for layer_index in range(LAYERS):
        received = []
        domain_rows = lax.all_gather(owned_rows, "edge", axis=0, tiled=True)
        face_rows = jnp.take(domain_rows, lists_all, axis=0)
        for face_index in range(face_count):
            received.append(passed_along(face_rows[:, face_index], "dom", offsets[face_index]))
        halo_all = jnp.stack(received, axis=1).reshape(-1, latent)
        node_table = jnp.concatenate([domain_rows, halo_all], axis=0)
        sender_rows = jnp.take(node_table, senders, axis=0)
        receiver_rows = jnp.take(domain_rows, receivers, axis=0)
        edge_rows, messages = edge_update(
            edge_rows,
            sender_rows,
            receiver_rows,
            edge_w1[layer_index],
            edge_b1[layer_index],
            edge_w2[layer_index],
            edge_gain[layer_index],
            live_rows,
        )
        summed = lax.psum_scatter(
            jax.ops.segment_sum(
                messages, receivers, num_segments=lax.axis_size("edge") * node_count
            ).astype(jnp.bfloat16),
            "edge",
            scatter_dimension=0,
            tiled=True,
        )
        owned_rows = node_update(
            owned_rows,
            summed,
            node_w1[layer_index],
            node_b1[layer_index],
            node_w2[layer_index],
            node_gain[layer_index],
        )
    return (owned_rows, edge_rows)


def solution(mesh):
    in_specs = (
        P(("dom", "edge"), None),
        P(("dom", "edge"), None),
        P(("dom", "edge")),
        P(("dom", "edge")),
        P("dom", "edge"),
        P(("dom", "edge"), None, None),
        P(),
        P(),
        P(),
        P(),
        P(),
        P(),
        P(),
        P(),
    )
    out_specs = (P(("dom", "edge"), None), P(("dom", "edge"), None))
    return jax.shard_map(shards, mesh=mesh, in_specs=in_specs, out_specs=out_specs, check_vma=False)
```
